128 devices in a mesh: lon: 8 (over z_hi, x), lat: 16 (over z_lo, y, core).
Axes of the slice: x: 4, y: 4, z: 4 (z_hi: 2, z_lo: 2; z = z_hi * 2 + z_lo), core: 2. Of those that a mesh axis runs over, the one named last changes fastest.
Arguments:
- tracers: float32 [2, 16, 512, 1024], P(None, None, 'lat', 'lon'), may hold values from -6 to 6
- velocity: float32 [2, 16, 512, 1024], P(None, None, 'lat', 'lon'), may hold values from -3 to 3
- land_mask: int32 [512, 1024], P('lat', 'lon'), may hold values 0 or 1
- mixing: float32 [512, 1024], P('lat', 'lon'), may hold values from 0.05 to 0.25
- owners: int32 [4096, 1], P(('lon', 'lat')), may hold values from 0 to 127; in each aligned block of 32 rows (0 to 31, 32 to 63, ...) at most 2 rows name the same one
- atm_row: int32 [4096], P(('lon', 'lat')), may hold values from 0 to 31
Outputs:
- tracers_out: float32 [2, 16, 512, 1024], P(None, None, 'lat', 'lon')
- velocity_out: float32 [2, 16, 512, 1024], P(None, None, 'lat', 'lon')
- atm_surface: float32 [4, 4096, 128], P(None, ('lon', 'lat'))
- atm_cover: float32 [4096, 128], P(('lon', 'lat'))
The draws below stay inside these ranges and needn't reach their ends.
Inputs may be any that keep to these rules, and one draw needn't show every extreme that they name: `owners`: among the 32 blocks of one device at most 2 name the same owner, and in every draw some owner is named by exactly 2 blocks of some device.
All inputs are finite; a program needn't handle non-finite values. No bound on the sum of `land_mask` on one device may be relied on, other than what follows from the above.
Results may differ from the reference program's by a relative error of at most 0.00007.
Values sent between devices are 32-bit elements; how exact they have to be, the bound alone decides.
A program may use at most 64 MiB of HBM per device.

```python
import math
import jax
import jax.numpy as jnp
import numpy as np

CX = 128
CY = 32
KZ = 16
STEPS = 2
ATM_ROWS = 32
NX = 1024
NY = 512
NB = 32
NBT = 4096
CAP = 2
N_LON = 8
N_LAT = 16


def set_ends(drawn, stream_key, least, top_value):
    place = [jax.random.randint(jax.random.fold_in(stream_key, axis), (), 0, length) for axis, length in enumerate(drawn.shape)]
    longest = drawn.shape.index(max(drawn.shape))
    next_to = place[:longest] + [(place[longest] + 1) % drawn.shape[longest]] + place[longest + 1:]
    return drawn.at[tuple(place)].set(least).at[tuple(next_to)].set(top_value)


def steps_of(own_key, dims, pieces, smallest, top_value):
    def one(axis_at, parts):
        heights = jax.random.uniform(jax.random.fold_in(jax.random.fold_in(own_key, 6), axis_at), (parts,), jnp.float32, smallest / len(pieces), top_value / len(pieces))
        return jnp.repeat(jnp.exp(heights), dims[axis_at] // parts).reshape((-1,) + (1,) * (len(dims) - axis_at - 1))

    factor_of = one(*pieces[0])
    for cut in pieces[1:]:
        factor_of = factor_of * one(*cut)
    return factor_of


def shared_out(rng, own, number, rows, number_of, top, reach, slope):
    order = jax.random.permutation(rng, number_of)
    heavy_load, common = shares(number_of, rows * top, reach, slope, True), shares(number_of, rows * top, reach, slope, False)
    places = jnp.arange(number_of)

    def named(sizes, offset_by):
        used = int((sizes > 0).sum())
        fixed = max(1, used // 4)
        passed = fixed + (places - fixed + offset_by * (used - fixed)) % max(1, number_of - fixed)
        return jnp.zeros((number_of,), jnp.int32).at[order[jnp.where(places < fixed, places, passed)]].set(jnp.asarray(sizes, jnp.int32))

    sizes = jnp.where(number % 4 == 0, named(heavy_load, number // 4), named(common, number - number // 4 - 1))
    mixed = jax.random.permutation(jax.random.fold_in(own, 3), number_of)
    giver, taker = mixed[0:number_of // 2 * 2:2], mixed[1:number_of // 2 * 2:2]
    margin = jnp.minimum(sizes[giver] - 1, reach - sizes[taker]) // 2
    margin = jnp.where((giver == order[0]) | (taker == order[0]) | (sizes[taker] == 0), 0, jnp.maximum(margin, 0))
    passed = jax.random.randint(jax.random.fold_in(own, 4), (number_of // 2,), 0, 1 << 20) % (margin + 1)
    sizes = sizes.at[giver].add(-passed).at[taker].add(passed)
    items = jnp.searchsorted(jnp.cumsum(sizes), jnp.arange(rows * top), side="right").astype(jnp.int32)
    table = items.reshape(top, rows).T
    table = table[jax.random.permutation(jax.random.fold_in(own, 1), rows)]
    offset_by = jax.random.randint(jax.random.fold_in(own, 2), (rows, 1), 0, top)
    return jnp.take_along_axis(table, (jnp.arange(top)[None, :] + offset_by) % top, axis=1)


def shares(number_of, total, bound, lean, full):
    weights = [(1 << 20) // math.isqrt(grade ** lean) + 1 for grade in range(1, number_of + 1)]
    largest = bound if full else min(bound, max(-(-total // number_of), total * weights[0] // sum(weights)))
    least = 1 if total - largest >= number_of - 1 else 0
    holding, spare = [largest] + [least] * (number_of - 1), total - largest - least * (number_of - 1)
    while spare > 0:
        movable = [i for i in range(1, number_of) if holding[i] < largest] or [i for i in range(1, number_of) if holding[i] < bound]
        whole, remaining = sum([weights[i] for i in movable]), spare
        for i in movable:
            more = min(bound - holding[i], max(1, remaining * weights[i] // whole), spare)
            holding[i] = holding[i] + more
            spare = spare - more
    return np.array(holding)


def scatter_about(stream_key, extent, spread, reach, cuts=(), held_as=jnp.bfloat16):
    gain = steps_of(stream_key, extent, cuts, -0.22, 0.18) if cuts else 1.0
    result = jax.random.normal(stream_key, extent, jnp.float32) * spread * gain
    return jnp.minimum(jnp.maximum(result, -reach), reach).astype(held_as)


def setup_inputs(seed: int = 0) -> dict:
    key_list = jax.random.split(jax.random.key(seed), 7)
    tracers = scatter_about(key_list[0], (2, KZ, NY, NX), 1.0, 6.0, ((2, 16), (3, 8)), jnp.float32)
    velocity = scatter_about(key_list[1], (2, KZ, NY, NX), 0.5, 3.0, ((2, 16), (3, 8)), jnp.float32)
    land_mask = set_ends((jax.random.randint(key_list[2], (NY, NX), 0, 4) < 3).astype(jnp.int32), jax.random.fold_in(key_list[2], 1), 0, 1)
    mixing = jnp.clip(jnp.exp(math.log(0.25) - 1.609438 * jax.random.uniform(key_list[3], (NY, NX), jnp.float32) ** steps_of(key_list[3], (NY, NX), ((0, 16), (1, 8)), -0.2, 0.2)), 0.05, 0.25)
    owners_keys = jax.random.split(jax.random.fold_in(key_list[4], 1), NBT // NB)
    owners_turns = jax.random.permutation(jax.random.fold_in(key_list[4], 3), NBT // NB)
    owners = jax.vmap(lambda own, number: shared_out(jax.random.fold_in(key_list[4], 2), own, number, NB, N_LON * N_LAT, 1, CAP, 2))(owners_keys, owners_turns).reshape((NBT, 1))
    atm_row = set_ends(jax.random.randint(key_list[5], (NBT,), 0, ATM_ROWS), jax.random.fold_in(key_list[5], 1), 0, ATM_ROWS - 1).astype(jnp.int32)
    return dict(tracers=tracers, velocity=velocity, land_mask=land_mask, mixing=mixing, owners=owners, atm_row=atm_row)


THERMAL = 0.2
HALINE = 0.15
GRAVITY = 0.2
TIMESTEP = 0.8
VERTICAL_MIX = 0.1
VISCOSITY = 0.2
CORIOLIS_MAX = 0.3


def split_state(stacked):
    levels = (stacked.shape[0] - 1) // 4
    return stacked[:-1].reshape(4, levels, stacked.shape[1], stacked.shape[2]), stacked[-1]


def pressure(fields):
    density = HALINE * fields[1] - THERMAL * fields[0]
    return GRAVITY * (jnp.cumsum(density, axis=0) - 0.5 * density)


def coriolis_table(latitude, total_rows):
    return CORIOLIS_MAX * jnp.sin(math.pi * (-0.43 + 0.93 * (latitude + 0.5) / total_rows))


def advance(center, east_side, west_side, north_side, south_side, diffusivity, coriolis):
    fields, wet_mask = split_state(center)
    fields_east, wet_east = split_state(east_side)
    fields_west, wet_west = split_state(west_side)
    fields_north, wet_north = split_state(north_side)
    fields_south, wet_south = split_state(south_side)
    laplace = wet_east * (fields_east - fields) + wet_west * (fields_west - fields)
    laplace = laplace + wet_north * (fields_north - fields) + wet_south * (fields_south - fields)
    zonal_vel = fields[2]
    merid_vel = fields[3]
    advect = 0.5 * (zonal_vel * (fields_east - fields_west) + merid_vel * (fields_north - fields_south))
    level_above = jnp.concatenate([fields[:, :1], fields[:, :-1]], axis=1)
    level_below = jnp.concatenate([fields[:, 1:], fields[:, -1:]], axis=1)
    vertical = level_above + level_below - 2.0 * fields
    grad_east = 0.5 * (pressure(fields_east) - pressure(fields_west))
    grad_north = 0.5 * (pressure(fields_north) - pressure(fields_south))
    tend_temp = -advect[0] + diffusivity * laplace[0] + VERTICAL_MIX * vertical[0]
    tend_salt = -advect[1] + diffusivity * laplace[1] + VERTICAL_MIX * vertical[1]
    tend_zonal = -advect[2] + coriolis * merid_vel - grad_east + VISCOSITY * laplace[2] + VERTICAL_MIX * vertical[2]
    tend_merid = -advect[3] - coriolis * zonal_vel - grad_north + VISCOSITY * laplace[3] + VERTICAL_MIX * vertical[3]
    tendency = jnp.stack([tend_temp, tend_salt, tend_zonal, tend_merid])
    updated = wet_mask * (fields + TIMESTEP * tendency)
    return jnp.concatenate([updated.reshape(-1, center.shape[1], center.shape[2]), wet_mask[None]], axis=0)


def initial_state(tracers, velocity, wet_mask):
    levels = tracers.shape[1]
    rows_here, cols_here = wet_mask.shape
    return jnp.concatenate([(tracers * wet_mask).reshape(2 * levels, rows_here, cols_here),
                            (velocity * wet_mask).reshape(2 * levels, rows_here, cols_here),
                            wet_mask[None]], axis=0)


def fold_signs(levels):
    return jnp.concatenate([jnp.ones((2 * levels,), jnp.float32), -jnp.ones((2 * levels,), jnp.float32),
                            jnp.ones((1,), jnp.float32)])[:, None]


def reference(tracers, velocity, land_mask, mixing, owners, atm_row):
    wet_mask = land_mask.astype(jnp.float32)
    levels = tracers.shape[1]
    rows_total, cols_total = land_mask.shape
    stacked = initial_state(tracers, velocity, wet_mask)
    sign_rows = fold_signs(levels)
    coriolis = coriolis_table(jnp.arange(rows_total).astype(jnp.float32), rows_total)[:, None]
    for step_index in range(STEPS):
        fold_row = sign_rows * stacked[:, -1, ::-1]
        north_side = jnp.concatenate([stacked[:, 1:], fold_row[:, None]], axis=1)
        south_side = jnp.concatenate([jnp.zeros_like(stacked[:, :1]), stacked[:, :-1]], axis=1)
        east_side = jnp.roll(stacked, -1, axis=2)
        west_side = jnp.roll(stacked, 1, axis=2)
        stacked = advance(stacked, east_side, west_side, north_side, south_side, mixing, coriolis)
    fields = stacked[:-1].reshape(4, levels, rows_total, cols_total)
    surface = jnp.concatenate([fields[:, 0], wet_mask[None]], axis=0)
    blocks = surface.reshape(5, N_LAT, CY, N_LON, CX // 128, 128).transpose(3, 1, 2, 4, 0, 5).reshape(-1, 5, 128)
    segment_key = owners[:, 0] * ATM_ROWS + atm_row
    totals = jax.ops.segment_sum(blocks, segment_key, num_segments=N_LON * N_LAT * ATM_ROWS)
    ocean_count = totals[:, 4]
    atm_surface = (totals[:, :4] / jnp.maximum(ocean_count, 1.0)[:, None]).transpose(1, 0, 2)
    return fields[:2], fields[2:], atm_surface, ocean_count
```

```python
import functools
import math

import jax
import jax.numpy as jnp
from jax import lax
from jax.experimental import pallas as pl
from jax.experimental.pallas import tpu as pltpu
from jax.sharding import PartitionSpec as P

THERMAL = 0.2
HALINE = 0.15
GRAVITY = 0.2
TIMESTEP = 0.8
VERTICAL_MIX = 0.1
VISCOSITY = 0.2
CORIOLIS_MAX = 0.3
ATM_ROWS = 32

MESH = pl.DeviceIdType.MESH
ROW0 = 8
f32 = jnp.float32
bf16 = jnp.bfloat16


def iota(shape, dim):
    return lax.broadcasted_iota(jnp.int32, shape, dim)


def split3(x):
    hi = x.astype(bf16)
    rest = x - hi.astype(f32)
    mid = rest.astype(bf16)
    lo = (rest - mid.astype(f32)).astype(bf16)
    return hi, mid, lo


def dot(a, b):
    return lax.dot_general(a, b, (((1,), (0,)), ((), ())), preferred_element_type=f32)


def reverse_lanes(x):
    lane = iota(x.shape, x.ndim - 1)
    size = x.shape[-1]
    step = size // 2
    while step:
        x = jnp.where(
            (lane & step) == 0,
            pltpu.roll(x, size - step, x.ndim - 1),
            pltpu.roll(x, step, x.ndim - 1),
        )
        step //= 2
    return x


def kernel(
    n_lon, n_lat, levels, rows, cols,
    tracers, velocity, land_mask, mixing, owners, atm_row,
    tracers_out, velocity_out, surface_out, cover_out,
    x0, x1, x2, wet_pad, mask_i, mix_v, own_v, row_v,
    pack0, pack1a, pack1b, from_e0, from_w0, from_ea, from_wa, from_eb, from_wb, wet_e, wet_w,
    edge0, edge2a, edge2b, fold0, fold_wet, fold1,
    coef, onehot, out_early, in_early, out_late, in_late, row_hot, cover_v, surf_v,
    in_sem, out_sem, h_send, h_recv, a_send, a_recv, ready,
):
    devices = n_lon * n_lat
    lon = lax.axis_index("lon")
    lat = lax.axis_index("lat")
    me = lon * n_lat + lat
    top = n_lat - 1
    east = (lax.rem(lon + 1, n_lon), lat)
    west = (lax.rem(lon + n_lon - 1, n_lon), lat)
    north = (lon, lax.min(lat + 1, top))
    south = (lon, lax.max(lat - 1, 0))
    mirror = (n_lon - 1 - lon, lat)
    end = ROW0 + rows
    chunks = rows // 8

    loads = [
        pltpu.make_async_copy(land_mask, mask_i, in_sem.at[0]),
        pltpu.make_async_copy(mixing, mix_v, in_sem.at[1]),
        pltpu.make_async_copy(owners, own_v, in_sem.at[2]),
        pltpu.make_async_copy(atm_row, row_v, in_sem.at[3]),
    ]
    for f in range(4):
        src = (tracers if f < 2 else velocity).at[f % 2]
        loads.append(pltpu.make_async_copy(src, x0.at[:, f, ROW0:end, :], in_sem.at[4 + f]))
    for load in loads:
        load.start()

    barrier = pltpu.get_barrier_semaphore()
    for d in range(1, n_lon):
        pl.semaphore_signal(barrier, inc=1, device_id=(lax.rem(lon + d, n_lon), lat), device_id_type=MESH)
    for d in range(1, n_lat):
        pl.semaphore_signal(barrier, inc=1, device_id=(lon, lax.rem(lat + d, n_lat)), device_id_type=MESH)

    lane8 = iota((8, cols), 1)
    lane = iota((rows, cols), 1)
    first = lane8 == 0
    last = lane8 == cols - 1

    def part(c):
        return slice(ROW0 + 8 * c, ROW0 + 8 * c + 8)

    def packed(tile, value, i):
        where = (lane8 == 2 * i) | (lane8 == lax.rem(2 * i + cols - 1, cols))
        return jnp.where(where, pltpu.roll(value, 2 * i, 1), tile)

    loads[0].wait()
    wet = mask_i[...].astype(f32)
    wet_pad[ROW0:end, :] = wet
    for load in loads[4:]:
        load.wait()

    def prepare(k, tiles):
        tiles = list(tiles)
        for f in range(4):
            for c in range(chunks):
                q = x0[k, f, part(c), :] * wet_pad[part(c), :]
                x0[k, f, part(c), :] = q
                tiles[c] = packed(tiles[c], q, 4 * k + f)
        return tuple(tiles)

    tiles = lax.fori_loop(0, levels, prepare, tuple(jnp.zeros((8, cols), f32) for _ in range(chunks)))
    for c in range(chunks):
        pack0[8 * c : 8 * c + 8, :] = tiles[c]

    @pl.when(lat == 0)
    def _():
        x0[:, :, ROW0 - 1, :] = jnp.zeros((levels, 4, cols), f32)
        x1[:, :, ROW0 - 1, :] = jnp.zeros((levels, 4, cols), f32)
        wet_pad[ROW0 - 1 : ROW0, :] = jnp.zeros((1, cols), f32)

    pl.semaphore_wait(barrier, n_lon + n_lat - 2)

    def remote(src, dst, sem, device):
        return pltpu.make_async_remote_copy(
            src_ref=src, dst_ref=dst, send_sem=h_send.at[sem], recv_sem=h_recv.at[sem],
            device_id=device, device_id_type=MESH,
        )

    def row_copies(x, fold, lo, hi, sem):
        rows_of = lambda ref, r: ref.at[lo:hi, :, r, :]
        up = remote(rows_of(x, end - 1), rows_of(x, ROW0 - 1), sem, north)
        over = remote(rows_of(x, end - 1), fold.at[lo:hi], sem + 1, mirror)
        down = remote(rows_of(x, ROW0), rows_of(x, end), sem + 1, south)
        return up, over, down

    def start_rows(up, over, down):
        pl.when(lat < top)(up.start)
        pl.when(lat == top)(over.start)
        pl.when(lat > 0)(down.start)

    def wait_rows(up, over, down):
        pl.when(lat > 0)(up.wait_recv)
        pl.when(lat == top)(over.wait_recv)
        pl.when(lat < top)(down.wait_recv)

    def drain_rows(up, over, down):
        pl.when(lat < top)(up.wait_send)
        pl.when(lat == top)(over.wait_send)
        pl.when(lat > 0)(down.wait_send)

    def col_copies(pack, from_w, from_e, sem):
        return remote(pack, from_w, sem, east), remote(pack, from_e, sem + 1, west)

    halo0_rows = row_copies(x0, fold0, 0, levels, 0)
    halo0_cols = col_copies(pack0, from_w0, from_e0, 2)
    wet_cols = col_copies(wet_pad.at[ROW0:end, :], wet_w, wet_e, 4)
    one = lambda ref, r: ref.at[r : r + 1, :]
    wet_rows = (
        remote(one(wet_pad, end - 1), one(wet_pad, ROW0 - 1), 6, north),
        remote(one(wet_pad, end - 1), fold_wet, 7, mirror),
        remote(one(wet_pad, ROW0), one(wet_pad, end), 7, south),
    )
    start_rows(*halo0_rows)
    for copy in halo0_cols + wet_cols:
        copy.start()
    start_rows(*wet_rows)

    for d in range(1, n_lat):
        pl.semaphore_signal(ready, inc=1, device_id=(lon, lax.rem(lat + d, n_lat)), device_id_type=MESH)

    loads[2].wait()
    loads[3].wait()
    blocks = rows
    pad_row = lambda ref: jnp.concatenate([ref[...].astype(f32)] * (cols // blocks), axis=1)
    own_lane = pad_row(own_v)
    row_lane = pad_row(row_v)
    sub = iota((blocks, cols), 0)
    own_col = jnp.sum(jnp.where(lane == sub, own_lane, 0.0), axis=1, keepdims=True)
    row_col = jnp.sum(jnp.where(lane == sub, row_lane + 1.0, 0.0), axis=1, keepdims=True)
    same = jnp.where((own_col == own_lane) & (sub < lax.rem(lane, blocks)), 1.0, 0.0)
    position = jnp.sum(same, axis=0, keepdims=True)
    lane1 = iota((1, cols), 1)
    target = own_lane.astype(jnp.int32) * 8 + (lane1 // blocks) * 2 + position.astype(jnp.int32)
    onehot[...] = jnp.where(iota((devices * 8, cols), 0) == target, 1.0, 0.0).astype(bf16)
    early = jnp.concatenate(
        [wet, jnp.broadcast_to(row_col, (blocks, cols)), jnp.zeros((2 * blocks, cols), f32)], axis=0
    )
    out_early[...] = dot(onehot[...], early.astype(bf16)).reshape(devices, 8, cols)
    in_early[pl.ds(me, 1)] = out_early[pl.ds(me, 1)]

    latitude = (lat * rows + iota((rows, cols), 0)).astype(f32)
    coriolis = CORIOLIS_MAX * jnp.sin(math.pi * (-0.43 + 0.93 * (latitude + 0.5) / (n_lat * rows)))
    loads[1].wait()

    for copy in wet_cols:
        copy.wait_recv()
    wait_rows(*wet_rows)

    @pl.when(lat == top)
    def _():
        wet_pad[end : end + 1, :] = reverse_lanes(jnp.broadcast_to(fold_wet[...], (8, cols)))[0:1]

    w_east = pltpu.roll(jnp.where(lane == 0, wet_e[...], wet), cols - 1, 1)
    w_west = pltpu.roll(jnp.where(lane == cols - 1, wet_w[...], wet), 1, 1)
    w_north = wet_pad[ROW0 + 1 : end + 1, :]
    w_south = wet_pad[ROW0 - 1 : end - 1, :]
    total = w_east + w_west + w_north + w_south
    centre = 1.0 - 2.0 * TIMESTEP * VERTICAL_MIX
    for base, rate in ((0, TIMESTEP * mix_v[...]), (5, TIMESTEP * VISCOSITY)):
        coef[base] = wet * (centre - rate * total)
        for j, w in enumerate((w_east, w_west, w_north, w_south)):
            coef[base + 1 + j] = wet * (rate * w)
    coef[10] = (TIMESTEP * VERTICAL_MIX) * wet
    coef[11] = TIMESTEP * coriolis * wet

    pressure_rate = 0.5 * TIMESTEP * GRAVITY
    assert abs(pressure_rate - TIMESTEP * VERTICAL_MIX) < 1e-12

    def level(x, k, edge, carry, store):
        above = lax.max(k - 1, 0) if not isinstance(k, int) else max(k - 1, 0)
        below = lax.min(k + 1, levels - 1) if not isinstance(k, int) else min(k + 1, levels - 1)
        carry = list(carry)
        for c in range(chunks):
            mid, up, down = part(c), slice(ROW0 + 8 * c + 1, ROW0 + 8 * c + 9), slice(ROW0 + 8 * c - 1, ROW0 + 8 * c + 7)
            own = slice(8 * c, 8 * c + 8)
            halo = edge[own, :]
            q, e, w, n, s = [], [], [], [], []
            for f in range(4):
                value = x[k, f, mid, :]
                side = pltpu.roll(halo, lax.rem(2 * cols - 2 * (4 * k + f), cols), 1)
                q.append(value)
                e.append(pltpu.roll(jnp.where(first, side, value), cols - 1, 1))
                w.append(pltpu.roll(jnp.where(last, side, value), 1, 1))
                n.append(x[k, f, up, :])
                s.append(x[k, f, down, :])
            gx = HALINE * (e[1] - w[1]) - THERMAL * (e[0] - w[0])
            gy = HALINE * (n[1] - s[1]) - THERMAL * (n[0] - s[0])
            sx = carry[2 * c] + gx
            sy = carry[2 * c + 1] + gy
            carry[2 * c], carry[2 * c + 1] = sx, sy
            push = (None, None, sx - 0.5 * gx, sy - 0.5 * gy)
            u = (0.5 * TIMESTEP) * q[2]
            v = (0.5 * TIMESTEP) * q[3]
            vert = coef[10, own, :]
            turn = coef[11, own, :]
            for f in range(4):
                if f % 2 == 0:
                    base = 0 if f == 0 else 5
                    a = coef[base, own, :]
                    ce = coef[base + 1, own, :] - u
                    cw = coef[base + 2, own, :] + u
                    cn = coef[base + 3, own, :] - v
                    cs = coef[base + 4, own, :] + v
                column = x[above, f, mid, :] + x[below, f, mid, :]
                if f >= 2:
                    column = column - push[f]
                value = (a * q[f] + vert * column) + (ce * e[f] + cw * w[f]) + (cn * n[f] + cs * s[f])
                if f == 2:
                    value = value + turn * q[3]
                if f == 3:
                    value = value - turn * q[2]
                store(k, f, c, value)
        return tuple(carry)

    def merge(edge, from_e, from_w):
        edge[...] = jnp.where(lax.rem(lane, 2) == 0, from_e[...], from_w[...])

    def unfold(x, fold, lo, hi):
        @pl.when(lat == top)
        def _():
            for k in range(lo, hi, 2):
                width = min(2, hi - k)
                pair = fold[k : k + width].reshape(4 * width, cols)
                pair = reverse_lanes(pair)
                field = lax.rem(iota(pair.shape, 0), 4)
                pair = jnp.where(field < 2, pair, -pair)
                for j in range(width):
                    for f in range(4):
                        x[k + j, f, end : end + 1, :] = pair[4 * j + f : 4 * j + f + 1]

    for copy in halo0_cols:
        copy.wait_recv()
    wait_rows(*halo0_rows)
    merge(edge0, from_e0, from_w0)
    unfold(x0, fold0, 0, levels)

    zeros = tuple(jnp.zeros((8, cols), f32) for _ in range(2 * chunks))
    empty = [jnp.zeros((8, cols), f32) for _ in range(chunks)]

    def step1(k, carry, tiles):
        tiles = list(tiles)

        def store(k, f, c, value):
            x1[k, f, part(c), :] = value
            tiles[c] = packed(tiles[c], value, 4 * k + f)

        carry = level(x0, k, edge0, carry, store)
        return carry, tuple(tiles)

    carry, tiles = step1(0, zeros, empty)
    for c in range(chunks):
        pack1a[8 * c : 8 * c + 8, :] = tiles[c]
    halo1_rows = row_copies(x1, fold1, 0, 1, 8)
    halo1_cols = col_copies(pack1a, from_wa, from_ea, 10)
    start_rows(*halo1_rows)
    for copy in halo1_cols:
        copy.start()

    pl.semaphore_wait(ready, n_lat - 1)

    def exchange(out, into, sem, height):
        def copy(d):
            peer = lax.rem(me + d, devices)
            return pltpu.make_async_remote_copy(
                src_ref=out.at[peer, 0:height, :], dst_ref=into.at[me, 0:height, :],
                send_sem=a_send.at[sem], recv_sem=a_recv.at[sem],
                device_id=(peer // n_lat, lax.rem(peer, n_lat)), device_id_type=MESH,
            )

        def go(d, _):
            copy(d).start()
            return 0

        lax.fori_loop(1, devices, go, 0)
        return pltpu.make_async_remote_copy(
            src_ref=out.at[0 : devices - 1, 0:height, :], dst_ref=into.at[0 : devices - 1, 0:height, :],
            send_sem=a_send.at[sem], recv_sem=a_recv.at[sem],
            device_id=east, device_id_type=MESH,
        )

    early_all = exchange(out_early, in_early, 0, 4)

    carry, tiles = lax.fori_loop(1, levels, lambda k, s: step1(k, *s), (carry, tiles))
    for c in range(chunks):
        pack1b[8 * c : 8 * c + 8, :] = tiles[c]
    halo2_rows = row_copies(x1, fold1, 1, levels, 12)
    halo2_cols = col_copies(pack1b, from_wb, from_eb, 14)
    start_rows(*halo2_rows)
    for copy in halo2_cols:
        copy.start()

    for copy in halo1_cols:
        copy.wait_recv()
    wait_rows(*halo1_rows)
    merge(edge2a, from_ea, from_wa)
    unfold(x1, fold1, 0, 1)

    def store2(k, f, c, value):
        x2[k, f, 8 * c : 8 * c + 8, :] = value

    carry = level(x1, 0, edge2a, zeros, store2)
    surf = x2[0].reshape(4 * rows, cols)
    hot = onehot[...]
    late = sum(dot(hot, piece) for piece in split3(surf))
    out_late[...] = late.reshape(devices, 8, cols)
    in_late[pl.ds(me, 1)] = out_late[pl.ds(me, 1)]
    late_all = exchange(out_late, in_late, 1, 8)

    for copy in halo2_cols:
        copy.wait_recv()
    wait_rows(*halo2_rows)
    merge(edge2b, from_eb, from_wb)
    unfold(x1, fold1, 1, levels)
    lax.fori_loop(1, levels, lambda k, s: level(x1, k, edge2b, s, store2), carry)
    stores = []
    for f in range(4):
        dst = (tracers_out if f < 2 else velocity_out).at[f % 2]
        stores.append(pltpu.make_async_copy(x2.at[:, f], dst, out_sem.at[f]))
        stores[-1].start()

    early_all.wait_recv()
    tile = (cols // 8, 8, cols)
    sub3 = iota(tile, 1)
    lane3 = iota(tile, 2)
    keep = (sub3 // 2) == (lane3 // ATM_ROWS)
    wanted = (lax.rem(lane3, ATM_ROWS) + 1).astype(f32)
    for j in range(devices * 8 // cols):
        got = in_early[tile[0] * j : tile[0] * (j + 1)]
        ids = jnp.where((sub3 // 2) == 1, got, 0.0)
        ids = (ids + pltpu.roll(ids, 2, 1)) + (pltpu.roll(ids, 4, 1) + pltpu.roll(ids, 6, 1))
        hit = jnp.where(keep & (ids == wanted), 1.0, 0.0)
        row_hot[:, cols * j : cols * (j + 1)] = hit.reshape(cols, cols).T.astype(bf16)
    wets = jnp.where(iota((devices, 8, cols), 1) < 2, in_early[...], 0.0)
    cover = dot(row_hot[0:ATM_ROWS, :], wets.reshape(devices * 8, cols).astype(bf16))
    cover_v[...] = cover
    share = 1.0 / jnp.maximum(cover, 1.0)
    stores.append(pltpu.make_async_copy(cover_v, cover_out, out_sem.at[4]))
    stores[-1].start()

    late_all.wait_recv()
    placed = row_hot[...]
    sums = sum(dot(placed, piece) for piece in split3(in_late[...].reshape(devices * 8, cols)))
    surf_v[...] = sums.reshape(4, ATM_ROWS, cols) * share
    stores.append(pltpu.make_async_copy(surf_v, surface_out, out_sem.at[5]))
    stores[-1].start()

    drain_rows(*halo0_rows)
    drain_rows(*wet_rows)
    drain_rows(*halo1_rows)
    drain_rows(*halo2_rows)
    for copy in halo0_cols + wet_cols + halo1_cols + halo2_cols:
        copy.wait_send()
    early_all.wait_send()
    late_all.wait_send()
    for store in stores:
        store.wait()


def local(tracers, velocity, land_mask, mixing, owners, atm_row):
    n_lon, n_lat = lax.axis_size("lon"), lax.axis_size("lat")
    levels = tracers.shape[1]
    rows, cols = land_mask.shape
    devices = n_lon * n_lat
    blocks = rows * cols // 128
    assert cols == 128 and blocks == rows and ATM_ROWS == 32
    any_spec = pl.BlockSpec(memory_space=pl.ANY)
    vmem = lambda *shape: pltpu.VMEM(shape, f32)
    tile = vmem(rows, cols)
    padded = rows + 16
    scratch = (
        [vmem(levels, 4, padded, cols)] * 2
        + [vmem(levels, 4, rows, cols), vmem(padded, cols)]
        + [pltpu.VMEM((rows, cols), jnp.int32), tile]
        + [pltpu.VMEM((1, blocks), jnp.int32)] * 2
        + [tile] * 14
        + [vmem(levels, 4, cols), vmem(1, cols), vmem(levels, 4, cols)]
        + [vmem(12, rows, cols), pltpu.VMEM((devices * 8, cols), bf16)]
        + [vmem(devices, 8, cols)] * 4
        + [pltpu.VMEM((4 * ATM_ROWS, devices * 8), bf16), tile, vmem(4, ATM_ROWS, cols)]
        + [pltpu.SemaphoreType.DMA((8,)), pltpu.SemaphoreType.DMA((6,))]
        + [pltpu.SemaphoreType.DMA((16,))] * 2
        + [pltpu.SemaphoreType.DMA((2,))] * 2
        + [pltpu.SemaphoreType.REGULAR]
    )
    return pl.pallas_call(
        functools.partial(kernel, n_lon, n_lat, levels, rows, cols),
        out_shape=(
            jax.ShapeDtypeStruct(tracers.shape, f32),
            jax.ShapeDtypeStruct(velocity.shape, f32),
            jax.ShapeDtypeStruct((4, ATM_ROWS, cols), f32),
            jax.ShapeDtypeStruct((ATM_ROWS, cols), f32),
        ),
        in_specs=[any_spec] * 6,
        out_specs=(any_spec,) * 4,
        scratch_shapes=scratch,
        compiler_params=pltpu.CompilerParams(collective_id=0, has_side_effects=True),
        name="ocean",
    )(tracers, velocity, land_mask, mixing, owners.reshape(1, blocks), atm_row.reshape(1, blocks))


def solution(mesh):
    in_specs = (
        P(None, None, "lat", "lon"),
        P(None, None, "lat", "lon"),
        P("lat", "lon"),
        P("lat", "lon"),
        P(("lon", "lat"), None),
        P(("lon", "lat")),
    )
    out_specs = (
        P(None, None, "lat", "lon"),
        P(None, None, "lat", "lon"),
        P(None, ("lon", "lat"), None),
        P(("lon", "lat"), None),
    )
    return jax.shard_map(local, mesh=mesh, in_specs=in_specs, out_specs=out_specs, check_vma=False)
```

```python
import functools
import math

import jax
import jax.numpy as jnp
from jax import lax
from jax.experimental import pallas as pl
from jax.experimental.pallas import tpu as pltpu
from jax.sharding import PartitionSpec as P

THERMAL = 0.2
HALINE = 0.15
GRAVITY = 0.2
TIMESTEP = 0.8
VERTICAL_MIX = 0.1
VISCOSITY = 0.2
CORIOLIS_MAX = 0.3
ATM_ROWS = 32

MESH = pl.DeviceIdType.MESH
ROW0 = 8
f32 = jnp.float32
bf16 = jnp.bfloat16


def iota(shape, dim):
    return lax.broadcasted_iota(jnp.int32, shape, dim)


def split3(x):
    hi = x.astype(bf16)
    rest = x - hi.astype(f32)
    mid = rest.astype(bf16)
    lo = (rest - mid.astype(f32)).astype(bf16)
    return hi, mid, lo


def dot(a, b):
    return lax.dot_general(a, b, (((1,), (0,)), ((), ())), preferred_element_type=f32)


def reverse_lanes(x):
    lane = iota(x.shape, x.ndim - 1)
    size = x.shape[-1]
    step = size // 2
    while step:
        x = jnp.where(
            (lane & step) == 0,
            pltpu.roll(x, size - step, x.ndim - 1),
            pltpu.roll(x, step, x.ndim - 1),
        )
        step //= 2
    return x


def kernel(
    n_lon, n_lat, levels, rows, cols,
    tracers, velocity, land_mask, mixing, owners, atm_row,
    x2, surf_v, cover_v,
    x0, x1, wet_pad, mask_i, mix_v, own_v, row_v,
    pack0, pack1a, pack1b, from_e0, from_w0, from_ea, from_wa, from_eb, from_wb, wet_e, wet_w,
    edge0, edge2a, edge2b, fold0, fold_wet, fold1,
    coef, onehot, out_early, in_early, out_late, in_late, row_hot,
    in_sem, h_send, h_recv, a_send, a_recv, ready,
):
    devices = n_lon * n_lat
    lon = lax.axis_index("lon")
    lat = lax.axis_index("lat")
    me = lon * n_lat + lat
    top = n_lat - 1
    east = (lax.rem(lon + 1, n_lon), lat)
    west = (lax.rem(lon + n_lon - 1, n_lon), lat)
    north = (lon, lax.min(lat + 1, top))
    south = (lon, lax.max(lat - 1, 0))
    mirror = (n_lon - 1 - lon, lat)
    end = ROW0 + rows
    chunks = rows // 8

    loads = [
        pltpu.make_async_copy(land_mask, mask_i, in_sem.at[0]),
        pltpu.make_async_copy(mixing, mix_v, in_sem.at[1]),
        pltpu.make_async_copy(owners, own_v, in_sem.at[2]),
        pltpu.make_async_copy(atm_row, row_v, in_sem.at[3]),
    ]
    for f in range(4):
        src = (tracers if f < 2 else velocity).at[f % 2]
        loads.append(pltpu.make_async_copy(src, x0.at[:, f, ROW0:end, :], in_sem.at[4 + f]))
    for load in loads:
        load.start()

    barrier = pltpu.get_barrier_semaphore()
    for d in range(1, n_lon):
        pl.semaphore_signal(barrier, inc=1, device_id=(lax.rem(lon + d, n_lon), lat), device_id_type=MESH)
    for d in range(1, n_lat):
        pl.semaphore_signal(barrier, inc=1, device_id=(lon, lax.rem(lat + d, n_lat)), device_id_type=MESH)

    lane8 = iota((8, cols), 1)
    lane = iota((rows, cols), 1)
    first = lane8 == 0
    last = lane8 == cols - 1

    def part(c):
        return slice(ROW0 + 8 * c, ROW0 + 8 * c + 8)

    def packed(tile, value, i):
        where = (lane8 == 2 * i) | (lane8 == lax.rem(2 * i + cols - 1, cols))
        return jnp.where(where, pltpu.roll(value, 2 * i, 1), tile)

    loads[0].wait()
    wet = mask_i[...].astype(f32)
    wet_pad[ROW0:end, :] = wet
    for load in loads[4:]:
        load.wait()

    def prepare(k, tiles):
        tiles = list(tiles)
        for f in range(4):
            for c in range(chunks):
                q = x0[k, f, part(c), :] * wet_pad[part(c), :]
                x0[k, f, part(c), :] = q
                tiles[c] = packed(tiles[c], q, 4 * k + f)
        return tuple(tiles)

    tiles = lax.fori_loop(0, levels, prepare, tuple(jnp.zeros((8, cols), f32) for _ in range(chunks)))
    for c in range(chunks):
        pack0[8 * c : 8 * c + 8, :] = tiles[c]

    @pl.when(lat == 0)
    def _():
        x0[:, :, ROW0 - 1, :] = jnp.zeros((levels, 4, cols), f32)
        x1[:, :, ROW0 - 1, :] = jnp.zeros((levels, 4, cols), f32)
        wet_pad[ROW0 - 1 : ROW0, :] = jnp.zeros((1, cols), f32)

    pl.semaphore_wait(barrier, n_lon + n_lat - 2)

    def remote(src, dst, sem, device):
        return pltpu.make_async_remote_copy(
            src_ref=src, dst_ref=dst, send_sem=h_send.at[sem], recv_sem=h_recv.at[sem],
            device_id=device, device_id_type=MESH,
        )

    def row_copies(x, fold, lo, hi, sem):
        rows_of = lambda ref, r: ref.at[lo:hi, :, r, :]
        up = remote(rows_of(x, end - 1), rows_of(x, ROW0 - 1), sem, north)
        over = remote(rows_of(x, end - 1), fold.at[lo:hi], sem + 1, mirror)
        down = remote(rows_of(x, ROW0), rows_of(x, end), sem + 1, south)
        return up, over, down

    def start_rows(up, over, down):
        pl.when(lat < top)(up.start)
        pl.when(lat == top)(over.start)
        pl.when(lat > 0)(down.start)

    def wait_rows(up, over, down):
        pl.when(lat > 0)(up.wait_recv)
        pl.when(lat == top)(over.wait_recv)
        pl.when(lat < top)(down.wait_recv)

    def drain_rows(up, over, down):
        pl.when(lat < top)(up.wait_send)
        pl.when(lat == top)(over.wait_send)
        pl.when(lat > 0)(down.wait_send)

    def col_copies(pack, from_w, from_e, sem):
        return remote(pack, from_w, sem, east), remote(pack, from_e, sem + 1, west)

    halo0_rows = row_copies(x0, fold0, 0, levels, 0)
    halo0_cols = col_copies(pack0, from_w0, from_e0, 2)
    wet_cols = col_copies(wet_pad.at[ROW0:end, :], wet_w, wet_e, 4)
    one = lambda ref, r: ref.at[r : r + 1, :]
    wet_rows = (
        remote(one(wet_pad, end - 1), one(wet_pad, ROW0 - 1), 6, north),
        remote(one(wet_pad, end - 1), fold_wet, 7, mirror),
        remote(one(wet_pad, ROW0), one(wet_pad, end), 7, south),
    )
    start_rows(*halo0_rows)
    for copy in halo0_cols + wet_cols:
        copy.start()
    start_rows(*wet_rows)

    for d in range(1, n_lat):
        pl.semaphore_signal(ready, inc=1, device_id=(lon, lax.rem(lat + d, n_lat)), device_id_type=MESH)

    loads[2].wait()
    loads[3].wait()
    blocks = rows
    pad_row = lambda ref: jnp.concatenate([ref[...].astype(f32)] * (cols // blocks), axis=1)
    own_lane = pad_row(own_v)
    row_lane = pad_row(row_v)
    sub = iota((blocks, cols), 0)
    own_col = jnp.sum(jnp.where(lane == sub, own_lane, 0.0), axis=1, keepdims=True)
    row_col = jnp.sum(jnp.where(lane == sub, row_lane + 1.0, 0.0), axis=1, keepdims=True)
    same = jnp.where((own_col == own_lane) & (sub < lax.rem(lane, blocks)), 1.0, 0.0)
    position = jnp.sum(same, axis=0, keepdims=True)
    lane1 = iota((1, cols), 1)
    target = own_lane.astype(jnp.int32) * 8 + (lane1 // blocks) * 2 + position.astype(jnp.int32)
    onehot[...] = jnp.where(iota((devices * 8, cols), 0) == target, 1.0, 0.0).astype(bf16)
    early = jnp.concatenate(
        [wet, jnp.broadcast_to(row_col, (blocks, cols)), jnp.zeros((2 * blocks, cols), f32)], axis=0
    )
    out_early[...] = dot(onehot[...], early.astype(bf16)).reshape(devices, 8, cols)
    in_early[pl.ds(me, 1)] = out_early[pl.ds(me, 1)]

    latitude = (lat * rows + iota((rows, cols), 0)).astype(f32)
    coriolis = CORIOLIS_MAX * jnp.sin(math.pi * (-0.43 + 0.93 * (latitude + 0.5) / (n_lat * rows)))
    loads[1].wait()

    for copy in wet_cols:
        copy.wait_recv()
    wait_rows(*wet_rows)

    @pl.when(lat == top)
    def _():
        wet_pad[end : end + 1, :] = reverse_lanes(jnp.broadcast_to(fold_wet[...], (8, cols)))[0:1]

    w_east = pltpu.roll(jnp.where(lane == 0, wet_e[...], wet), cols - 1, 1)
    w_west = pltpu.roll(jnp.where(lane == cols - 1, wet_w[...], wet), 1, 1)
    w_north = wet_pad[ROW0 + 1 : end + 1, :]
    w_south = wet_pad[ROW0 - 1 : end - 1, :]
    total = w_east + w_west + w_north + w_south
    centre = 1.0 - 2.0 * TIMESTEP * VERTICAL_MIX
    for base, rate in ((0, TIMESTEP * mix_v[...]), (5, TIMESTEP * VISCOSITY)):
        coef[base] = wet * (centre - rate * total)
        for j, w in enumerate((w_east, w_west, w_north, w_south)):
            coef[base + 1 + j] = wet * (rate * w)
    coef[10] = (TIMESTEP * VERTICAL_MIX) * wet
    coef[11] = TIMESTEP * coriolis * wet

    pressure_rate = 0.5 * TIMESTEP * GRAVITY
    assert abs(pressure_rate - TIMESTEP * VERTICAL_MIX) < 1e-12

    def level(x, k, edge, carry, store):
        above = lax.max(k - 1, 0) if not isinstance(k, int) else max(k - 1, 0)
        below = lax.min(k + 1, levels - 1) if not isinstance(k, int) else min(k + 1, levels - 1)
        carry = list(carry)
        for c in range(chunks):
            mid, up, down = part(c), slice(ROW0 + 8 * c + 1, ROW0 + 8 * c + 9), slice(ROW0 + 8 * c - 1, ROW0 + 8 * c + 7)
            own = slice(8 * c, 8 * c + 8)
            halo = edge[own, :]
            q, e, w, n, s = [], [], [], [], []
            for f in range(4):
                value = x[k, f, mid, :]
                side = pltpu.roll(halo, lax.rem(2 * cols - 2 * (4 * k + f), cols), 1)
                q.append(value)
                e.append(pltpu.roll(jnp.where(first, side, value), cols - 1, 1))
                w.append(pltpu.roll(jnp.where(last, side, value), 1, 1))
                n.append(x[k, f, up, :])
                s.append(x[k, f, down, :])
            gx = HALINE * (e[1] - w[1]) - THERMAL * (e[0] - w[0])
            gy = HALINE * (n[1] - s[1]) - THERMAL * (n[0] - s[0])
            sx = carry[2 * c] + gx
            sy = carry[2 * c + 1] + gy
            carry[2 * c], carry[2 * c + 1] = sx, sy
            push = (None, None, sx - 0.5 * gx, sy - 0.5 * gy)
            u = (0.5 * TIMESTEP) * q[2]
            v = (0.5 * TIMESTEP) * q[3]
            vert = coef[10, own, :]
            turn = coef[11, own, :]
            for f in range(4):
                if f % 2 == 0:
                    base = 0 if f == 0 else 5
                    a = coef[base, own, :]
                    ce = coef[base + 1, own, :] - u
                    cw = coef[base + 2, own, :] + u
                    cn = coef[base + 3, own, :] - v
                    cs = coef[base + 4, own, :] + v
                column = x[above, f, mid, :] + x[below, f, mid, :]
                if f >= 2:
                    column = column - push[f]
                value = (a * q[f] + vert * column) + (ce * e[f] + cw * w[f]) + (cn * n[f] + cs * s[f])
                if f == 2:
                    value = value + turn * q[3]
                if f == 3:
                    value = value - turn * q[2]
                store(k, f, c, value)
        return tuple(carry)

    def merge(edge, from_e, from_w):
        edge[...] = jnp.where(lax.rem(lane, 2) == 0, from_e[...], from_w[...])

    def unfold(x, fold, lo, hi):
        @pl.when(lat == top)
        def _():
            for k in range(lo, hi, 2):
                width = min(2, hi - k)
                pair = fold[k : k + width].reshape(4 * width, cols)
                pair = reverse_lanes(pair)
                field = lax.rem(iota(pair.shape, 0), 4)
                pair = jnp.where(field < 2, pair, -pair)
                for j in range(width):
                    for f in range(4):
                        x[k + j, f, end : end + 1, :] = pair[4 * j + f : 4 * j + f + 1]

    for copy in halo0_cols:
        copy.wait_recv()
    wait_rows(*halo0_rows)
    merge(edge0, from_e0, from_w0)
    unfold(x0, fold0, 0, levels)

    zeros = tuple(jnp.zeros((8, cols), f32) for _ in range(2 * chunks))
    empty = [jnp.zeros((8, cols), f32) for _ in range(chunks)]

    def step1(k, carry, tiles):
        tiles = list(tiles)

        def store(k, f, c, value):
            x1[k, f, part(c), :] = value
            tiles[c] = packed(tiles[c], value, 4 * k + f)

        carry = level(x0, k, edge0, carry, store)
        return carry, tuple(tiles)

    carry, tiles = step1(0, zeros, empty)
    for c in range(chunks):
        pack1a[8 * c : 8 * c + 8, :] = tiles[c]
    halo1_rows = row_copies(x1, fold1, 0, 1, 8)
    halo1_cols = col_copies(pack1a, from_wa, from_ea, 10)
    start_rows(*halo1_rows)
    for copy in halo1_cols:
        copy.start()

    pl.semaphore_wait(ready, n_lat - 1)

    def exchange(out, into, sem, height):
        def copy(d):
            peer = lax.rem(me + d, devices)
            return pltpu.make_async_remote_copy(
                src_ref=out.at[peer, 0:height, :], dst_ref=into.at[me, 0:height, :],
                send_sem=a_send.at[sem], recv_sem=a_recv.at[sem],
                device_id=(peer // n_lat, lax.rem(peer, n_lat)), device_id_type=MESH,
            )

        for d in range(1, devices):
            copy(d).start()
        return pltpu.make_async_remote_copy(
            src_ref=out.at[0 : devices - 1, 0:height, :], dst_ref=into.at[0 : devices - 1, 0:height, :],
            send_sem=a_send.at[sem], recv_sem=a_recv.at[sem],
            device_id=east, device_id_type=MESH,
        )

    early_all = exchange(out_early, in_early, 0, 4)

    carry, tiles = lax.fori_loop(1, levels, lambda k, s: step1(k, *s), (carry, tiles))
    for c in range(chunks):
        pack1b[8 * c : 8 * c + 8, :] = tiles[c]
    halo2_rows = row_copies(x1, fold1, 1, levels, 12)
    halo2_cols = col_copies(pack1b, from_wb, from_eb, 14)
    start_rows(*halo2_rows)
    for copy in halo2_cols:
        copy.start()

    for copy in halo1_cols:
        copy.wait_recv()
    wait_rows(*halo1_rows)
    merge(edge2a, from_ea, from_wa)
    unfold(x1, fold1, 0, 1)

    def store2(k, f, c, value):
        x2[k, f, 8 * c : 8 * c + 8, :] = value

    carry = level(x1, 0, edge2a, zeros, store2)
    surf = x2[0].reshape(4 * rows, cols)
    hot = onehot[...]
    late = sum(dot(hot, piece) for piece in split3(surf))
    out_late[...] = late.reshape(devices, 8, cols)
    in_late[pl.ds(me, 1)] = out_late[pl.ds(me, 1)]
    late_all = exchange(out_late, in_late, 1, 8)

    for copy in halo2_cols:
        copy.wait_recv()
    wait_rows(*halo2_rows)
    merge(edge2b, from_eb, from_wb)
    unfold(x1, fold1, 1, levels)
    lax.fori_loop(1, levels, lambda k, s: level(x1, k, edge2b, s, store2), carry)
    early_all.wait_recv()
    tile = (cols // 8, 8, cols)
    sub3 = iota(tile, 1)
    lane3 = iota(tile, 2)
    keep = (sub3 // 2) == (lane3 // ATM_ROWS)
    wanted = (lax.rem(lane3, ATM_ROWS) + 1).astype(f32)
    for j in range(devices * 8 // cols):
        got = in_early[tile[0] * j : tile[0] * (j + 1)]
        ids = jnp.where((sub3 // 2) == 1, got, 0.0)
        ids = (ids + pltpu.roll(ids, 2, 1)) + (pltpu.roll(ids, 4, 1) + pltpu.roll(ids, 6, 1))
        hit = jnp.where(keep & (ids == wanted), 1.0, 0.0)
        row_hot[:, cols * j : cols * (j + 1)] = hit.reshape(cols, cols).T.astype(bf16)
    wets = jnp.where(iota((devices, 8, cols), 1) < 2, in_early[...], 0.0)
    cover = dot(row_hot[0:ATM_ROWS, :], wets.reshape(devices * 8, cols).astype(bf16))
    cover_v[...] = cover
    share = 1.0 / jnp.maximum(cover, 1.0)

    late_all.wait_recv()
    placed = row_hot[...]
    sums = sum(dot(placed, piece) for piece in split3(in_late[...].reshape(devices * 8, cols)))
    surf_v[...] = sums.reshape(4, ATM_ROWS, cols) * share

    drain_rows(*halo0_rows)
    drain_rows(*wet_rows)
    drain_rows(*halo1_rows)
    drain_rows(*halo2_rows)
    for copy in halo0_cols + wet_cols + halo1_cols + halo2_cols:
        copy.wait_send()
    early_all.wait_send()
    late_all.wait_send()


def write_out(x2, surf_v, cover_v, tracers_out, velocity_out, surface_out, cover_out, sem):
    stores = []
    for f in range(4):
        dst = (tracers_out if f < 2 else velocity_out).at[f % 2]
        stores.append(pltpu.make_async_copy(x2.at[:, f], dst, sem.at[f]))
    stores.append(pltpu.make_async_copy(cover_v, cover_out, sem.at[4]))
    stores.append(pltpu.make_async_copy(surf_v, surface_out, sem.at[5]))
    for store in stores:
        store.start()
    for store in stores:
        store.wait()


def local(tracers, velocity, land_mask, mixing, owners, atm_row):
    n_lon, n_lat = lax.axis_size("lon"), lax.axis_size("lat")
    levels = tracers.shape[1]
    rows, cols = land_mask.shape
    devices = n_lon * n_lat
    blocks = rows * cols // 128
    assert cols == 128 and blocks == rows and ATM_ROWS == 32
    any_spec = pl.BlockSpec(memory_space=pl.ANY)
    vmem = lambda *shape: pltpu.VMEM(shape, f32)
    tile = vmem(rows, cols)
    padded = rows + 16
    scratch = (
        [vmem(levels, 4, padded, cols)] * 2
        + [vmem(padded, cols)]
        + [pltpu.VMEM((rows, cols), jnp.int32), tile]
        + [pltpu.VMEM((1, blocks), jnp.int32)] * 2
        + [tile] * 14
        + [vmem(levels, 4, cols), vmem(1, cols), vmem(levels, 4, cols)]
        + [vmem(12, rows, cols), pltpu.VMEM((devices * 8, cols), bf16)]
        + [vmem(devices, 8, cols)] * 4
        + [pltpu.VMEM((4 * ATM_ROWS, devices * 8), bf16)]
        + [pltpu.SemaphoreType.DMA((8,))]
        + [pltpu.SemaphoreType.DMA((16,))] * 2
        + [pltpu.SemaphoreType.DMA((2,))] * 2
        + [pltpu.SemaphoreType.REGULAR]
    )
    held = pl.pallas_call(
        functools.partial(kernel, n_lon, n_lat, levels, rows, cols),
        out_shape=(vmem(levels, 4, rows, cols), vmem(4, ATM_ROWS, cols), vmem(ATM_ROWS, cols)),
        in_specs=[any_spec] * 6,
        scratch_shapes=scratch,
        compiler_params=pltpu.CompilerParams(collective_id=0, has_side_effects=True),
        name="ocean",
    )(tracers, velocity, land_mask, mixing, owners.reshape(1, blocks), atm_row.reshape(1, blocks))
    return pl.pallas_call(
        write_out,
        out_shape=(
            jax.ShapeDtypeStruct(tracers.shape, f32),
            jax.ShapeDtypeStruct(velocity.shape, f32),
            jax.ShapeDtypeStruct((4, ATM_ROWS, cols), f32),
            jax.ShapeDtypeStruct((ATM_ROWS, cols), f32),
        ),
        in_specs=[pl.BlockSpec(memory_space=pltpu.VMEM)] * 3,
        out_specs=(any_spec,) * 4,
        scratch_shapes=[pltpu.SemaphoreType.DMA((6,))],
        name="write_out",
    )(*(pltpu.with_memory_space_constraint(x, pltpu.VMEM) for x in held))


def solution(mesh):
    in_specs = (
        P(None, None, "lat", "lon"),
        P(None, None, "lat", "lon"),
        P("lat", "lon"),
        P("lat", "lon"),
        P(("lon", "lat"), None),
        P(("lon", "lat")),
    )
    out_specs = (
        P(None, None, "lat", "lon"),
        P(None, None, "lat", "lon"),
        P(None, ("lon", "lat"), None),
        P(("lon", "lat"), None),
    )
    return jax.shard_map(local, mesh=mesh, in_specs=in_specs, out_specs=out_specs, check_vma=False)
```

```python
import functools
import math

import jax
import jax.numpy as jnp
from jax import lax
from jax.experimental import pallas as pl
from jax.experimental.pallas import tpu as pltpu
from jax.sharding import PartitionSpec as P

THERMAL = 0.2
HALINE = 0.15
GRAVITY = 0.2
TIMESTEP = 0.8
VERTICAL_MIX = 0.1
VISCOSITY = 0.2
CORIOLIS_MAX = 0.3
ATM_ROWS = 32
UNROLL1, UNROLL2 = 2, 3
PIECES = 3

MESH = pl.DeviceIdType.MESH
ROW0 = 8
f32 = jnp.float32
bf16 = jnp.bfloat16


def iota(shape, dim):
    return lax.broadcasted_iota(jnp.int32, shape, dim)


def split(x):
    hi = x.astype(bf16)
    rest = x - hi.astype(f32)
    mid = rest.astype(bf16)
    lo = (rest - mid.astype(f32)).astype(bf16)
    return hi, mid, lo


def dot(a, b):
    return lax.dot_general(a, b, (((1,), (0,)), ((), ())), preferred_element_type=f32)


def reverse_lanes(x):
    lane = iota(x.shape, x.ndim - 1)
    size = x.shape[-1]
    step = size // 2
    while step:
        x = jnp.where(
            (lane & step) == 0,
            pltpu.roll(x, size - step, x.ndim - 1),
            pltpu.roll(x, step, x.ndim - 1),
        )
        step //= 2
    return x


def kernel(
    n_lon, n_lat, levels, rows, cols, offsets,
    tracers, velocity, land_mask, mixing, owners, atm_row,
    x2, surf_v, cover_v,
    x0, x1, wet_pad, mask_i, mix_v, own_v, row_v,
    pack0, pack1b, from_e0, from_w0, from_eb, from_wb, edge0, edge2b, rim, rim_e, rim_w, rim_new,
    rim_pad, fold0, fold1, own_up, up, down, r_s, r_se, r_sw, r_n, r_ne, r_nw,
    coef, onehot, out_early, in_early, out_late, in_late, row_hot,
    in_sem, c_send, c_recv, h_send, h_recv, a_send, a_recv, ready,
):
    devices = n_lon * n_lat
    lon = lax.axis_index("lon")
    lat = lax.axis_index("lat")
    me = lon * n_lat + lat
    top = n_lat - 1
    east = (lax.rem(lon + 1, n_lon), lat)
    west = (lax.rem(lon + n_lon - 1, n_lon), lat)
    north = (lon, lax.min(lat + 1, top))
    south = (lon, lax.max(lat - 1, 0))
    mirror = (n_lon - 1 - lon, lat)
    end = ROW0 + rows
    chunks = rows // 8

    loads = [
        pltpu.make_async_copy(land_mask, mask_i, in_sem.at[0]),
        pltpu.make_async_copy(mixing, mix_v, in_sem.at[1]),
        pltpu.make_async_copy(owners, own_v, in_sem.at[2]),
        pltpu.make_async_copy(atm_row, row_v, in_sem.at[3]),
    ]
    for f in range(4):
        src = (tracers if f < 2 else velocity).at[f % 2]
        loads.append(pltpu.make_async_copy(src, x0.at[:, f, ROW0:end, :], in_sem.at[4 + f]))
    for load in loads:
        load.start()

    barrier = pltpu.get_barrier_semaphore()
    for d in range(1, n_lon):
        pl.semaphore_signal(barrier, inc=1, device_id=(lax.rem(lon + d, n_lon), lat), device_id_type=MESH)
    for d in range(1, n_lat):
        pl.semaphore_signal(barrier, inc=1, device_id=(lon, lax.rem(lat + d, n_lat)), device_id_type=MESH)

    lat_n, lat_s = lax.rem(lat + 1, n_lat), lax.rem(lat + top, n_lat)
    for lon_to in (east[0], west[0]):
        for lat_to in (lat_n, lat_s):
            pl.semaphore_signal(barrier, inc=1, device_id=(lon_to, lat_to), device_id_type=MESH)

    lane8 = iota((8, cols), 1)
    lane = iota((rows, cols), 1)
    first = lane8 == 0
    last = lane8 == cols - 1

    def part(c):
        return slice(ROW0 + 8 * c, ROW0 + 8 * c + 8)

    def packed(tile, value, i):
        where = (lane8 == 2 * i) | (lane8 == lax.rem(2 * i + cols - 1, cols))
        return jnp.where(where, pltpu.roll(value, 2 * i, 1), tile)

    loads[0].wait()
    wet = mask_i[...].astype(f32)
    wet_pad[ROW0:end, :] = wet
    for load in loads[4:]:
        load.wait()

    def prepare(k, tiles):
        tiles = list(tiles)
        for f in range(4):
            for c in range(chunks):
                q = x0[k, f, part(c), :] * wet_pad[part(c), :]
                x0[k, f, part(c), :] = q
                tiles[c] = packed(tiles[c], q, 4 * k + f)
        return tuple(tiles)

    empty = tuple(jnp.zeros((8, cols), f32) for _ in range(chunks))
    tiles = lax.fori_loop(0, levels, prepare, empty, unroll=2)
    for c in range(chunks):
        pack0[8 * c : 8 * c + 8, :] = tiles[c]

    loads[1].wait()
    rate_t = TIMESTEP * mix_v[...]
    rate_v = jnp.full((rows, cols), TIMESTEP * VISCOSITY, f32)
    group = lane // 4
    packed_rim = jnp.zeros((rows, cols), f32)
    quantities = [x0[k, f, ROW0:end, :] for k in range(2) for f in range(4)]
    quantities += [wet] * 4 + [rate_t, rate_t, rate_v, rate_v]
    for i, value in enumerate(quantities):
        packed_rim = jnp.where(group == i, pltpu.roll(value, 4 * i + 2, 1), packed_rim)
    rim[...] = packed_rim
    for buf, edge, second in ((own_up, end - 1, end - 2), (down, ROW0, ROW0 + 1)):
        for f in range(4):
            buf[f : f + 1, :] = x0[0, f, edge : edge + 1, :]
            buf[4 + f : 5 + f, :] = x0[0, f, second : second + 1, :]
            buf[8 + f : 9 + f, :] = x0[1, f, edge : edge + 1, :]
        buf[12:13, :] = wet_pad[edge : edge + 1, :]
        buf[13:14, :] = wet_pad[second : second + 1, :]
        buf[14:15, :] = mix_v[edge - ROW0 : edge - ROW0 + 1, :]
        buf[15:16, :] = rim[edge - ROW0 : edge - ROW0 + 1, :]
    up[...] = own_up[...]

    @pl.when(lat == top)
    def _():
        raw = own_up[...]
        turned = reverse_lanes(raw)
        sub16, lane16 = iota((16, cols), 0), iota((16, cols), 1)
        swapped = jnp.where(lane16 % 4 == 1, pltpu.roll(raw, cols - 1, 1), pltpu.roll(raw, 1, 1))
        turned = jnp.where(sub16 == 15, swapped, turned)
        which = jnp.where(sub16 == 15, lane16 // 4, sub16)
        turned = jnp.where((which < jnp.where(sub16 == 15, 8, 12)) & (which % 4 >= 2), -turned, turned)
        up[...] = turned

    @pl.when(lat == 0)
    def _():
        x0[:, :, ROW0 - 1, :] = jnp.zeros((levels, 4, cols), f32)
        x1[:, :, ROW0 - 1, :] = jnp.zeros((levels, 4, cols), f32)
        for ref in (r_s, r_se, r_sw):
            ref[...] = jnp.zeros((16, cols), f32)

    pl.semaphore_wait(barrier, n_lon + n_lat + 2)

    def link(src, dst, send_sem, recv_sem, device):
        return pltpu.make_async_remote_copy(
            src_ref=src, dst_ref=dst, send_sem=send_sem, recv_sem=recv_sem,
            device_id=device, device_id_type=MESH,
        )

    def remote(src, dst, sem, device):
        return link(src, dst, h_send.at[sem], h_recv.at[sem], device)

    def first_link(src, dst, send_sem, recv_sem, device):
        return link(src, dst, c_send.at[send_sem], c_recv.at[recv_sem], device)

    fold_ne = lax.rem(2 * n_lon - 2 - lon, n_lon)
    fold_nw = lax.rem(n_lon - lon, n_lon)
    below_top, is_top, above_bottom = lat < top, lat == top, lat > 0
    ups = [
        (below_top, first_link(up, r_s, 0, 0, north)),
        (below_top, first_link(up, r_sw, 1, 2, (east[0], north[1]))),
        (below_top, first_link(up, r_se, 2, 1, (west[0], north[1]))),
        (is_top, first_link(up, r_n, 0, 3, mirror)),
        (is_top & (fold_ne != lon), first_link(up, r_ne, 1, 4, (fold_ne, lat))),
        (is_top & (fold_nw != lon), first_link(up, r_nw, 2, 5, (fold_nw, lat))),
    ]
    downs = [
        (above_bottom, first_link(down, r_n, 3, 3, south)),
        (above_bottom, first_link(down, r_nw, 4, 5, (east[0], south[1]))),
        (above_bottom, first_link(down, r_ne, 5, 4, (west[0], south[1]))),
    ]
    sides = [first_link(rim, rim_w, 6, 6, east), first_link(rim, rim_e, 7, 7, west)]
    for copy in sides:
        copy.start()
    for cond, copy in ups + downs:
        pl.when(cond)(copy.start)

    @pl.when(is_top & (fold_ne == lon))
    def _():
        r_ne[...] = up[...]

    @pl.when(is_top & (fold_nw == lon))
    def _():
        r_nw[...] = up[...]

    def row_copies(x, fold, lo, hi, sem):
        rows_of = lambda ref, r: ref.at[lo:hi, :, r, :]
        ahead = remote(rows_of(x, end - 1), rows_of(x, ROW0 - 1), sem, north)
        over = remote(rows_of(x, end - 1), fold.at[lo:hi], sem + 1, mirror)
        back = remote(rows_of(x, ROW0), rows_of(x, end), sem + 1, south)
        return ahead, over, back

    def start_rows(ahead, over, back):
        pl.when(lat < top)(ahead.start)
        pl.when(lat == top)(over.start)
        pl.when(lat > 0)(back.start)

    def wait_rows(ahead, over, back):
        pl.when(lat > 0)(ahead.wait_recv)
        pl.when(lat == top)(over.wait_recv)
        pl.when(lat < top)(back.wait_recv)

    def drain_rows(ahead, over, back):
        pl.when(lat < top)(ahead.wait_send)
        pl.when(lat == top)(over.wait_send)
        pl.when(lat > 0)(back.wait_send)

    def col_copies(pack, from_w, from_e, sem):
        return remote(pack, from_w, sem, east), remote(pack, from_e, sem + 1, west)

    halo0_rows = row_copies(x0, fold0, 2, levels, 0)
    halo0_cols = col_copies(pack0, from_w0, from_e0, 2)
    start_rows(*halo0_rows)
    for copy in halo0_cols:
        copy.start()

    for d in range(1, n_lat):
        pl.semaphore_signal(ready, inc=1, device_id=(lon, lax.rem(lat + d, n_lat)), device_id_type=MESH)

    loads[2].wait()
    loads[3].wait()
    blocks = rows
    pad_row = lambda ref: jnp.concatenate([ref[...].astype(f32)] * (cols // blocks), axis=1)
    own_lane = pad_row(own_v)
    row_lane = pad_row(row_v)
    sub = iota((blocks, cols), 0)
    own_col = jnp.sum(jnp.where(lane == sub, own_lane, 0.0), axis=1, keepdims=True)
    row_col = jnp.sum(jnp.where(lane == sub, row_lane + 1.0, 0.0), axis=1, keepdims=True)
    same = jnp.where((own_col == own_lane) & (sub < lax.rem(lane, blocks)), 1.0, 0.0)
    position = jnp.sum(same, axis=0, keepdims=True)
    lane1 = iota((1, cols), 1)
    target = own_lane.astype(jnp.int32) * 8 + (lane1 // blocks) * 2 + position.astype(jnp.int32)
    hot = jnp.where(iota((devices * 8, cols), 0) == target, 1.0, 0.0).astype(bf16)
    for j in range(PIECES):
        onehot[:, cols * j : cols * (j + 1)] = hot
    early = jnp.concatenate(
        [wet, jnp.broadcast_to(row_col, (blocks, cols)), jnp.zeros((2 * blocks, cols), f32)], axis=0
    )
    out_early[...] = dot(hot, early.astype(bf16)).reshape(devices, 8, cols)
    in_early[devices - 1 : devices] = out_early[pl.ds(me, 1)]

    def turning(row):
        angle = math.pi * (-0.43 + 0.93 * (row.astype(f32) + 0.5) / (n_lat * rows))
        return CORIOLIS_MAX * jnp.sin(angle)

    coriolis = turning(lat * rows + iota((rows, cols), 0))
    rim_row = jnp.where(iota((8, cols), 0) < 4, lat * rows - 1, lax.min((lat + 1) * rows, n_lat * rows - 1))
    coriolis8 = turning(rim_row)

    near = devices // 2

    def exchange(out, into, sem, height):
        for slot, (a, c) in enumerate(offsets):
            to_lon, to_lat = lax.rem(lon + a, n_lon), lax.rem(lat + c, n_lat)
            pltpu.make_async_remote_copy(
                src_ref=out.at[to_lon * n_lat + to_lat, 0:height, :], dst_ref=into.at[slot, 0:height, :],
                send_sem=a_send.at[sem], recv_sem=a_recv.at[2 * sem + slot // near],
                device_id=(to_lon, to_lat), device_id_type=MESH,
            ).start()
        parts = []
        for lo, hi, half in ((0, near, 0), (near, devices - 1, 1)):
            span = lambda ref: ref.at[lo:hi, 0:height, :]
            parts.append(pltpu.make_async_remote_copy(
                src_ref=span(out), dst_ref=span(into),
                send_sem=a_send.at[sem], recv_sem=a_recv.at[2 * sem + half],
                device_id=east, device_id_type=MESH,
            ))
        return parts

    pl.semaphore_wait(ready, n_lat - 1)
    early_all = exchange(out_early, in_early, 0, 4)

    for copy in sides:
        copy.wait_recv()
    arrivals = [
        (above_bottom, ups[0]), (above_bottom, ups[1]), (above_bottom, ups[2]),
        (below_top, downs[0]), (below_top, downs[1]), (below_top, downs[2]), (is_top, ups[3]),
        (is_top & (fold_ne != lon), ups[4]), (is_top & (fold_nw != lon), ups[5]),
    ]
    for cond, (_, copy) in arrivals:
        pl.when(cond)(copy.wait_recv)

    centre = 1.0 - 2.0 * TIMESTEP * VERTICAL_MIX
    vertical = TIMESTEP * VERTICAL_MIX

    def surface_step(q, e, w, n, s, below, wets, rate, turn, u, v, field, gx, gy):
        we, ww, wn, ws, wc = wets
        dx, dy = e - w, n - s
        extra = jnp.where(
            field == 2, TIMESTEP * turn * v - (0.25 * TIMESTEP * GRAVITY) * gx(dx),
            jnp.where(field == 3, -TIMESTEP * turn * u - (0.25 * TIMESTEP * GRAVITY) * gy(dy), 0.0),
        )
        spread = (we * e + ww * w) + (wn * n + ws * s)
        return wc * (
            q * (centre - rate * (we + ww + wn + ws)) + vertical * (q + below) + rate * spread
            - (0.5 * TIMESTEP) * (u * dx + v * dy) + extra
        )

    two = lambda a, b: jnp.concatenate([a, b], axis=0)
    four = lambda a, b: two(jnp.broadcast_to(a, (4, cols)), jnp.broadcast_to(b, (4, cols)))
    from_right = lambda x, corner: pltpu.roll(jnp.where(first, corner, x), cols - 1, 1)
    from_left = lambda x, corner: pltpu.roll(jnp.where(last, corner, x), 1, 1)
    both = lambda a, b, lo: two(a[lo : lo + 4, :], b[lo : lo + 4, :])
    line = lambda a, b, i: four(a[i : i + 1, :], b[i : i + 1, :])
    q8 = both(r_s, r_n, 0)
    wet8 = line(r_s, r_n, 12)
    field8 = iota((8, cols), 0) % 4
    of = lambda x, i: four(x[i : i + 1], x[4 + i : 5 + i])
    slope = lambda d: HALINE * of(d, 1) - THERMAL * of(d, 0)
    rows_new = surface_step(
        q8, from_right(q8, both(r_se, r_ne, 0)), from_left(q8, both(r_sw, r_nw, 0)),
        two(down[0:4, :], r_n[4:8, :]), two(r_s[4:8, :], own_up[0:4, :]), both(r_s, r_n, 8),
        (
            from_right(wet8, line(r_se, r_ne, 12)), from_left(wet8, line(r_sw, r_nw, 12)),
            four(down[12:13, :], r_n[13:14, :]), four(r_s[13:14, :], own_up[12:13, :]), wet8,
        ),
        jnp.where(field8 < 2, TIMESTEP * line(r_s, r_n, 14), TIMESTEP * VISCOSITY),
        coriolis8, of(q8, 2), of(q8, 3), field8, slope, slope,
    )
    for f in range(4):
        x1[0, f, ROW0 - 1 : ROW0, :] = rows_new[f : f + 1]
        x1[0, f, end : end + 1, :] = rows_new[4 + f : 5 + f]
        for k in range(2):
            x0[k, f, ROW0 - 1 : ROW0, :] = r_s[8 * k + f : 8 * k + f + 1, :]
            x0[k, f, end : end + 1, :] = r_n[8 * k + f : 8 * k + f + 1, :]
    wet_pad[ROW0 - 1 : ROW0, :] = r_s[12:13, :]
    wet_pad[end : end + 1, :] = r_n[12:13, :]

    low = lane % 4 < 2
    halves = lambda a, b: jnp.where(iota(a.shape, 1) < cols // 2, a, pltpu.roll(b, cols // 2 - 1, 1))
    own_rim, east_rim, west_rim = rim[...], rim_e[...], rim_w[...]
    strip = halves(jnp.where(low, west_rim, own_rim), jnp.where(low, own_rim, east_rim))
    rim_pad[ROW0:end, :] = strip
    wide = lambda ref: jnp.broadcast_to(ref[15:16, :], (8, cols))
    rim_pad[ROW0 - 1 : ROW0, :] = halves(wide(r_sw), wide(r_se))[0:1]
    rim_pad[end : end + 1, :] = halves(wide(r_nw), wide(r_ne))[0:1]
    strip_n = rim_pad[ROW0 + 1 : end + 1, :]
    strip_s = rim_pad[ROW0 - 1 : end - 1, :]
    right = lambda x, d: pltpu.roll(x, (d + cols) % cols, 1)
    wets = [right(x, -32) for x in (strip_n, strip_s, strip)]
    field = group % 16

    def spread_field(i):
        out = strip
        for f in range(4):
            if f != i:
                out = jnp.where(field == f, right(strip, 4 * (f - i)), out)
        return out

    rim_new[...] = surface_step(
        strip, right(strip, -1), right(strip, 1), strip_n, strip_s, right(strip, -16),
        (right(wets[2], -1), right(wets[2], 1), wets[0], wets[1], wets[2]),
        right(strip, -48), coriolis, spread_field(2), spread_field(3), field,
        lambda d: HALINE * right(d, 4) - THERMAL * right(d, 8),
        lambda d: HALINE * right(d, 8) - THERMAL * right(d, 12),
    )

    at = lambda x, src, dst: pltpu.roll(x, (dst - src + cols) % cols, 1)
    w_east = pltpu.roll(jnp.where(lane == 0, at(east_rim, 34, 0), wet), cols - 1, 1)
    w_west = pltpu.roll(jnp.where(lane == cols - 1, at(west_rim, 33, cols - 1), wet), 1, 1)
    w_north = wet_pad[ROW0 + 1 : end + 1, :]
    w_south = wet_pad[ROW0 - 1 : end - 1, :]
    total = w_east + w_west + w_north + w_south
    for base, rate in ((0, rate_t), (5, TIMESTEP * VISCOSITY)):
        coef[base] = wet * (centre - rate * total)
        for j, w in enumerate((w_east, w_west, w_north, w_south)):
            coef[base + 1 + j] = wet * (rate * w)
    coef[10] = vertical * wet
    coef[11] = TIMESTEP * coriolis * wet

    pressure_rate = 0.5 * TIMESTEP * GRAVITY
    assert abs(pressure_rate - TIMESTEP * VERTICAL_MIX) < 1e-12

    def level(x, k, side_of, carry, store):
        above = lax.max(k - 1, 0) if not isinstance(k, int) else max(k - 1, 0)
        below = lax.min(k + 1, levels - 1) if not isinstance(k, int) else min(k + 1, levels - 1)
        carry = list(carry)
        for c in range(chunks):
            mid = part(c)
            ahead = slice(ROW0 + 8 * c + 1, ROW0 + 8 * c + 9)
            behind = slice(ROW0 + 8 * c - 1, ROW0 + 8 * c + 7)
            own = slice(8 * c, 8 * c + 8)
            q, e, w, n, s = [], [], [], [], []
            for f in range(4):
                value = x[k, f, mid, :]
                side = side_of(own, k, f)
                q.append(value)
                e.append(pltpu.roll(jnp.where(first, side, value), cols - 1, 1))
                w.append(pltpu.roll(jnp.where(last, side, value), 1, 1))
                n.append(x[k, f, ahead, :])
                s.append(x[k, f, behind, :])
            gx = HALINE * (e[1] - w[1]) - THERMAL * (e[0] - w[0])
            gy = HALINE * (n[1] - s[1]) - THERMAL * (n[0] - s[0])
            sx = carry[2 * c] + gx
            sy = carry[2 * c + 1] + gy
            carry[2 * c], carry[2 * c + 1] = sx, sy
            push = (None, None, sx - 0.5 * gx, sy - 0.5 * gy)
            u = (0.5 * TIMESTEP) * q[2]
            v = (0.5 * TIMESTEP) * q[3]
            vert = coef[10, own, :]
            turn = coef[11, own, :]
            for f in range(4):
                if f % 2 == 0:
                    base = 0 if f == 0 else 5
                    a = coef[base, own, :]
                    ce = coef[base + 1, own, :] - u
                    cw = coef[base + 2, own, :] + u
                    cn = coef[base + 3, own, :] - v
                    cs = coef[base + 4, own, :] + v
                column = x[above, f, mid, :] + x[below, f, mid, :]
                if f >= 2:
                    column = column - push[f]
                value = (a * q[f] + vert * column) + (ce * e[f] + cw * w[f]) + (cn * n[f] + cs * s[f])
                if f == 2:
                    value = value + turn * q[3]
                if f == 3:
                    value = value - turn * q[2]
                store(k, f, c, value)
        return tuple(carry)

    def merge(edge, from_e, from_w):
        edge[...] = jnp.where(lax.rem(lane, 2) == 0, from_e[...], from_w[...])

    def unfold(x, fold, lo, hi):
        @pl.when(lat == top)
        def _():
            for k in range(lo, hi, 2):
                width = min(2, hi - k)
                pair = fold[k : k + width].reshape(4 * width, cols)
                pair = reverse_lanes(pair)
                field = lax.rem(iota(pair.shape, 0), 4)
                pair = jnp.where(field < 2, pair, -pair)
                for j in range(width):
                    for f in range(4):
                        x[k + j, f, end : end + 1, :] = pair[4 * j + f : 4 * j + f + 1]

    def packed_side(edge):
        return lambda own, k, f: pltpu.roll(edge[own, :], lax.rem(2 * cols - 2 * (4 * k + f), cols), 1)

    def rim_side(from_east, lane_e, from_west, lane_w):
        def side(own, k, f):
            i = 4 * (4 * k + f)
            east_value = at(from_east[own, :], lane_e + i, 0)
            return jnp.where(first, east_value, at(from_west[own, :], lane_w + i, cols - 1))

        return side

    zeros = tuple(jnp.zeros((8, cols), f32) for _ in range(2 * chunks))

    def step1(k, side_of, carry, tiles):
        tiles = list(tiles)

        def store(k, f, c, value):
            x1[k, f, part(c), :] = value
            if tiles:
                tiles[c] = packed(tiles[c], value, 4 * k + f)

        carry = level(x0, k, side_of, carry, store)
        return carry, tuple(tiles)

    near_side = rim_side(rim_e, 2, rim_w, 1)
    carry1, _ = step1(0, near_side, zeros, ())
    carry1, tiles = step1(1, near_side, carry1, empty)

    def store2(k, f, c, value):
        x2[k, f, 8 * c : 8 * c + 8, :] = value

    carry2 = level(x1, 0, rim_side(rim_new, 65, rim_new, 1), zeros, store2)
    surf = x2[0].reshape(4 * rows, cols)
    late = dot(onehot[...], jnp.concatenate(split(surf), axis=0))
    out_late[...] = late.reshape(devices, 8, cols)
    in_late[devices - 1 : devices] = out_late[pl.ds(me, 1)]
    late_all = exchange(out_late, in_late, 1, 8)

    for copy in halo0_cols:
        copy.wait_recv()
    wait_rows(*halo0_rows)
    merge(edge0, from_e0, from_w0)
    unfold(x0, fold0, 2, levels)
    _, tiles = lax.fori_loop(
        2, levels, lambda k, s: step1(k, packed_side(edge0), *s), (carry1, tiles), unroll=UNROLL1
    )
    for c in range(chunks):
        pack1b[8 * c : 8 * c + 8, :] = tiles[c]
    halo2_rows = row_copies(x1, fold1, 1, levels, 4)
    halo2_cols = col_copies(pack1b, from_wb, from_eb, 6)
    start_rows(*halo2_rows)
    for copy in halo2_cols:
        copy.start()

    for copy in halo2_cols:
        copy.wait_recv()
    wait_rows(*halo2_rows)
    merge(edge2b, from_eb, from_wb)
    unfold(x1, fold1, 1, levels)
    lax.fori_loop(1, levels, lambda k, s: level(x1, k, packed_side(edge2b), s, store2), carry2, unroll=UNROLL2)
    for copy in early_all:
        copy.wait_recv()
    tile = (cols // 8, 8, cols)
    sub3 = iota(tile, 1)
    lane3 = iota(tile, 2)
    keep = (sub3 // 2) == (lane3 // ATM_ROWS)
    wanted = (lax.rem(lane3, ATM_ROWS) + 1).astype(f32)
    for j in range(devices * 8 // cols):
        got = in_early[tile[0] * j : tile[0] * (j + 1)]
        ids = jnp.where((sub3 // 2) == 1, got, 0.0)
        ids = (ids + pltpu.roll(ids, 2, 1)) + (pltpu.roll(ids, 4, 1) + pltpu.roll(ids, 6, 1))
        hit = jnp.where(keep & (ids == wanted), 1.0, 0.0)
        row_hot[:, cols * j : cols * (j + 1)] = hit.reshape(cols, cols).T.astype(bf16)
    wets = jnp.where(iota((devices, 8, cols), 1) < 2, in_early[...], 0.0)
    cover = dot(row_hot[0:ATM_ROWS, :], wets.reshape(devices * 8, cols).astype(bf16))
    cover_v[...] = cover
    share = 1.0 / jnp.maximum(cover, 1.0)

    sums = jnp.zeros((4 * ATM_ROWS, cols), f32)
    for half, copy in enumerate(late_all):
        copy.wait_recv()
        got = in_late[near * half : near * (half + 1)].reshape(near * 8, cols)
        placed = row_hot[:, near * 8 * half : near * 8 * (half + 1)]
        for piece in split(got):
            sums = sums + dot(placed, piece)
    surf_v[...] = sums.reshape(4, ATM_ROWS, cols) * share

    for cond, copy in ups + downs:
        pl.when(cond)(copy.wait_send)
    drain_rows(*halo0_rows)
    drain_rows(*halo2_rows)
    for copy in [*sides, *halo0_cols, *halo2_cols]:
        copy.wait_send()
    whole = lambda ref, height: ref.at[0 : devices - 1, 0:height, :]
    for sem, (out, into, height) in enumerate(((out_early, in_early, 4), (out_late, in_late, 8))):
        pltpu.make_async_remote_copy(
            src_ref=whole(out, height), dst_ref=whole(into, height),
            send_sem=a_send.at[sem], recv_sem=a_recv.at[2 * sem], device_id=east, device_id_type=MESH,
        ).wait_send()


def write_out(x2, surf_v, cover_v, tracers_out, velocity_out, surface_out, cover_out, sem):
    stores = []
    for f in range(4):
        dst = (tracers_out if f < 2 else velocity_out).at[f % 2]
        stores.append(pltpu.make_async_copy(x2.at[:, f], dst, sem.at[f]))
    stores.append(pltpu.make_async_copy(cover_v, cover_out, sem.at[4]))
    stores.append(pltpu.make_async_copy(surf_v, surface_out, sem.at[5]))
    for store in stores:
        store.start()
    for store in stores:
        store.wait()


def local(tracers, velocity, land_mask, mixing, owners, atm_row):
    n_lon, n_lat = lax.axis_size("lon"), lax.axis_size("lat")
    levels = tracers.shape[1]
    rows, cols = land_mask.shape
    devices = n_lon * n_lat
    blocks = rows * cols // 128
    assert cols == 128 and blocks == rows and ATM_ROWS == 32
    any_spec = pl.BlockSpec(memory_space=pl.ANY)
    vmem = lambda *shape: pltpu.VMEM(shape, f32)
    tile = vmem(rows, cols)
    padded = rows + 16
    scratch = (
        [vmem(levels, 4, padded, cols)] * 2
        + [vmem(padded, cols)]
        + [pltpu.VMEM((rows, cols), jnp.int32), tile]
        + [pltpu.VMEM((1, blocks), jnp.int32)] * 2
        + [tile] * 12
        + [vmem(padded, cols)]
        + [vmem(levels, 4, cols)] * 2
        + [vmem(16, cols)] * 9
        + [vmem(12, rows, cols), pltpu.VMEM((devices * 8, PIECES * cols), bf16)]
        + [vmem(devices, 8, cols)] * 4
        + [pltpu.VMEM((4 * ATM_ROWS, devices * 8), bf16)]
        + [pltpu.SemaphoreType.DMA((8,))]
        + [pltpu.SemaphoreType.DMA((8,))] * 4
        + [pltpu.SemaphoreType.DMA((2,)), pltpu.SemaphoreType.DMA((4,))]
        + [pltpu.SemaphoreType.REGULAR]
    )
    ring = lambda d, size: min(d % size, size - d % size)
    half_lat = n_lat // 2
    hops = lambda a, c: ring(a, n_lon // 2) + ring(c // 2, half_lat // 2) + 2 * (a // (n_lon // 2)) + c // half_lat
    offsets = [(a, c) for a in range(n_lon) for c in range(n_lat) if a or c]
    offsets.sort(key=lambda o: hops(*o))
    held = pl.pallas_call(
        functools.partial(kernel, n_lon, n_lat, levels, rows, cols, offsets),
        out_shape=(vmem(levels, 4, rows, cols), vmem(4, ATM_ROWS, cols), vmem(ATM_ROWS, cols)),
        in_specs=[any_spec] * 6,
        scratch_shapes=scratch,
        compiler_params=pltpu.CompilerParams(collective_id=0, has_side_effects=True),
        name="ocean",
    )(tracers, velocity, land_mask, mixing, owners.reshape(1, blocks), atm_row.reshape(1, blocks))
    return pl.pallas_call(
        write_out,
        out_shape=(
            jax.ShapeDtypeStruct(tracers.shape, f32),
            jax.ShapeDtypeStruct(velocity.shape, f32),
            jax.ShapeDtypeStruct((4, ATM_ROWS, cols), f32),
            jax.ShapeDtypeStruct((ATM_ROWS, cols), f32),
        ),
        in_specs=[pl.BlockSpec(memory_space=pltpu.VMEM)] * 3,
        out_specs=(any_spec,) * 4,
        scratch_shapes=[pltpu.SemaphoreType.DMA((6,))],
        name="write_out",
    )(*(pltpu.with_memory_space_constraint(x, pltpu.VMEM) for x in held))


def solution(mesh):
    in_specs = (
        P(None, None, "lat", "lon"),
        P(None, None, "lat", "lon"),
        P("lat", "lon"),
        P("lat", "lon"),
        P(("lon", "lat"), None),
        P(("lon", "lat")),
    )
    out_specs = (
        P(None, None, "lat", "lon"),
        P(None, None, "lat", "lon"),
        P(None, ("lon", "lat"), None),
        P(("lon", "lat"), None),
    )
    return jax.shard_map(local, mesh=mesh, in_specs=in_specs, out_specs=out_specs, check_vma=False)
```

```python
import functools
import math

import jax
import jax.numpy as jnp
from jax import lax
from jax.experimental import pallas as pl
from jax.experimental.pallas import tpu as pltpu
from jax.sharding import PartitionSpec as P

THERMAL = 0.2
HALINE = 0.15
GRAVITY = 0.2
TIMESTEP = 0.8
VERTICAL_MIX = 0.1
VISCOSITY = 0.2
CORIOLIS_MAX = 0.3
ATM_ROWS = 32
UNROLL1, UNROLL2 = 2, 3
PIECES = 3

MESH = pl.DeviceIdType.MESH
ROW0 = 8
f32 = jnp.float32
bf16 = jnp.bfloat16


def iota(shape, dim):
    return lax.broadcasted_iota(jnp.int32, shape, dim)


def split(x):
    hi = x.astype(bf16)
    rest = x - hi.astype(f32)
    mid = rest.astype(bf16)
    lo = (rest - mid.astype(f32)).astype(bf16)
    return hi, mid, lo


def dot(a, b):
    return lax.dot_general(a, b, (((1,), (0,)), ((), ())), preferred_element_type=f32)


def reverse_lanes(x):
    lane = iota(x.shape, x.ndim - 1)
    size = x.shape[-1]
    step = size // 2
    while step:
        x = jnp.where(
            (lane & step) == 0,
            pltpu.roll(x, size - step, x.ndim - 1),
            pltpu.roll(x, step, x.ndim - 1),
        )
        step //= 2
    return x


def kernel(
    n_lon, n_lat, levels, rows, cols, offsets,
    tracers, velocity, land_mask, mixing, owners, atm_row,
    x2, surf_v, cover_v,
    x0, x1, wet_pad, mask_i, mix_v, own_v, row_v,
    pack0, pack1b, from_e0, from_w0, from_eb, from_wb, edge0, edge2b, rim, rim_e, rim_w, rim_new,
    rim_pad, fold0, rows_s, rows_n, own_up, up, down, r_s, r_se, r_sw, r_n, r_ne, r_nw,
    coef, onehot, out_early, in_early, out_late, in_late, row_hot,
    in_sem, c_send, c_recv, h_send, h_recv, a_send, a_recv, ready,
):
    devices = n_lon * n_lat
    lon = lax.axis_index("lon")
    lat = lax.axis_index("lat")
    me = lon * n_lat + lat
    top = n_lat - 1
    east = (lax.rem(lon + 1, n_lon), lat)
    west = (lax.rem(lon + n_lon - 1, n_lon), lat)
    north = (lon, lax.min(lat + 1, top))
    south = (lon, lax.max(lat - 1, 0))
    mirror = (n_lon - 1 - lon, lat)
    end = ROW0 + rows
    chunks = rows // 8

    loads = [
        pltpu.make_async_copy(land_mask, mask_i, in_sem.at[0]),
        pltpu.make_async_copy(mixing, mix_v, in_sem.at[1]),
        pltpu.make_async_copy(owners, own_v, in_sem.at[2]),
        pltpu.make_async_copy(atm_row, row_v, in_sem.at[3]),
    ]
    for f in range(4):
        src = (tracers if f < 2 else velocity).at[f % 2]
        loads.append(pltpu.make_async_copy(src, x0.at[:, f, ROW0:end, :], in_sem.at[4 + f]))
    for load in loads:
        load.start()

    barrier = pltpu.get_barrier_semaphore()
    for d in range(1, n_lon):
        pl.semaphore_signal(barrier, inc=1, device_id=(lax.rem(lon + d, n_lon), lat), device_id_type=MESH)
    for d in range(1, n_lat):
        pl.semaphore_signal(barrier, inc=1, device_id=(lon, lax.rem(lat + d, n_lat)), device_id_type=MESH)

    lat_n, lat_s = lax.rem(lat + 1, n_lat), lax.rem(lat + top, n_lat)
    for lon_to in (east[0], west[0]):
        for lat_to in (lat_n, lat_s):
            pl.semaphore_signal(barrier, inc=1, device_id=(lon_to, lat_to), device_id_type=MESH)

    lane8 = iota((8, cols), 1)
    lane = iota((rows, cols), 1)
    first = lane8 == 0
    last = lane8 == cols - 1

    def part(c):
        return slice(ROW0 + 8 * c, ROW0 + 8 * c + 8)

    def packed(tile, value, i):
        where = (lane8 == 2 * i) | (lane8 == lax.rem(2 * i + cols - 1, cols))
        return jnp.where(where, pltpu.roll(value, 2 * i, 1), tile)

    for row in (ROW0 - 1, end):
        x1[:, :, row, :] = jnp.zeros((levels, 4, cols), f32)

    loads[0].wait()
    wet = mask_i[...].astype(f32)
    wet_pad[ROW0:end, :] = wet
    for load in loads[4:]:
        load.wait()

    def prepare(k, tiles):
        tiles = list(tiles)
        for f in range(4):
            for c in range(chunks):
                q = x0[k, f, part(c), :] * wet_pad[part(c), :]
                x0[k, f, part(c), :] = q
                tiles[c] = packed(tiles[c], q, 4 * k + f)
        return tuple(tiles)

    empty = tuple(jnp.zeros((8, cols), f32) for _ in range(chunks))
    tiles = lax.fori_loop(0, levels, prepare, empty, unroll=2)
    for c in range(chunks):
        pack0[8 * c : 8 * c + 8, :] = tiles[c]

    loads[1].wait()
    rate_t = TIMESTEP * mix_v[...]
    rate_v = jnp.full((rows, cols), TIMESTEP * VISCOSITY, f32)
    group = lane // 4
    packed_rim = jnp.zeros((rows, cols), f32)
    quantities = [x0[k, f, ROW0:end, :] for k in range(2) for f in range(4)]
    quantities += [wet] * 4 + [rate_t, rate_t, rate_v, rate_v]
    for i, value in enumerate(quantities):
        packed_rim = jnp.where(group == i, pltpu.roll(value, 4 * i + 2, 1), packed_rim)
    rim[...] = packed_rim
    for buf, edge, second in ((own_up, end - 1, end - 2), (down, ROW0, ROW0 + 1)):
        for f in range(4):
            buf[f : f + 1, :] = x0[0, f, edge : edge + 1, :]
            buf[4 + f : 5 + f, :] = x0[0, f, second : second + 1, :]
            buf[8 + f : 9 + f, :] = x0[1, f, edge : edge + 1, :]
        buf[12:13, :] = wet_pad[edge : edge + 1, :]
        buf[13:14, :] = wet_pad[second : second + 1, :]
        buf[14:15, :] = mix_v[edge - ROW0 : edge - ROW0 + 1, :]
        buf[15:16, :] = rim[edge - ROW0 : edge - ROW0 + 1, :]
    up[...] = own_up[...]

    @pl.when(lat == top)
    def _():
        raw = own_up[...]
        turned = reverse_lanes(raw)
        sub16, lane16 = iota((16, cols), 0), iota((16, cols), 1)
        swapped = jnp.where(lane16 % 4 == 1, pltpu.roll(raw, cols - 1, 1), pltpu.roll(raw, 1, 1))
        turned = jnp.where(sub16 == 15, swapped, turned)
        which = jnp.where(sub16 == 15, lane16 // 4, sub16)
        turned = jnp.where((which < jnp.where(sub16 == 15, 8, 12)) & (which % 4 >= 2), -turned, turned)
        up[...] = turned

    @pl.when(lat == 0)
    def _():
        x0[:, :, ROW0 - 1, :] = jnp.zeros((levels, 4, cols), f32)
        rows_s[...] = jnp.zeros((levels, 4, cols), f32)
        for ref in (r_s, r_se, r_sw):
            ref[...] = jnp.zeros((16, cols), f32)

    pl.semaphore_wait(barrier, n_lon + n_lat + 2)

    def link(src, dst, send_sem, recv_sem, device):
        return pltpu.make_async_remote_copy(
            src_ref=src, dst_ref=dst, send_sem=send_sem, recv_sem=recv_sem,
            device_id=device, device_id_type=MESH,
        )

    def remote(src, dst, sem, device):
        return link(src, dst, h_send.at[sem], h_recv.at[sem], device)

    def first_link(src, dst, send_sem, recv_sem, device):
        return link(src, dst, c_send.at[send_sem], c_recv.at[recv_sem], device)

    fold_ne = lax.rem(2 * n_lon - 2 - lon, n_lon)
    fold_nw = lax.rem(n_lon - lon, n_lon)
    below_top, is_top, above_bottom = lat < top, lat == top, lat > 0
    ups = [
        (below_top, first_link(up, r_s, 0, 0, north)),
        (below_top, first_link(up, r_sw, 1, 2, (east[0], north[1]))),
        (below_top, first_link(up, r_se, 2, 1, (west[0], north[1]))),
        (is_top, first_link(up, r_n, 0, 3, mirror)),
        (is_top & (fold_ne != lon), first_link(up, r_ne, 1, 4, (fold_ne, lat))),
        (is_top & (fold_nw != lon), first_link(up, r_nw, 2, 5, (fold_nw, lat))),
    ]
    downs = [
        (above_bottom, first_link(down, r_n, 3, 3, south)),
        (above_bottom, first_link(down, r_nw, 4, 5, (east[0], south[1]))),
        (above_bottom, first_link(down, r_ne, 5, 4, (west[0], south[1]))),
    ]
    sides = [first_link(rim, rim_w, 6, 6, east), first_link(rim, rim_e, 7, 7, west)]
    for copy in sides:
        copy.start()
    for cond, copy in ups + downs:
        pl.when(cond)(copy.start)

    @pl.when(is_top & (fold_ne == lon))
    def _():
        r_ne[...] = up[...]

    @pl.when(is_top & (fold_nw == lon))
    def _():
        r_nw[...] = up[...]

    def row_copies(x, lo, sem, into_s, into_n, into_fold):
        last_row, first_row = x.at[lo:levels, :, end - 1, :], x.at[lo:levels, :, ROW0, :]
        ahead = remote(last_row, into_s, sem, north)
        over = remote(last_row, into_fold, sem + 1, mirror)
        back = remote(first_row, into_n, sem + 1, south)
        return ahead, over, back

    def start_rows(ahead, over, back):
        pl.when(lat < top)(ahead.start)
        pl.when(lat == top)(over.start)
        pl.when(lat > 0)(back.start)

    def wait_rows(ahead, over, back):
        pl.when(lat > 0)(ahead.wait_recv)
        pl.when(lat == top)(over.wait_recv)
        pl.when(lat < top)(back.wait_recv)

    def drain_rows(ahead, over, back):
        pl.when(lat < top)(ahead.wait_send)
        pl.when(lat == top)(over.wait_send)
        pl.when(lat > 0)(back.wait_send)

    def col_copies(pack, from_w, from_e, sem):
        return remote(pack, from_w, sem, east), remote(pack, from_e, sem + 1, west)

    halo0_rows = row_copies(
        x0, 2, 0, x0.at[2:levels, :, ROW0 - 1, :], x0.at[2:levels, :, end, :], fold0.at[2:levels]
    )
    halo0_cols = col_copies(pack0, from_w0, from_e0, 2)
    start_rows(*halo0_rows)
    for copy in halo0_cols:
        copy.start()

    for d in range(1, n_lat):
        pl.semaphore_signal(ready, inc=1, device_id=(lon, lax.rem(lat + d, n_lat)), device_id_type=MESH)

    loads[2].wait()
    loads[3].wait()
    blocks = rows
    pad_row = lambda ref: jnp.concatenate([ref[...].astype(f32)] * (cols // blocks), axis=1)
    own_lane = pad_row(own_v)
    row_lane = pad_row(row_v)
    sub = iota((blocks, cols), 0)
    own_col = jnp.sum(jnp.where(lane == sub, own_lane, 0.0), axis=1, keepdims=True)
    row_col = jnp.sum(jnp.where(lane == sub, row_lane + 1.0, 0.0), axis=1, keepdims=True)
    same = jnp.where((own_col == own_lane) & (sub < lax.rem(lane, blocks)), 1.0, 0.0)
    position = jnp.sum(same, axis=0, keepdims=True)
    lane1 = iota((1, cols), 1)
    target = own_lane.astype(jnp.int32) * 8 + (lane1 // blocks) * 2 + position.astype(jnp.int32)
    hot = jnp.where(iota((devices * 8, cols), 0) == target, 1.0, 0.0).astype(bf16)
    for j in range(PIECES):
        onehot[:, cols * j : cols * (j + 1)] = hot
    early = jnp.concatenate(
        [wet, jnp.broadcast_to(row_col, (blocks, cols)), jnp.zeros((2 * blocks, cols), f32)], axis=0
    )
    out_early[...] = dot(hot, early.astype(bf16)).reshape(devices, 8, cols)
    in_early[devices - 1 : devices] = out_early[pl.ds(me, 1)]

    def turning(row):
        angle = math.pi * (-0.43 + 0.93 * (row.astype(f32) + 0.5) / (n_lat * rows))
        return CORIOLIS_MAX * jnp.sin(angle)

    coriolis = turning(lat * rows + iota((rows, cols), 0))
    rim_row = jnp.where(iota((8, cols), 0) < 4, lat * rows - 1, lax.min((lat + 1) * rows, n_lat * rows - 1))
    coriolis8 = turning(rim_row)

    near = devices // 2

    def exchange(out, into, sem, height):
        for slot, (a, c) in enumerate(offsets):
            to_lon, to_lat = lax.rem(lon + a, n_lon), lax.rem(lat + c, n_lat)
            pltpu.make_async_remote_copy(
                src_ref=out.at[to_lon * n_lat + to_lat, 0:height, :], dst_ref=into.at[slot, 0:height, :],
                send_sem=a_send.at[sem], recv_sem=a_recv.at[2 * sem + slot // near],
                device_id=(to_lon, to_lat), device_id_type=MESH,
            ).start()
        parts = []
        for lo, hi, half in ((0, near, 0), (near, devices - 1, 1)):
            span = lambda ref: ref.at[lo:hi, 0:height, :]
            parts.append(pltpu.make_async_remote_copy(
                src_ref=span(out), dst_ref=span(into),
                send_sem=a_send.at[sem], recv_sem=a_recv.at[2 * sem + half],
                device_id=east, device_id_type=MESH,
            ))
        return parts

    pl.semaphore_wait(ready, n_lat - 1)
    early_all = exchange(out_early, in_early, 0, 4)

    for copy in sides:
        copy.wait_recv()
    arrivals = [
        (above_bottom, ups[0]), (above_bottom, ups[1]), (above_bottom, ups[2]),
        (below_top, downs[0]), (below_top, downs[1]), (below_top, downs[2]), (is_top, ups[3]),
        (is_top & (fold_ne != lon), ups[4]), (is_top & (fold_nw != lon), ups[5]),
    ]
    for cond, (_, copy) in arrivals:
        pl.when(cond)(copy.wait_recv)

    centre = 1.0 - 2.0 * TIMESTEP * VERTICAL_MIX
    vertical = TIMESTEP * VERTICAL_MIX

    def surface_step(q, e, w, n, s, below, wets, rate, turn, u, v, field, gx, gy):
        we, ww, wn, ws, wc = wets
        dx, dy = e - w, n - s
        extra = jnp.where(
            field == 2, TIMESTEP * turn * v - (0.25 * TIMESTEP * GRAVITY) * gx(dx),
            jnp.where(field == 3, -TIMESTEP * turn * u - (0.25 * TIMESTEP * GRAVITY) * gy(dy), 0.0),
        )
        spread = (we * e + ww * w) + (wn * n + ws * s)
        return wc * (
            q * (centre - rate * (we + ww + wn + ws)) + vertical * (q + below) + rate * spread
            - (0.5 * TIMESTEP) * (u * dx + v * dy) + extra
        )

    two = lambda a, b: jnp.concatenate([a, b], axis=0)
    four = lambda a, b: two(jnp.broadcast_to(a, (4, cols)), jnp.broadcast_to(b, (4, cols)))
    from_right = lambda x, corner: pltpu.roll(jnp.where(first, corner, x), cols - 1, 1)
    from_left = lambda x, corner: pltpu.roll(jnp.where(last, corner, x), 1, 1)
    both = lambda a, b, lo: two(a[lo : lo + 4, :], b[lo : lo + 4, :])
    line = lambda a, b, i: four(a[i : i + 1, :], b[i : i + 1, :])
    q8 = both(r_s, r_n, 0)
    wet8 = line(r_s, r_n, 12)
    field8 = iota((8, cols), 0) % 4
    of = lambda x, i: four(x[i : i + 1], x[4 + i : 5 + i])
    slope = lambda d: HALINE * of(d, 1) - THERMAL * of(d, 0)
    rows_new = surface_step(
        q8, from_right(q8, both(r_se, r_ne, 0)), from_left(q8, both(r_sw, r_nw, 0)),
        two(down[0:4, :], r_n[4:8, :]), two(r_s[4:8, :], own_up[0:4, :]), both(r_s, r_n, 8),
        (
            from_right(wet8, line(r_se, r_ne, 12)), from_left(wet8, line(r_sw, r_nw, 12)),
            four(down[12:13, :], r_n[13:14, :]), four(r_s[13:14, :], own_up[12:13, :]), wet8,
        ),
        jnp.where(field8 < 2, TIMESTEP * line(r_s, r_n, 14), TIMESTEP * VISCOSITY),
        coriolis8, of(q8, 2), of(q8, 3), field8, slope, slope,
    )
    for f in range(4):
        x1[0, f, ROW0 - 1 : ROW0, :] = rows_new[f : f + 1]
        x1[0, f, end : end + 1, :] = rows_new[4 + f : 5 + f]
        for k in range(2):
            x0[k, f, ROW0 - 1 : ROW0, :] = r_s[8 * k + f : 8 * k + f + 1, :]
            x0[k, f, end : end + 1, :] = r_n[8 * k + f : 8 * k + f + 1, :]
    wet_pad[ROW0 - 1 : ROW0, :] = r_s[12:13, :]
    wet_pad[end : end + 1, :] = r_n[12:13, :]

    low = lane % 4 < 2
    halves = lambda a, b: jnp.where(iota(a.shape, 1) < cols // 2, a, pltpu.roll(b, cols // 2 - 1, 1))
    own_rim, east_rim, west_rim = rim[...], rim_e[...], rim_w[...]
    strip = halves(jnp.where(low, west_rim, own_rim), jnp.where(low, own_rim, east_rim))
    rim_pad[ROW0:end, :] = strip
    wide = lambda ref: jnp.broadcast_to(ref[15:16, :], (8, cols))
    rim_pad[ROW0 - 1 : ROW0, :] = halves(wide(r_sw), wide(r_se))[0:1]
    rim_pad[end : end + 1, :] = halves(wide(r_nw), wide(r_ne))[0:1]
    strip_n = rim_pad[ROW0 + 1 : end + 1, :]
    strip_s = rim_pad[ROW0 - 1 : end - 1, :]
    right = lambda x, d: pltpu.roll(x, (d + cols) % cols, 1)
    wets = [right(x, -32) for x in (strip_n, strip_s, strip)]
    field = group % 16

    def spread_field(i):
        out = strip
        for f in range(4):
            if f != i:
                out = jnp.where(field == f, right(strip, 4 * (f - i)), out)
        return out

    rim_new[...] = surface_step(
        strip, right(strip, -1), right(strip, 1), strip_n, strip_s, right(strip, -16),
        (right(wets[2], -1), right(wets[2], 1), wets[0], wets[1], wets[2]),
        right(strip, -48), coriolis, spread_field(2), spread_field(3), field,
        lambda d: HALINE * right(d, 4) - THERMAL * right(d, 8),
        lambda d: HALINE * right(d, 8) - THERMAL * right(d, 12),
    )

    at = lambda x, src, dst: pltpu.roll(x, (dst - src + cols) % cols, 1)
    w_east = pltpu.roll(jnp.where(lane == 0, at(east_rim, 34, 0), wet), cols - 1, 1)
    w_west = pltpu.roll(jnp.where(lane == cols - 1, at(west_rim, 33, cols - 1), wet), 1, 1)
    w_north = wet_pad[ROW0 + 1 : end + 1, :]
    w_south = wet_pad[ROW0 - 1 : end - 1, :]
    total = w_east + w_west + w_north + w_south
    for base, rate in ((0, rate_t), (5, TIMESTEP * VISCOSITY)):
        coef[base] = wet * (centre - rate * total)
        for j, w in enumerate((w_east, w_west, w_north, w_south)):
            coef[base + 1 + j] = wet * (rate * w)
    coef[10] = vertical * wet
    coef[11] = TIMESTEP * coriolis * wet

    pressure_rate = 0.5 * TIMESTEP * GRAVITY
    assert abs(pressure_rate - TIMESTEP * VERTICAL_MIX) < 1e-12

    def level(x, k, side_of, carry, store):
        above = lax.max(k - 1, 0) if not isinstance(k, int) else max(k - 1, 0)
        below = lax.min(k + 1, levels - 1) if not isinstance(k, int) else min(k + 1, levels - 1)
        carry = list(carry)
        for c in range(chunks):
            mid = part(c)
            ahead = slice(ROW0 + 8 * c + 1, ROW0 + 8 * c + 9)
            behind = slice(ROW0 + 8 * c - 1, ROW0 + 8 * c + 7)
            own = slice(8 * c, 8 * c + 8)
            q, e, w, n, s = [], [], [], [], []
            for f in range(4):
                value = x[k, f, mid, :]
                side = side_of(own, k, f)
                q.append(value)
                e.append(pltpu.roll(jnp.where(first, side, value), cols - 1, 1))
                w.append(pltpu.roll(jnp.where(last, side, value), 1, 1))
                n.append(x[k, f, ahead, :])
                s.append(x[k, f, behind, :])
            gx = HALINE * (e[1] - w[1]) - THERMAL * (e[0] - w[0])
            gy = HALINE * (n[1] - s[1]) - THERMAL * (n[0] - s[0])
            sx = carry[2 * c] + gx
            sy = carry[2 * c + 1] + gy
            carry[2 * c], carry[2 * c + 1] = sx, sy
            push = (None, None, sx - 0.5 * gx, sy - 0.5 * gy)
            u = (0.5 * TIMESTEP) * q[2]
            v = (0.5 * TIMESTEP) * q[3]
            vert = coef[10, own, :]
            turn = coef[11, own, :]
            for f in range(4):
                if f % 2 == 0:
                    base = 0 if f == 0 else 5
                    a = coef[base, own, :]
                    ce = coef[base + 1, own, :] - u
                    cw = coef[base + 2, own, :] + u
                    cn = coef[base + 3, own, :] - v
                    cs = coef[base + 4, own, :] + v
                column = x[above, f, mid, :] + x[below, f, mid, :]
                if f >= 2:
                    column = column - push[f]
                value = (a * q[f] + vert * column) + (ce * e[f] + cw * w[f]) + (cn * n[f] + cs * s[f])
                if f == 2:
                    value = value + turn * q[3]
                if f == 3:
                    value = value - turn * q[2]
                store(k, f, c, value)
        return tuple(carry)

    def merge(edge, from_e, from_w):
        edge[...] = jnp.where(lax.rem(lane, 2) == 0, from_e[...], from_w[...])

    def unfold(fold, lo, hi, put):
        @pl.when(lat == top)
        def _():
            for k in range(lo, hi, 2):
                width = min(2, hi - k)
                pair = fold[k : k + width].reshape(4 * width, cols)
                pair = reverse_lanes(pair)
                field = lax.rem(iota(pair.shape, 0), 4)
                pair = jnp.where(field < 2, pair, -pair)
                put(k, width, pair)

    def packed_side(edge):
        return lambda own, k, f: pltpu.roll(edge[own, :], lax.rem(2 * cols - 2 * (4 * k + f), cols), 1)

    def rim_side(from_east, lane_e, from_west, lane_w):
        def side(own, k, f):
            i = 4 * (4 * k + f)
            east_value = at(from_east[own, :], lane_e + i, 0)
            return jnp.where(first, east_value, at(from_west[own, :], lane_w + i, cols - 1))

        return side

    zeros = tuple(jnp.zeros((8, cols), f32) for _ in range(2 * chunks))

    def step1(k, side_of, carry, tiles):
        tiles = list(tiles)

        def store(k, f, c, value):
            x1[k, f, part(c), :] = value
            if tiles:
                tiles[c] = packed(tiles[c], value, 4 * k + f)

        carry = level(x0, k, side_of, carry, store)
        return carry, tuple(tiles)

    near_side = rim_side(rim_e, 2, rim_w, 1)
    carry1, _ = step1(0, near_side, zeros, ())
    carry1, tiles = step1(1, near_side, carry1, empty)

    def store2(k, f, c, value):
        x2[k, f, 8 * c : 8 * c + 8, :] = value

    carry2 = level(x1, 0, rim_side(rim_new, 65, rim_new, 1), zeros, store2)
    surf = x2[0].reshape(4 * rows, cols)
    late = dot(onehot[...], jnp.concatenate(split(surf), axis=0))
    out_late[...] = late.reshape(devices, 8, cols)
    in_late[devices - 1 : devices] = out_late[pl.ds(me, 1)]
    late_all = exchange(out_late, in_late, 1, 8)

    for copy in halo0_cols:
        copy.wait_recv()
    wait_rows(*halo0_rows)
    merge(edge0, from_e0, from_w0)

    def put_rows(k, width, pair):
        for j in range(width):
            for f in range(4):
                x0[k + j, f, end : end + 1, :] = pair[4 * j + f : 4 * j + f + 1]

    unfold(fold0, 2, levels, put_rows)
    _, tiles = lax.fori_loop(
        2, levels, lambda k, s: step1(k, packed_side(edge0), *s), (carry1, tiles), unroll=UNROLL1
    )
    for c in range(chunks):
        pack1b[8 * c : 8 * c + 8, :] = tiles[c]
    halo2_rows = row_copies(
        x1, 1, 4, rows_s.at[1:levels], rows_n.at[1:levels], rows_n.at[1:levels]
    )
    halo2_cols = col_copies(pack1b, from_wb, from_eb, 6)
    start_rows(*halo2_rows)
    for copy in halo2_cols:
        copy.start()

    nothing = jnp.zeros((8, cols), f32)
    lax.fori_loop(
        1, levels, lambda k, s: level(x1, k, lambda own, k, f: nothing, s, store2), carry2, unroll=UNROLL2
    )

    for copy in halo2_cols:
        copy.wait_recv()
    wait_rows(*halo2_rows)
    edge2b[...] = jnp.where(
        lax.rem(lane, 2) == 0, pltpu.roll(from_wb[...], 1, 1), pltpu.roll(from_eb[...], cols - 1, 1)
    )

    def put_back(k, width, pair):
        rows_n[k : k + width] = pair.reshape(width, 4, cols)

    unfold(rows_n, 1, levels, put_back)

    def share(k, carry):
        carry = list(carry)
        for c in range(chunks):
            own, mid = slice(8 * c, 8 * c + 8), part(c)
            u = (0.5 * TIMESTEP) * x1[k, 2, mid, :]
            v = (0.5 * TIMESTEP) * x1[k, 3, mid, :]
            vert = coef[10, own, :]
            side = edge2b[own, :]
            halo = [pltpu.roll(side, lax.rem(2 * cols - 2 * (4 * k + f), cols), 1) for f in range(4)]
            gx = HALINE * halo[1] - THERMAL * halo[0]
            gx = jnp.where(last, gx, jnp.where(first, -gx, 0.0))
            carry[c] = carry[c] + gx
            add = []
            for f in range(4):
                base = 0 if f < 2 else 5
                rate = jnp.where(
                    last, coef[base + 1, own, :] - u, jnp.where(first, coef[base + 2, own, :] + u, 0.0)
                )
                add.append(rate * halo[f])
            add[2] = add[2] - vert * (carry[c] - 0.5 * gx)
            for outside, rows_of, edge, index, sign in (
                (c == 0, rows_s, 0, 4, 1.0), (c == chunks - 1, rows_n, 7, 3, -1.0)
            ):
                if outside:
                    here = iota((8, cols), 0) == edge
                    line_of = [
                        jnp.where(here, jnp.broadcast_to(rows_of[k, f : f + 1, :], (8, cols)), 0.0)
                        for f in range(4)
                    ]
                    gy = -sign * (HALINE * line_of[1] - THERMAL * line_of[0])
                    slot = chunks + (0 if c == 0 else 1)
                    carry[slot] = carry[slot] + gy
                    for f in range(4):
                        base = 0 if f < 2 else 5
                        add[f] = add[f] + (coef[base + index, own, :] + sign * v) * line_of[f]
                    add[3] = add[3] - vert * (carry[slot] - 0.5 * gy)
            for f in range(4):
                x2[k, f, own, :] = x2[k, f, own, :] + add[f]
        return tuple(carry)

    lax.fori_loop(1, levels, share, (nothing,) * (chunks + 2), unroll=UNROLL2)
    for copy in early_all:
        copy.wait_recv()
    tile = (cols // 8, 8, cols)
    sub3 = iota(tile, 1)
    lane3 = iota(tile, 2)
    keep = (sub3 // 2) == (lane3 // ATM_ROWS)
    wanted = (lax.rem(lane3, ATM_ROWS) + 1).astype(f32)
    for j in range(devices * 8 // cols):
        got = in_early[tile[0] * j : tile[0] * (j + 1)]
        ids = jnp.where((sub3 // 2) == 1, got, 0.0)
        ids = (ids + pltpu.roll(ids, 2, 1)) + (pltpu.roll(ids, 4, 1) + pltpu.roll(ids, 6, 1))
        hit = jnp.where(keep & (ids == wanted), 1.0, 0.0)
        row_hot[:, cols * j : cols * (j + 1)] = hit.reshape(cols, cols).T.astype(bf16)
    wets = jnp.where(iota((devices, 8, cols), 1) < 2, in_early[...], 0.0)
    cover = dot(row_hot[0:ATM_ROWS, :], wets.reshape(devices * 8, cols).astype(bf16))
    cover_v[...] = cover
    share = 1.0 / jnp.maximum(cover, 1.0)

    sums = jnp.zeros((4 * ATM_ROWS, cols), f32)
    for half, copy in enumerate(late_all):
        copy.wait_recv()
        got = in_late[near * half : near * (half + 1)].reshape(near * 8, cols)
        placed = row_hot[:, near * 8 * half : near * 8 * (half + 1)]
        for piece in split(got):
            sums = sums + dot(placed, piece)
    surf_v[...] = sums.reshape(4, ATM_ROWS, cols) * share

    for cond, copy in ups + downs:
        pl.when(cond)(copy.wait_send)
    drain_rows(*halo0_rows)
    drain_rows(*halo2_rows)
    for copy in [*sides, *halo0_cols, *halo2_cols]:
        copy.wait_send()
    whole = lambda ref, height: ref.at[0 : devices - 1, 0:height, :]
    for sem, (out, into, height) in enumerate(((out_early, in_early, 4), (out_late, in_late, 8))):
        pltpu.make_async_remote_copy(
            src_ref=whole(out, height), dst_ref=whole(into, height),
            send_sem=a_send.at[sem], recv_sem=a_recv.at[2 * sem], device_id=east, device_id_type=MESH,
        ).wait_send()


def write_out(x2, surf_v, cover_v, tracers_out, velocity_out, surface_out, cover_out, sem):
    stores = []
    for f in range(4):
        dst = (tracers_out if f < 2 else velocity_out).at[f % 2]
        stores.append(pltpu.make_async_copy(x2.at[:, f], dst, sem.at[f]))
    stores.append(pltpu.make_async_copy(cover_v, cover_out, sem.at[4]))
    stores.append(pltpu.make_async_copy(surf_v, surface_out, sem.at[5]))
    for store in stores:
        store.start()
    for store in stores:
        store.wait()


def local(tracers, velocity, land_mask, mixing, owners, atm_row):
    n_lon, n_lat = lax.axis_size("lon"), lax.axis_size("lat")
    levels = tracers.shape[1]
    rows, cols = land_mask.shape
    devices = n_lon * n_lat
    blocks = rows * cols // 128
    assert cols == 128 and blocks == rows and ATM_ROWS == 32
    any_spec = pl.BlockSpec(memory_space=pl.ANY)
    vmem = lambda *shape: pltpu.VMEM(shape, f32)
    tile = vmem(rows, cols)
    padded = rows + 16
    scratch = (
        [vmem(levels, 4, padded, cols)] * 2
        + [vmem(padded, cols)]
        + [pltpu.VMEM((rows, cols), jnp.int32), tile]
        + [pltpu.VMEM((1, blocks), jnp.int32)] * 2
        + [tile] * 12
        + [vmem(padded, cols)]
        + [vmem(levels, 4, cols)] * 3
        + [vmem(16, cols)] * 9
        + [vmem(12, rows, cols), pltpu.VMEM((devices * 8, PIECES * cols), bf16)]
        + [vmem(devices, 8, cols)] * 4
        + [pltpu.VMEM((4 * ATM_ROWS, devices * 8), bf16)]
        + [pltpu.SemaphoreType.DMA((8,))]
        + [pltpu.SemaphoreType.DMA((8,))] * 4
        + [pltpu.SemaphoreType.DMA((2,)), pltpu.SemaphoreType.DMA((4,))]
        + [pltpu.SemaphoreType.REGULAR]
    )
    ring = lambda d, size: min(d % size, size - d % size)
    half_lat = n_lat // 2
    hops = lambda a, c: ring(a, n_lon // 2) + ring(c // 2, half_lat // 2) + 2 * (a // (n_lon // 2)) + c // half_lat
    offsets = [(a, c) for a in range(n_lon) for c in range(n_lat) if a or c]
    offsets.sort(key=lambda o: hops(*o))
    held = pl.pallas_call(
        functools.partial(kernel, n_lon, n_lat, levels, rows, cols, offsets),
        out_shape=(vmem(levels, 4, rows, cols), vmem(4, ATM_ROWS, cols), vmem(ATM_ROWS, cols)),
        in_specs=[any_spec] * 6,
        scratch_shapes=scratch,
        compiler_params=pltpu.CompilerParams(collective_id=0, has_side_effects=True),
        name="ocean",
    )(tracers, velocity, land_mask, mixing, owners.reshape(1, blocks), atm_row.reshape(1, blocks))
    return pl.pallas_call(
        write_out,
        out_shape=(
            jax.ShapeDtypeStruct(tracers.shape, f32),
            jax.ShapeDtypeStruct(velocity.shape, f32),
            jax.ShapeDtypeStruct((4, ATM_ROWS, cols), f32),
            jax.ShapeDtypeStruct((ATM_ROWS, cols), f32),
        ),
        in_specs=[pl.BlockSpec(memory_space=pltpu.VMEM)] * 3,
        out_specs=(any_spec,) * 4,
        scratch_shapes=[pltpu.SemaphoreType.DMA((6,))],
        name="write_out",
    )(*(pltpu.with_memory_space_constraint(x, pltpu.VMEM) for x in held))


def solution(mesh):
    in_specs = (
        P(None, None, "lat", "lon"),
        P(None, None, "lat", "lon"),
        P("lat", "lon"),
        P("lat", "lon"),
        P(("lon", "lat"), None),
        P(("lon", "lat")),
    )
    out_specs = (
        P(None, None, "lat", "lon"),
        P(None, None, "lat", "lon"),
        P(None, ("lon", "lat"), None),
        P(("lon", "lat"), None),
    )
    return jax.shard_map(local, mesh=mesh, in_specs=in_specs, out_specs=out_specs, check_vma=False)
```

```python
import functools
import math

import jax
import jax.numpy as jnp
from jax import lax
from jax.experimental import pallas as pl
from jax.experimental.pallas import tpu as pltpu
from jax.sharding import PartitionSpec as P

THERMAL = 0.2
HALINE = 0.15
GRAVITY = 0.2
TIMESTEP = 0.8
VERTICAL_MIX = 0.1
VISCOSITY = 0.2
CORIOLIS_MAX = 0.3
ATM_ROWS = 32
UNROLL1, UNROLL2 = 2, 3
PIECES = 3

MESH = pl.DeviceIdType.MESH
ROW0 = 8
f32 = jnp.float32
bf16 = jnp.bfloat16


def iota(shape, dim):
    return lax.broadcasted_iota(jnp.int32, shape, dim)


def split(x):
    hi = x.astype(bf16)
    rest = x - hi.astype(f32)
    mid = rest.astype(bf16)
    lo = (rest - mid.astype(f32)).astype(bf16)
    return hi, mid, lo


def dot(a, b):
    return lax.dot_general(a, b, (((1,), (0,)), ((), ())), preferred_element_type=f32)


def reverse_lanes(x):
    lane = iota(x.shape, x.ndim - 1)
    size = x.shape[-1]
    step = size // 2
    while step:
        x = jnp.where(
            (lane & step) == 0,
            pltpu.roll(x, size - step, x.ndim - 1),
            pltpu.roll(x, step, x.ndim - 1),
        )
        step //= 2
    return x


def kernel(
    n_lon, n_lat, levels, rows, cols, offsets,
    tracers, velocity, land_mask, mixing, owners, atm_row,
    x2, surf_v, cover_v,
    x0, x1, wet_pad, mask_i, mix_v, own_v, row_v,
    pack0, pack1b, from_e0, from_w0, from_eb, from_wb, edge0, edge2b, rim, rim_e, rim_w, rim_new,
    rim_pad, fold0, rows_s, rows_n, own_up, up, down, r_s, r_se, r_sw, r_n, r_ne, r_nw,
    coef, onehot, out_early, in_early, out_late, in_late, row_hot,
    in_sem, c_send, c_recv, h_send, h_recv, a_send, a_recv, ready,
):
    devices = n_lon * n_lat
    lon = lax.axis_index("lon")
    lat = lax.axis_index("lat")
    me = lon * n_lat + lat
    top = n_lat - 1
    east = (lax.rem(lon + 1, n_lon), lat)
    west = (lax.rem(lon + n_lon - 1, n_lon), lat)
    north = (lon, lax.min(lat + 1, top))
    south = (lon, lax.max(lat - 1, 0))
    mirror = (n_lon - 1 - lon, lat)
    end = ROW0 + rows
    chunks = rows // 8

    loads = [
        pltpu.make_async_copy(land_mask, mask_i, in_sem.at[0]),
        pltpu.make_async_copy(mixing, mix_v, in_sem.at[1]),
        pltpu.make_async_copy(owners, own_v, in_sem.at[2]),
        pltpu.make_async_copy(atm_row, row_v, in_sem.at[3]),
    ]
    for lo, hi, sem in ((0, 2, 4), (2, levels, 8)):
        for f in range(4):
            src = (tracers if f < 2 else velocity).at[f % 2, lo:hi]
            loads.append(pltpu.make_async_copy(src, x0.at[lo:hi, f, ROW0:end, :], in_sem.at[sem + f]))
    for load in loads:
        load.start()

    barrier = pltpu.get_barrier_semaphore()
    for d in range(1, n_lon):
        pl.semaphore_signal(barrier, inc=1, device_id=(lax.rem(lon + d, n_lon), lat), device_id_type=MESH)
    for d in range(1, n_lat):
        pl.semaphore_signal(barrier, inc=1, device_id=(lon, lax.rem(lat + d, n_lat)), device_id_type=MESH)

    lat_n, lat_s = lax.rem(lat + 1, n_lat), lax.rem(lat + top, n_lat)
    for lon_to in (east[0], west[0]):
        for lat_to in (lat_n, lat_s):
            pl.semaphore_signal(barrier, inc=1, device_id=(lon_to, lat_to), device_id_type=MESH)

    lane8 = iota((8, cols), 1)
    lane = iota((rows, cols), 1)
    first = lane8 == 0
    last = lane8 == cols - 1

    def part(c):
        return slice(ROW0 + 8 * c, ROW0 + 8 * c + 8)

    def packed(tile, value, i):
        where = (lane8 == 2 * i) | (lane8 == lax.rem(2 * i + cols - 1, cols))
        return jnp.where(where, pltpu.roll(value, 2 * i, 1), tile)

    for row in (ROW0 - 1, end):
        x1[:, :, row, :] = jnp.zeros((levels, 4, cols), f32)

    loads[0].wait()
    wet = mask_i[...].astype(f32)
    wet_pad[ROW0:end, :] = wet
    for load in loads[4:8]:
        load.wait()

    def prepare(k, tiles):
        tiles = list(tiles)
        for f in range(4):
            for c in range(chunks):
                q = x0[k, f, part(c), :] * wet_pad[part(c), :]
                x0[k, f, part(c), :] = q
                tiles[c] = packed(tiles[c], q, 4 * k + f)
        return tuple(tiles)

    empty = tuple(jnp.zeros((8, cols), f32) for _ in range(chunks))
    packs = prepare(1, prepare(0, empty))

    loads[1].wait()
    rate_t = TIMESTEP * mix_v[...]
    rate_v = jnp.full((rows, cols), TIMESTEP * VISCOSITY, f32)
    group = lane // 4
    packed_rim = jnp.zeros((rows, cols), f32)
    quantities = [x0[k, f, ROW0:end, :] for k in range(2) for f in range(4)]
    quantities += [wet] * 4 + [rate_t, rate_t, rate_v, rate_v]
    for i, value in enumerate(quantities):
        packed_rim = jnp.where(group == i, pltpu.roll(value, 4 * i + 2, 1), packed_rim)
    rim[...] = packed_rim
    for buf, edge, second in ((own_up, end - 1, end - 2), (down, ROW0, ROW0 + 1)):
        for f in range(4):
            buf[f : f + 1, :] = x0[0, f, edge : edge + 1, :]
            buf[4 + f : 5 + f, :] = x0[0, f, second : second + 1, :]
            buf[8 + f : 9 + f, :] = x0[1, f, edge : edge + 1, :]
        buf[12:13, :] = wet_pad[edge : edge + 1, :]
        buf[13:14, :] = wet_pad[second : second + 1, :]
        buf[14:15, :] = mix_v[edge - ROW0 : edge - ROW0 + 1, :]
        buf[15:16, :] = rim[edge - ROW0 : edge - ROW0 + 1, :]
    up[...] = own_up[...]

    @pl.when(lat == top)
    def _():
        raw = own_up[...]
        turned = reverse_lanes(raw)
        sub16, lane16 = iota((16, cols), 0), iota((16, cols), 1)
        swapped = jnp.where(lane16 % 4 == 1, pltpu.roll(raw, cols - 1, 1), pltpu.roll(raw, 1, 1))
        turned = jnp.where(sub16 == 15, swapped, turned)
        which = jnp.where(sub16 == 15, lane16 // 4, sub16)
        turned = jnp.where((which < jnp.where(sub16 == 15, 8, 12)) & (which % 4 >= 2), -turned, turned)
        up[...] = turned

    @pl.when(lat == 0)
    def _():
        x0[:, :, ROW0 - 1, :] = jnp.zeros((levels, 4, cols), f32)
        rows_s[...] = jnp.zeros((levels, 4, cols), f32)
        for ref in (r_s, r_se, r_sw):
            ref[...] = jnp.zeros((16, cols), f32)

    pl.semaphore_wait(barrier, n_lon + n_lat + 2)

    def link(src, dst, send_sem, recv_sem, device):
        return pltpu.make_async_remote_copy(
            src_ref=src, dst_ref=dst, send_sem=send_sem, recv_sem=recv_sem,
            device_id=device, device_id_type=MESH,
        )

    def remote(src, dst, sem, device):
        return link(src, dst, h_send.at[sem], h_recv.at[sem], device)

    def first_link(src, dst, send_sem, recv_sem, device):
        return link(src, dst, c_send.at[send_sem], c_recv.at[recv_sem], device)

    fold_ne = lax.rem(2 * n_lon - 2 - lon, n_lon)
    fold_nw = lax.rem(n_lon - lon, n_lon)
    below_top, is_top, above_bottom = lat < top, lat == top, lat > 0
    ups = [
        (below_top, first_link(up, r_s, 0, 0, north)),
        (below_top, first_link(up, r_sw, 1, 2, (east[0], north[1]))),
        (below_top, first_link(up, r_se, 2, 1, (west[0], north[1]))),
        (is_top, first_link(up, r_n, 0, 3, mirror)),
        (is_top & (fold_ne != lon), first_link(up, r_ne, 1, 4, (fold_ne, lat))),
        (is_top & (fold_nw != lon), first_link(up, r_nw, 2, 5, (fold_nw, lat))),
    ]
    downs = [
        (above_bottom, first_link(down, r_n, 3, 3, south)),
        (above_bottom, first_link(down, r_nw, 4, 5, (east[0], south[1]))),
        (above_bottom, first_link(down, r_ne, 5, 4, (west[0], south[1]))),
    ]
    sides = [first_link(rim, rim_w, 6, 6, east), first_link(rim, rim_e, 7, 7, west)]
    for copy in sides:
        copy.start()
    for cond, copy in ups + downs:
        pl.when(cond)(copy.start)

    @pl.when(is_top & (fold_ne == lon))
    def _():
        r_ne[...] = up[...]

    @pl.when(is_top & (fold_nw == lon))
    def _():
        r_nw[...] = up[...]

    def row_copies(x, lo, sem, into_s, into_n, into_fold):
        last_row, first_row = x.at[lo:levels, :, end - 1, :], x.at[lo:levels, :, ROW0, :]
        ahead = remote(last_row, into_s, sem, north)
        over = remote(last_row, into_fold, sem + 1, mirror)
        back = remote(first_row, into_n, sem + 1, south)
        return ahead, over, back

    def start_rows(ahead, over, back):
        pl.when(lat < top)(ahead.start)
        pl.when(lat == top)(over.start)
        pl.when(lat > 0)(back.start)

    def wait_rows(ahead, over, back):
        pl.when(lat > 0)(ahead.wait_recv)
        pl.when(lat == top)(over.wait_recv)
        pl.when(lat < top)(back.wait_recv)

    def drain_rows(ahead, over, back):
        pl.when(lat < top)(ahead.wait_send)
        pl.when(lat == top)(over.wait_send)
        pl.when(lat > 0)(back.wait_send)

    def col_copies(pack, from_w, from_e, sem):
        return remote(pack, from_w, sem, east), remote(pack, from_e, sem + 1, west)

    for d in range(1, n_lat):
        pl.semaphore_signal(ready, inc=1, device_id=(lon, lax.rem(lat + d, n_lat)), device_id_type=MESH)

    for load in loads[8:]:
        load.wait()
    tiles = lax.fori_loop(2, levels, prepare, packs, unroll=2)
    for c in range(chunks):
        pack0[8 * c : 8 * c + 8, :] = tiles[c]
    halo0_rows = row_copies(
        x0, 2, 0, x0.at[2:levels, :, ROW0 - 1, :], x0.at[2:levels, :, end, :], fold0.at[2:levels]
    )
    halo0_cols = col_copies(pack0, from_w0, from_e0, 2)
    start_rows(*halo0_rows)
    for copy in halo0_cols:
        copy.start()

    loads[2].wait()
    loads[3].wait()
    blocks = rows
    pad_row = lambda ref: jnp.concatenate([ref[...].astype(f32)] * (cols // blocks), axis=1)
    own_lane = pad_row(own_v)
    row_lane = pad_row(row_v)
    sub = iota((blocks, cols), 0)
    own_col = jnp.sum(jnp.where(lane == sub, own_lane, 0.0), axis=1, keepdims=True)
    row_col = jnp.sum(jnp.where(lane == sub, row_lane + 1.0, 0.0), axis=1, keepdims=True)
    same = jnp.where((own_col == own_lane) & (sub < lax.rem(lane, blocks)), 1.0, 0.0)
    position = jnp.sum(same, axis=0, keepdims=True)
    lane1 = iota((1, cols), 1)
    target = own_lane.astype(jnp.int32) * 8 + (lane1 // blocks) * 2 + position.astype(jnp.int32)
    hot = jnp.where(iota((devices * 8, cols), 0) == target, 1.0, 0.0).astype(bf16)
    for j in range(PIECES):
        onehot[:, cols * j : cols * (j + 1)] = hot
    early = jnp.concatenate(
        [wet, jnp.broadcast_to(row_col, (blocks, cols)), jnp.zeros((2 * blocks, cols), f32)], axis=0
    )
    out_early[...] = dot(hot, early.astype(bf16)).reshape(devices, 8, cols)
    in_early[devices - 1 : devices] = out_early[pl.ds(me, 1)]

    def turning(row):
        angle = math.pi * (-0.43 + 0.93 * (row.astype(f32) + 0.5) / (n_lat * rows))
        return CORIOLIS_MAX * jnp.sin(angle)

    coriolis = turning(lat * rows + iota((rows, cols), 0))
    rim_row = jnp.where(iota((8, cols), 0) < 4, lat * rows - 1, lax.min((lat + 1) * rows, n_lat * rows - 1))
    coriolis8 = turning(rim_row)

    near = devices // 2

    def exchange(out, into, sem, height):
        for slot, (a, c) in enumerate(offsets):
            to_lon, to_lat = lax.rem(lon + a, n_lon), lax.rem(lat + c, n_lat)
            pltpu.make_async_remote_copy(
                src_ref=out.at[to_lon * n_lat + to_lat, 0:height, :], dst_ref=into.at[slot, 0:height, :],
                send_sem=a_send.at[sem], recv_sem=a_recv.at[2 * sem + slot // near],
                device_id=(to_lon, to_lat), device_id_type=MESH,
            ).start()
        parts = []
        for lo, hi, half in ((0, near, 0), (near, devices - 1, 1)):
            span = lambda ref: ref.at[lo:hi, 0:height, :]
            parts.append(pltpu.make_async_remote_copy(
                src_ref=span(out), dst_ref=span(into),
                send_sem=a_send.at[sem], recv_sem=a_recv.at[2 * sem + half],
                device_id=east, device_id_type=MESH,
            ))
        return parts

    pl.semaphore_wait(ready, n_lat - 1)
    early_all = exchange(out_early, in_early, 0, 4)

    for copy in sides:
        copy.wait_recv()
    arrivals = [
        (above_bottom, ups[0]), (above_bottom, ups[1]), (above_bottom, ups[2]),
        (below_top, downs[0]), (below_top, downs[1]), (below_top, downs[2]), (is_top, ups[3]),
        (is_top & (fold_ne != lon), ups[4]), (is_top & (fold_nw != lon), ups[5]),
    ]
    for cond, (_, copy) in arrivals:
        pl.when(cond)(copy.wait_recv)

    centre = 1.0 - 2.0 * TIMESTEP * VERTICAL_MIX
    vertical = TIMESTEP * VERTICAL_MIX

    def surface_step(q, e, w, n, s, below, wets, rate, turn, u, v, field, gx, gy):
        we, ww, wn, ws, wc = wets
        dx, dy = e - w, n - s
        extra = jnp.where(
            field == 2, TIMESTEP * turn * v - (0.25 * TIMESTEP * GRAVITY) * gx(dx),
            jnp.where(field == 3, -TIMESTEP * turn * u - (0.25 * TIMESTEP * GRAVITY) * gy(dy), 0.0),
        )
        spread = (we * e + ww * w) + (wn * n + ws * s)
        return wc * (
            q * (centre - rate * (we + ww + wn + ws)) + vertical * (q + below) + rate * spread
            - (0.5 * TIMESTEP) * (u * dx + v * dy) + extra
        )

    two = lambda a, b: jnp.concatenate([a, b], axis=0)
    four = lambda a, b: two(jnp.broadcast_to(a, (4, cols)), jnp.broadcast_to(b, (4, cols)))
    from_right = lambda x, corner: pltpu.roll(jnp.where(first, corner, x), cols - 1, 1)
    from_left = lambda x, corner: pltpu.roll(jnp.where(last, corner, x), 1, 1)
    both = lambda a, b, lo: two(a[lo : lo + 4, :], b[lo : lo + 4, :])
    line = lambda a, b, i: four(a[i : i + 1, :], b[i : i + 1, :])
    q8 = both(r_s, r_n, 0)
    wet8 = line(r_s, r_n, 12)
    field8 = iota((8, cols), 0) % 4
    of = lambda x, i: four(x[i : i + 1], x[4 + i : 5 + i])
    slope = lambda d: HALINE * of(d, 1) - THERMAL * of(d, 0)
    rows_new = surface_step(
        q8, from_right(q8, both(r_se, r_ne, 0)), from_left(q8, both(r_sw, r_nw, 0)),
        two(down[0:4, :], r_n[4:8, :]), two(r_s[4:8, :], own_up[0:4, :]), both(r_s, r_n, 8),
        (
            from_right(wet8, line(r_se, r_ne, 12)), from_left(wet8, line(r_sw, r_nw, 12)),
            four(down[12:13, :], r_n[13:14, :]), four(r_s[13:14, :], own_up[12:13, :]), wet8,
        ),
        jnp.where(field8 < 2, TIMESTEP * line(r_s, r_n, 14), TIMESTEP * VISCOSITY),
        coriolis8, of(q8, 2), of(q8, 3), field8, slope, slope,
    )
    for f in range(4):
        x1[0, f, ROW0 - 1 : ROW0, :] = rows_new[f : f + 1]
        x1[0, f, end : end + 1, :] = rows_new[4 + f : 5 + f]
        for k in range(2):
            x0[k, f, ROW0 - 1 : ROW0, :] = r_s[8 * k + f : 8 * k + f + 1, :]
            x0[k, f, end : end + 1, :] = r_n[8 * k + f : 8 * k + f + 1, :]
    wet_pad[ROW0 - 1 : ROW0, :] = r_s[12:13, :]
    wet_pad[end : end + 1, :] = r_n[12:13, :]

    low = lane % 4 < 2
    halves = lambda a, b: jnp.where(iota(a.shape, 1) < cols // 2, a, pltpu.roll(b, cols // 2 - 1, 1))
    own_rim, east_rim, west_rim = rim[...], rim_e[...], rim_w[...]
    strip = halves(jnp.where(low, west_rim, own_rim), jnp.where(low, own_rim, east_rim))
    rim_pad[ROW0:end, :] = strip
    wide = lambda ref: jnp.broadcast_to(ref[15:16, :], (8, cols))
    rim_pad[ROW0 - 1 : ROW0, :] = halves(wide(r_sw), wide(r_se))[0:1]
    rim_pad[end : end + 1, :] = halves(wide(r_nw), wide(r_ne))[0:1]
    strip_n = rim_pad[ROW0 + 1 : end + 1, :]
    strip_s = rim_pad[ROW0 - 1 : end - 1, :]
    right = lambda x, d: pltpu.roll(x, (d + cols) % cols, 1)
    wets = [right(x, -32) for x in (strip_n, strip_s, strip)]
    field = group % 16

    def spread_field(i):
        out = strip
        for f in range(4):
            if f != i:
                out = jnp.where(field == f, right(strip, 4 * (f - i)), out)
        return out

    rim_new[...] = surface_step(
        strip, right(strip, -1), right(strip, 1), strip_n, strip_s, right(strip, -16),
        (right(wets[2], -1), right(wets[2], 1), wets[0], wets[1], wets[2]),
        right(strip, -48), coriolis, spread_field(2), spread_field(3), field,
        lambda d: HALINE * right(d, 4) - THERMAL * right(d, 8),
        lambda d: HALINE * right(d, 8) - THERMAL * right(d, 12),
    )

    at = lambda x, src, dst: pltpu.roll(x, (dst - src + cols) % cols, 1)
    w_east = pltpu.roll(jnp.where(lane == 0, at(east_rim, 34, 0), wet), cols - 1, 1)
    w_west = pltpu.roll(jnp.where(lane == cols - 1, at(west_rim, 33, cols - 1), wet), 1, 1)
    w_north = wet_pad[ROW0 + 1 : end + 1, :]
    w_south = wet_pad[ROW0 - 1 : end - 1, :]
    total = w_east + w_west + w_north + w_south
    for base, rate in ((0, rate_t), (5, TIMESTEP * VISCOSITY)):
        coef[base] = wet * (centre - rate * total)
        for j, w in enumerate((w_east, w_west, w_north, w_south)):
            coef[base + 1 + j] = wet * (rate * w)
    coef[10] = vertical * wet
    coef[11] = TIMESTEP * coriolis * wet

    pressure_rate = 0.5 * TIMESTEP * GRAVITY
    assert abs(pressure_rate - TIMESTEP * VERTICAL_MIX) < 1e-12

    def level(x, k, side_of, carry, store):
        above = lax.max(k - 1, 0) if not isinstance(k, int) else max(k - 1, 0)
        below = lax.min(k + 1, levels - 1) if not isinstance(k, int) else min(k + 1, levels - 1)
        carry = list(carry)
        for c in range(chunks):
            mid = part(c)
            ahead = slice(ROW0 + 8 * c + 1, ROW0 + 8 * c + 9)
            behind = slice(ROW0 + 8 * c - 1, ROW0 + 8 * c + 7)
            own = slice(8 * c, 8 * c + 8)
            q, e, w, n, s = [], [], [], [], []
            for f in range(4):
                value = x[k, f, mid, :]
                side = side_of(own, k, f)
                q.append(value)
                e.append(pltpu.roll(jnp.where(first, side, value), cols - 1, 1))
                w.append(pltpu.roll(jnp.where(last, side, value), 1, 1))
                n.append(x[k, f, ahead, :])
                s.append(x[k, f, behind, :])
            gx = HALINE * (e[1] - w[1]) - THERMAL * (e[0] - w[0])
            gy = HALINE * (n[1] - s[1]) - THERMAL * (n[0] - s[0])
            sx = carry[2 * c] + gx
            sy = carry[2 * c + 1] + gy
            carry[2 * c], carry[2 * c + 1] = sx, sy
            push = (None, None, sx - 0.5 * gx, sy - 0.5 * gy)
            u = (0.5 * TIMESTEP) * q[2]
            v = (0.5 * TIMESTEP) * q[3]
            vert = coef[10, own, :]
            turn = coef[11, own, :]
            for f in range(4):
                if f % 2 == 0:
                    base = 0 if f == 0 else 5
                    a = coef[base, own, :]
                    ce = coef[base + 1, own, :] - u
                    cw = coef[base + 2, own, :] + u
                    cn = coef[base + 3, own, :] - v
                    cs = coef[base + 4, own, :] + v
                column = x[above, f, mid, :] + x[below, f, mid, :]
                if f >= 2:
                    column = column - push[f]
                value = (a * q[f] + vert * column) + (ce * e[f] + cw * w[f]) + (cn * n[f] + cs * s[f])
                if f == 2:
                    value = value + turn * q[3]
                if f == 3:
                    value = value - turn * q[2]
                store(k, f, c, value)
        return tuple(carry)

    def merge(edge, from_e, from_w):
        edge[...] = jnp.where(lax.rem(lane, 2) == 0, from_e[...], from_w[...])

    def unfold(fold, lo, hi, put):
        @pl.when(lat == top)
        def _():
            for k in range(lo, hi, 2):
                width = min(2, hi - k)
                pair = fold[k : k + width].reshape(4 * width, cols)
                pair = reverse_lanes(pair)
                field = lax.rem(iota(pair.shape, 0), 4)
                pair = jnp.where(field < 2, pair, -pair)
                put(k, width, pair)

    def packed_side(edge):
        return lambda own, k, f: pltpu.roll(edge[own, :], lax.rem(2 * cols - 2 * (4 * k + f), cols), 1)

    def rim_side(from_east, lane_e, from_west, lane_w):
        def side(own, k, f):
            i = 4 * (4 * k + f)
            east_value = at(from_east[own, :], lane_e + i, 0)
            return jnp.where(first, east_value, at(from_west[own, :], lane_w + i, cols - 1))

        return side

    zeros = tuple(jnp.zeros((8, cols), f32) for _ in range(2 * chunks))

    def step1(k, side_of, carry, tiles):
        tiles = list(tiles)

        def store(k, f, c, value):
            x1[k, f, part(c), :] = value
            if tiles:
                tiles[c] = packed(tiles[c], value, 4 * k + f)

        carry = level(x0, k, side_of, carry, store)
        return carry, tuple(tiles)

    near_side = rim_side(rim_e, 2, rim_w, 1)
    carry1, _ = step1(0, near_side, zeros, ())
    carry1, tiles = step1(1, near_side, carry1, empty)

    def store2(k, f, c, value):
        x2[k, f, 8 * c : 8 * c + 8, :] = value

    carry2 = level(x1, 0, rim_side(rim_new, 65, rim_new, 1), zeros, store2)
    surf = x2[0].reshape(4 * rows, cols)
    late = dot(onehot[...], jnp.concatenate(split(surf), axis=0))
    out_late[...] = late.reshape(devices, 8, cols)
    in_late[devices - 1 : devices] = out_late[pl.ds(me, 1)]
    late_all = exchange(out_late, in_late, 1, 8)

    for copy in halo0_cols:
        copy.wait_recv()
    wait_rows(*halo0_rows)
    merge(edge0, from_e0, from_w0)

    def put_rows(k, width, pair):
        for j in range(width):
            for f in range(4):
                x0[k + j, f, end : end + 1, :] = pair[4 * j + f : 4 * j + f + 1]

    unfold(fold0, 2, levels, put_rows)
    _, tiles = lax.fori_loop(
        2, levels, lambda k, s: step1(k, packed_side(edge0), *s), (carry1, tiles), unroll=UNROLL1
    )
    for c in range(chunks):
        pack1b[8 * c : 8 * c + 8, :] = tiles[c]
    halo2_rows = row_copies(
        x1, 1, 4, rows_s.at[1:levels], rows_n.at[1:levels], rows_n.at[1:levels]
    )
    halo2_cols = col_copies(pack1b, from_wb, from_eb, 6)
    start_rows(*halo2_rows)
    for copy in halo2_cols:
        copy.start()

    nothing = jnp.zeros((8, cols), f32)
    lax.fori_loop(
        1, levels, lambda k, s: level(x1, k, lambda own, k, f: nothing, s, store2), carry2, unroll=UNROLL2
    )

    for copy in early_all:
        copy.wait_recv()
    tile = (cols // 8, 8, cols)
    sub3 = iota(tile, 1)
    lane3 = iota(tile, 2)
    keep = (sub3 // 2) == (lane3 // ATM_ROWS)
    wanted = (lax.rem(lane3, ATM_ROWS) + 1).astype(f32)
    for j in range(devices * 8 // cols):
        got = in_early[tile[0] * j : tile[0] * (j + 1)]
        ids = jnp.where((sub3 // 2) == 1, got, 0.0)
        ids = (ids + pltpu.roll(ids, 2, 1)) + (pltpu.roll(ids, 4, 1) + pltpu.roll(ids, 6, 1))
        hit = jnp.where(keep & (ids == wanted), 1.0, 0.0)
        row_hot[:, cols * j : cols * (j + 1)] = hit.reshape(cols, cols).T.astype(bf16)
    wets = jnp.where(iota((devices, 8, cols), 1) < 2, in_early[...], 0.0)
    cover = dot(row_hot[0:ATM_ROWS, :], wets.reshape(devices * 8, cols).astype(bf16))
    cover_v[...] = cover
    share = 1.0 / jnp.maximum(cover, 1.0)

    for copy in halo2_cols:
        copy.wait_recv()
    wait_rows(*halo2_rows)
    edge2b[...] = jnp.where(
        lax.rem(lane, 2) == 0, pltpu.roll(from_wb[...], 1, 1), pltpu.roll(from_eb[...], cols - 1, 1)
    )

    def put_back(k, width, pair):
        rows_n[k : k + width] = pair.reshape(width, 4, cols)

    unfold(rows_n, 1, levels, put_back)

    def halo_share(k, carry):
        carry = list(carry)
        for c in range(chunks):
            own, mid = slice(8 * c, 8 * c + 8), part(c)
            u = (0.5 * TIMESTEP) * x1[k, 2, mid, :]
            v = (0.5 * TIMESTEP) * x1[k, 3, mid, :]
            vert = coef[10, own, :]
            side = edge2b[own, :]
            halo = [pltpu.roll(side, lax.rem(2 * cols - 2 * (4 * k + f), cols), 1) for f in range(4)]
            gx = HALINE * halo[1] - THERMAL * halo[0]
            gx = jnp.where(last, gx, jnp.where(first, -gx, 0.0))
            carry[c] = carry[c] + gx
            add = []
            for f in range(4):
                base = 0 if f < 2 else 5
                rate = jnp.where(
                    last, coef[base + 1, own, :] - u, jnp.where(first, coef[base + 2, own, :] + u, 0.0)
                )
                add.append(rate * halo[f])
            add[2] = add[2] - vert * (carry[c] - 0.5 * gx)
            for outside, rows_of, edge, index, sign in (
                (c == 0, rows_s, 0, 4, 1.0), (c == chunks - 1, rows_n, 7, 3, -1.0)
            ):
                if outside:
                    here = iota((8, cols), 0) == edge
                    line_of = [
                        jnp.where(here, jnp.broadcast_to(rows_of[k, f : f + 1, :], (8, cols)), 0.0)
                        for f in range(4)
                    ]
                    gy = -sign * (HALINE * line_of[1] - THERMAL * line_of[0])
                    slot = chunks + (0 if c == 0 else 1)
                    carry[slot] = carry[slot] + gy
                    for f in range(4):
                        base = 0 if f < 2 else 5
                        add[f] = add[f] + (coef[base + index, own, :] + sign * v) * line_of[f]
                    add[3] = add[3] - vert * (carry[slot] - 0.5 * gy)
            for f in range(4):
                x2[k, f, own, :] = x2[k, f, own, :] + add[f]
        return tuple(carry)

    lax.fori_loop(1, levels, halo_share, (nothing,) * (chunks + 2), unroll=UNROLL2)
    sums = jnp.zeros((4 * ATM_ROWS, cols), f32)
    for half, copy in enumerate(late_all):
        copy.wait_recv()
        got = in_late[near * half : near * (half + 1)].reshape(near * 8, cols)
        placed = row_hot[:, near * 8 * half : near * 8 * (half + 1)]
        for piece in split(got):
            sums = sums + dot(placed, piece)
    surf_v[...] = sums.reshape(4, ATM_ROWS, cols) * share

    for cond, copy in ups + downs:
        pl.when(cond)(copy.wait_send)
    drain_rows(*halo0_rows)
    drain_rows(*halo2_rows)
    for copy in [*sides, *halo0_cols, *halo2_cols]:
        copy.wait_send()
    whole = lambda ref, height: ref.at[0 : devices - 1, 0:height, :]
    for sem, (out, into, height) in enumerate(((out_early, in_early, 4), (out_late, in_late, 8))):
        pltpu.make_async_remote_copy(
            src_ref=whole(out, height), dst_ref=whole(into, height),
            send_sem=a_send.at[sem], recv_sem=a_recv.at[2 * sem], device_id=east, device_id_type=MESH,
        ).wait_send()


def write_out(x2, surf_v, cover_v, tracers_out, velocity_out, surface_out, cover_out, sem):
    stores = []
    for f in range(4):
        dst = (tracers_out if f < 2 else velocity_out).at[f % 2]
        stores.append(pltpu.make_async_copy(x2.at[:, f], dst, sem.at[f]))
    stores.append(pltpu.make_async_copy(cover_v, cover_out, sem.at[4]))
    stores.append(pltpu.make_async_copy(surf_v, surface_out, sem.at[5]))
    for store in stores:
        store.start()
    for store in stores:
        store.wait()


def local(tracers, velocity, land_mask, mixing, owners, atm_row):
    n_lon, n_lat = lax.axis_size("lon"), lax.axis_size("lat")
    levels = tracers.shape[1]
    rows, cols = land_mask.shape
    devices = n_lon * n_lat
    blocks = rows * cols // 128
    assert cols == 128 and blocks == rows and ATM_ROWS == 32
    any_spec = pl.BlockSpec(memory_space=pl.ANY)
    vmem = lambda *shape: pltpu.VMEM(shape, f32)
    tile = vmem(rows, cols)
    padded = rows + 16
    scratch = (
        [vmem(levels, 4, padded, cols)] * 2
        + [vmem(padded, cols)]
        + [pltpu.VMEM((rows, cols), jnp.int32), tile]
        + [pltpu.VMEM((1, blocks), jnp.int32)] * 2
        + [tile] * 12
        + [vmem(padded, cols)]
        + [vmem(levels, 4, cols)] * 3
        + [vmem(16, cols)] * 9
        + [vmem(12, rows, cols), pltpu.VMEM((devices * 8, PIECES * cols), bf16)]
        + [vmem(devices, 8, cols)] * 4
        + [pltpu.VMEM((4 * ATM_ROWS, devices * 8), bf16)]
        + [pltpu.SemaphoreType.DMA((12,))]
        + [pltpu.SemaphoreType.DMA((8,))] * 4
        + [pltpu.SemaphoreType.DMA((2,)), pltpu.SemaphoreType.DMA((4,))]
        + [pltpu.SemaphoreType.REGULAR]
    )
    ring = lambda d, size: min(d % size, size - d % size)
    half_lat = n_lat // 2
    hops = lambda a, c: ring(a, n_lon // 2) + ring(c // 2, half_lat // 2) + 2 * (a // (n_lon // 2)) + c // half_lat
    offsets = [(a, c) for a in range(n_lon) for c in range(n_lat) if a or c]
    offsets.sort(key=lambda o: hops(*o))
    held = pl.pallas_call(
        functools.partial(kernel, n_lon, n_lat, levels, rows, cols, offsets),
        out_shape=(vmem(levels, 4, rows, cols), vmem(4, ATM_ROWS, cols), vmem(ATM_ROWS, cols)),
        in_specs=[any_spec] * 6,
        scratch_shapes=scratch,
        compiler_params=pltpu.CompilerParams(collective_id=0, has_side_effects=True),
        name="ocean",
    )(tracers, velocity, land_mask, mixing, owners.reshape(1, blocks), atm_row.reshape(1, blocks))
    return pl.pallas_call(
        write_out,
        out_shape=(
            jax.ShapeDtypeStruct(tracers.shape, f32),
            jax.ShapeDtypeStruct(velocity.shape, f32),
            jax.ShapeDtypeStruct((4, ATM_ROWS, cols), f32),
            jax.ShapeDtypeStruct((ATM_ROWS, cols), f32),
        ),
        in_specs=[pl.BlockSpec(memory_space=pltpu.VMEM)] * 3,
        out_specs=(any_spec,) * 4,
        scratch_shapes=[pltpu.SemaphoreType.DMA((6,))],
        name="write_out",
    )(*(pltpu.with_memory_space_constraint(x, pltpu.VMEM) for x in held))


def solution(mesh):
    in_specs = (
        P(None, None, "lat", "lon"),
        P(None, None, "lat", "lon"),
        P("lat", "lon"),
        P("lat", "lon"),
        P(("lon", "lat"), None),
        P(("lon", "lat")),
    )
    out_specs = (
        P(None, None, "lat", "lon"),
        P(None, None, "lat", "lon"),
        P(None, ("lon", "lat"), None),
        P(("lon", "lat"), None),
    )
    return jax.shard_map(local, mesh=mesh, in_specs=in_specs, out_specs=out_specs, check_vma=False)
```

```python
import functools
import math

import jax
import jax.numpy as jnp
from jax import lax
from jax.experimental import pallas as pl
from jax.experimental.pallas import tpu as pltpu
from jax.sharding import PartitionSpec as P

THERMAL = 0.2
HALINE = 0.15
GRAVITY = 0.2
TIMESTEP = 0.8
VERTICAL_MIX = 0.1
VISCOSITY = 0.2
CORIOLIS_MAX = 0.3
ATM_ROWS = 32
UNROLL1, UNROLL2 = 2, 3
PIECES = 3

MESH = pl.DeviceIdType.MESH
ROW0 = 8
f32 = jnp.float32
bf16 = jnp.bfloat16


def iota(shape, dim):
    return lax.broadcasted_iota(jnp.int32, shape, dim)


def split(x):
    hi = x.astype(bf16)
    rest = x - hi.astype(f32)
    mid = rest.astype(bf16)
    lo = (rest - mid.astype(f32)).astype(bf16)
    return hi, mid, lo


def dot(a, b):
    return lax.dot_general(a, b, (((1,), (0,)), ((), ())), preferred_element_type=f32)


def reverse_lanes(x):
    lane = iota(x.shape, x.ndim - 1)
    size = x.shape[-1]
    step = size // 2
    while step:
        x = jnp.where(
            (lane & step) == 0,
            pltpu.roll(x, size - step, x.ndim - 1),
            pltpu.roll(x, step, x.ndim - 1),
        )
        step //= 2
    return x


def kernel(
    n_lon, n_lat, levels, rows, cols, offsets,
    tracers, velocity, land_mask, mixing, owners, atm_row,
    x2, surf_v, cover_v,
    x0, x1, wet_pad, mask_i, mix_v, own_v, row_v,
    pack0, pack1b, from_e0, from_w0, from_eb, from_wb, edge0, edge2b, rim, rim_e, rim_w, rim_new,
    rim_pad, fold0, rows_s, rows_n, own_up, up, down, r_s, r_se, r_sw, r_n, r_ne, r_nw,
    coef, onehot, out_early, in_early, out_late, in_late, row_hot,
    in_sem, c_send, c_recv, h_send, h_recv, a_send, a_recv, ready,
):
    devices = n_lon * n_lat
    lon = lax.axis_index("lon")
    lat = lax.axis_index("lat")
    me = lon * n_lat + lat
    top = n_lat - 1
    east = (lax.rem(lon + 1, n_lon), lat)
    west = (lax.rem(lon + n_lon - 1, n_lon), lat)
    north = (lon, lax.min(lat + 1, top))
    south = (lon, lax.max(lat - 1, 0))
    mirror = (n_lon - 1 - lon, lat)
    end = ROW0 + rows
    chunks = rows // 8

    loads = [
        pltpu.make_async_copy(land_mask, mask_i, in_sem.at[0]),
        pltpu.make_async_copy(mixing, mix_v, in_sem.at[1]),
        pltpu.make_async_copy(owners, own_v, in_sem.at[2]),
        pltpu.make_async_copy(atm_row, row_v, in_sem.at[3]),
    ]
    for lo, hi, sem in ((0, 2, 4), (2, levels, 8)):
        for f in range(4):
            src = (tracers if f < 2 else velocity).at[f % 2, lo:hi]
            loads.append(pltpu.make_async_copy(src, x0.at[lo:hi, f, ROW0:end, :], in_sem.at[sem + f]))
    for load in loads:
        load.start()

    barrier = pltpu.get_barrier_semaphore()
    for d in range(1, n_lon):
        pl.semaphore_signal(barrier, inc=1, device_id=(lax.rem(lon + d, n_lon), lat), device_id_type=MESH)
    for d in range(1, n_lat):
        pl.semaphore_signal(barrier, inc=1, device_id=(lon, lax.rem(lat + d, n_lat)), device_id_type=MESH)

    lat_n, lat_s = lax.rem(lat + 1, n_lat), lax.rem(lat + top, n_lat)
    for lon_to in (east[0], west[0]):
        for has, lat_to in ((lat < top, lat_n), (lat > 0, lat_s)):

            @pl.when(has)
            def _():
                pl.semaphore_signal(barrier, inc=1, device_id=(lon_to, lat_to), device_id_type=MESH)

    lane8 = iota((8, cols), 1)
    lane = iota((rows, cols), 1)
    first = lane8 == 0
    last = lane8 == cols - 1

    def part(c):
        return slice(ROW0 + 8 * c, ROW0 + 8 * c + 8)

    def packed(tile, value, i):
        where = (lane8 == 2 * i) | (lane8 == lax.rem(2 * i + cols - 1, cols))
        return jnp.where(where, pltpu.roll(value, 2 * i, 1), tile)

    for row in (ROW0 - 1, end):
        x1[:, :, row, :] = jnp.zeros((levels, 4, cols), f32)

    loads[0].wait()
    wet = mask_i[...].astype(f32)
    wet_pad[ROW0:end, :] = wet
    for load in loads[4:8]:
        load.wait()

    def prepare(k, tiles):
        tiles = list(tiles)
        for f in range(4):
            for c in range(chunks):
                q = x0[k, f, part(c), :] * wet_pad[part(c), :]
                x0[k, f, part(c), :] = q
                tiles[c] = packed(tiles[c], q, 4 * k + f)
        return tuple(tiles)

    empty = tuple(jnp.zeros((8, cols), f32) for _ in range(chunks))
    packs = prepare(1, prepare(0, empty))

    loads[1].wait()
    rate_t = TIMESTEP * mix_v[...]
    rate_v = jnp.full((rows, cols), TIMESTEP * VISCOSITY, f32)
    group = lane // 4
    packed_rim = jnp.zeros((rows, cols), f32)
    quantities = [x0[k, f, ROW0:end, :] for k in range(2) for f in range(4)]
    quantities += [wet] * 4 + [rate_t, rate_t, rate_v, rate_v]
    for i, value in enumerate(quantities):
        packed_rim = jnp.where(group == i, pltpu.roll(value, 4 * i + 2, 1), packed_rim)
    rim[...] = packed_rim
    for buf, edge, second in ((own_up, end - 1, end - 2), (down, ROW0, ROW0 + 1)):
        for f in range(4):
            buf[f : f + 1, :] = x0[0, f, edge : edge + 1, :]
            buf[4 + f : 5 + f, :] = x0[0, f, second : second + 1, :]
            buf[8 + f : 9 + f, :] = x0[1, f, edge : edge + 1, :]
        buf[12:13, :] = wet_pad[edge : edge + 1, :]
        buf[13:14, :] = wet_pad[second : second + 1, :]
        buf[14:15, :] = mix_v[edge - ROW0 : edge - ROW0 + 1, :]
        buf[15:16, :] = rim[edge - ROW0 : edge - ROW0 + 1, :]
    up[...] = own_up[...]

    @pl.when(lat == top)
    def _():
        raw = own_up[...]
        turned = reverse_lanes(raw)
        sub16, lane16 = iota((16, cols), 0), iota((16, cols), 1)
        swapped = jnp.where(lane16 % 4 == 1, pltpu.roll(raw, cols - 1, 1), pltpu.roll(raw, 1, 1))
        turned = jnp.where(sub16 == 15, swapped, turned)
        which = jnp.where(sub16 == 15, lane16 // 4, sub16)
        turned = jnp.where((which < jnp.where(sub16 == 15, 8, 12)) & (which % 4 >= 2), -turned, turned)
        up[...] = turned

    @pl.when(lat == 0)
    def _():
        x0[:, :, ROW0 - 1, :] = jnp.zeros((levels, 4, cols), f32)
        rows_s[...] = jnp.zeros((levels, 4, cols), f32)
        for ref in (r_s, r_se, r_sw):
            ref[...] = jnp.zeros((16, cols), f32)

    pl.semaphore_wait(barrier, n_lon + n_lat + 2 - 2 * jnp.where((lat == 0) | (lat == top), 1, 0))

    def link(src, dst, send_sem, recv_sem, device):
        return pltpu.make_async_remote_copy(
            src_ref=src, dst_ref=dst, send_sem=send_sem, recv_sem=recv_sem,
            device_id=device, device_id_type=MESH,
        )

    def remote(src, dst, sem, device):
        return link(src, dst, h_send.at[sem], h_recv.at[sem], device)

    def first_link(src, dst, send_sem, recv_sem, device):
        return link(src, dst, c_send.at[send_sem], c_recv.at[recv_sem], device)

    fold_ne = lax.rem(2 * n_lon - 2 - lon, n_lon)
    fold_nw = lax.rem(n_lon - lon, n_lon)
    below_top, is_top, above_bottom = lat < top, lat == top, lat > 0
    ups = [
        (below_top, first_link(up, r_s, 0, 0, north)),
        (below_top, first_link(up, r_sw, 1, 2, (east[0], north[1]))),
        (below_top, first_link(up, r_se, 2, 1, (west[0], north[1]))),
        (is_top, first_link(up, r_n, 0, 3, mirror)),
        (is_top & (fold_ne != lon), first_link(up, r_ne, 1, 4, (fold_ne, lat))),
        (is_top & (fold_nw != lon), first_link(up, r_nw, 2, 5, (fold_nw, lat))),
    ]
    downs = [
        (above_bottom, first_link(down, r_n, 3, 3, south)),
        (above_bottom, first_link(down, r_nw, 4, 5, (east[0], south[1]))),
        (above_bottom, first_link(down, r_ne, 5, 4, (west[0], south[1]))),
    ]
    sides = [first_link(rim, rim_w, 6, 6, east), first_link(rim, rim_e, 7, 7, west)]
    for copy in sides:
        copy.start()
    for cond, copy in ups + downs:
        pl.when(cond)(copy.start)

    @pl.when(is_top & (fold_ne == lon))
    def _():
        r_ne[...] = up[...]

    @pl.when(is_top & (fold_nw == lon))
    def _():
        r_nw[...] = up[...]

    def row_copies(x, lo, sem, into_s, into_n, into_fold):
        last_row, first_row = x.at[lo:levels, :, end - 1, :], x.at[lo:levels, :, ROW0, :]
        ahead = remote(last_row, into_s, sem, north)
        over = remote(last_row, into_fold, sem + 1, mirror)
        back = remote(first_row, into_n, sem + 1, south)
        return ahead, over, back

    def start_rows(ahead, over, back):
        pl.when(lat < top)(ahead.start)
        pl.when(lat == top)(over.start)
        pl.when(lat > 0)(back.start)

    def wait_rows(ahead, over, back):
        pl.when(lat > 0)(ahead.wait_recv)
        pl.when(lat == top)(over.wait_recv)
        pl.when(lat < top)(back.wait_recv)

    def drain_rows(ahead, over, back):
        pl.when(lat < top)(ahead.wait_send)
        pl.when(lat == top)(over.wait_send)
        pl.when(lat > 0)(back.wait_send)

    def col_copies(pack, from_w, from_e, sem):
        return remote(pack, from_w, sem, east), remote(pack, from_e, sem + 1, west)

    for d in range(1, n_lat):
        pl.semaphore_signal(ready, inc=1, device_id=(lon, lax.rem(lat + d, n_lat)), device_id_type=MESH)

    for load in loads[8:]:
        load.wait()
    tiles = lax.fori_loop(2, levels, prepare, packs, unroll=2)
    for c in range(chunks):
        pack0[8 * c : 8 * c + 8, :] = tiles[c]
    halo0_rows = row_copies(
        x0, 2, 0, x0.at[2:levels, :, ROW0 - 1, :], x0.at[2:levels, :, end, :], fold0.at[2:levels]
    )
    halo0_cols = col_copies(pack0, from_w0, from_e0, 2)
    start_rows(*halo0_rows)
    for copy in halo0_cols:
        copy.start()

    loads[2].wait()
    loads[3].wait()
    blocks = rows
    pad_row = lambda ref: jnp.concatenate([ref[...].astype(f32)] * (cols // blocks), axis=1)
    own_lane = pad_row(own_v)
    row_lane = pad_row(row_v)
    sub = iota((blocks, cols), 0)
    own_col = jnp.sum(jnp.where(lane == sub, own_lane, 0.0), axis=1, keepdims=True)
    row_col = jnp.sum(jnp.where(lane == sub, row_lane + 1.0, 0.0), axis=1, keepdims=True)
    same = jnp.where((own_col == own_lane) & (sub < lax.rem(lane, blocks)), 1.0, 0.0)
    position = jnp.sum(same, axis=0, keepdims=True)
    lane1 = iota((1, cols), 1)
    target = own_lane.astype(jnp.int32) * 8 + (lane1 // blocks) * 2 + position.astype(jnp.int32)
    hot = jnp.where(iota((devices * 8, cols), 0) == target, 1.0, 0.0).astype(bf16)
    for j in range(PIECES):
        onehot[:, cols * j : cols * (j + 1)] = hot
    early = jnp.concatenate(
        [wet, jnp.broadcast_to(row_col, (blocks, cols)), jnp.zeros((2 * blocks, cols), f32)], axis=0
    )
    out_early[...] = dot(hot, early.astype(bf16)).reshape(devices, 8, cols)
    in_early[devices - 1 : devices] = out_early[pl.ds(me, 1)]

    def turning(row):
        angle = math.pi * (-0.43 + 0.93 * (row.astype(f32) + 0.5) / (n_lat * rows))
        return CORIOLIS_MAX * jnp.sin(angle)

    coriolis = turning(lat * rows + iota((rows, cols), 0))
    rim_row = jnp.where(iota((8, cols), 0) < 4, lat * rows - 1, lax.min((lat + 1) * rows, n_lat * rows - 1))
    coriolis8 = turning(rim_row)

    near = devices // 8 * 7

    def exchange(out, into, sem, height):
        for slot, (a, c) in enumerate(offsets):
            to_lon, to_lat = lax.rem(lon + a, n_lon), lax.rem(lat + c, n_lat)
            pltpu.make_async_remote_copy(
                src_ref=out.at[to_lon * n_lat + to_lat, 0:height, :], dst_ref=into.at[slot, 0:height, :],
                send_sem=a_send.at[sem], recv_sem=a_recv.at[2 * sem + slot // near],
                device_id=(to_lon, to_lat), device_id_type=MESH,
            ).start()
        parts = []
        for lo, hi, half in ((0, near, 0), (near, devices - 1, 1)):
            span = lambda ref: ref.at[lo:hi, 0:height, :]
            parts.append(pltpu.make_async_remote_copy(
                src_ref=span(out), dst_ref=span(into),
                send_sem=a_send.at[sem], recv_sem=a_recv.at[2 * sem + half],
                device_id=east, device_id_type=MESH,
            ))
        return parts

    pl.semaphore_wait(ready, n_lat - 1)
    early_all = exchange(out_early, in_early, 0, 4)

    for copy in sides:
        copy.wait_recv()
    arrivals = [
        (above_bottom, ups[0]), (above_bottom, ups[1]), (above_bottom, ups[2]),
        (below_top, downs[0]), (below_top, downs[1]), (below_top, downs[2]), (is_top, ups[3]),
        (is_top & (fold_ne != lon), ups[4]), (is_top & (fold_nw != lon), ups[5]),
    ]
    for cond, (_, copy) in arrivals:
        pl.when(cond)(copy.wait_recv)

    centre = 1.0 - 2.0 * TIMESTEP * VERTICAL_MIX
    vertical = TIMESTEP * VERTICAL_MIX

    def surface_step(q, e, w, n, s, below, wets, rate, turn, u, v, field, gx, gy):
        we, ww, wn, ws, wc = wets
        dx, dy = e - w, n - s
        extra = jnp.where(
            field == 2, TIMESTEP * turn * v - (0.25 * TIMESTEP * GRAVITY) * gx(dx),
            jnp.where(field == 3, -TIMESTEP * turn * u - (0.25 * TIMESTEP * GRAVITY) * gy(dy), 0.0),
        )
        spread = (we * e + ww * w) + (wn * n + ws * s)
        return wc * (
            q * (centre - rate * (we + ww + wn + ws)) + vertical * (q + below) + rate * spread
            - (0.5 * TIMESTEP) * (u * dx + v * dy) + extra
        )

    two = lambda a, b: jnp.concatenate([a, b], axis=0)
    four = lambda a, b: two(jnp.broadcast_to(a, (4, cols)), jnp.broadcast_to(b, (4, cols)))
    from_right = lambda x, corner: pltpu.roll(jnp.where(first, corner, x), cols - 1, 1)
    from_left = lambda x, corner: pltpu.roll(jnp.where(last, corner, x), 1, 1)
    both = lambda a, b, lo: two(a[lo : lo + 4, :], b[lo : lo + 4, :])
    line = lambda a, b, i: four(a[i : i + 1, :], b[i : i + 1, :])
    q8 = both(r_s, r_n, 0)
    wet8 = line(r_s, r_n, 12)
    field8 = iota((8, cols), 0) % 4
    of = lambda x, i: four(x[i : i + 1], x[4 + i : 5 + i])
    slope = lambda d: HALINE * of(d, 1) - THERMAL * of(d, 0)
    rows_new = surface_step(
        q8, from_right(q8, both(r_se, r_ne, 0)), from_left(q8, both(r_sw, r_nw, 0)),
        two(down[0:4, :], r_n[4:8, :]), two(r_s[4:8, :], own_up[0:4, :]), both(r_s, r_n, 8),
        (
            from_right(wet8, line(r_se, r_ne, 12)), from_left(wet8, line(r_sw, r_nw, 12)),
            four(down[12:13, :], r_n[13:14, :]), four(r_s[13:14, :], own_up[12:13, :]), wet8,
        ),
        jnp.where(field8 < 2, TIMESTEP * line(r_s, r_n, 14), TIMESTEP * VISCOSITY),
        coriolis8, of(q8, 2), of(q8, 3), field8, slope, slope,
    )
    for f in range(4):
        x1[0, f, ROW0 - 1 : ROW0, :] = rows_new[f : f + 1]
        x1[0, f, end : end + 1, :] = rows_new[4 + f : 5 + f]
        for k in range(2):
            x0[k, f, ROW0 - 1 : ROW0, :] = r_s[8 * k + f : 8 * k + f + 1, :]
            x0[k, f, end : end + 1, :] = r_n[8 * k + f : 8 * k + f + 1, :]
    wet_pad[ROW0 - 1 : ROW0, :] = r_s[12:13, :]
    wet_pad[end : end + 1, :] = r_n[12:13, :]

    low = lane % 4 < 2
    halves = lambda a, b: jnp.where(iota(a.shape, 1) < cols // 2, a, pltpu.roll(b, cols // 2 - 1, 1))
    own_rim, east_rim, west_rim = rim[...], rim_e[...], rim_w[...]
    strip = halves(jnp.where(low, west_rim, own_rim), jnp.where(low, own_rim, east_rim))
    rim_pad[ROW0:end, :] = strip
    wide = lambda ref: jnp.broadcast_to(ref[15:16, :], (8, cols))
    rim_pad[ROW0 - 1 : ROW0, :] = halves(wide(r_sw), wide(r_se))[0:1]
    rim_pad[end : end + 1, :] = halves(wide(r_nw), wide(r_ne))[0:1]
    strip_n = rim_pad[ROW0 + 1 : end + 1, :]
    strip_s = rim_pad[ROW0 - 1 : end - 1, :]
    right = lambda x, d: pltpu.roll(x, (d + cols) % cols, 1)
    wets = [right(x, -32) for x in (strip_n, strip_s, strip)]
    field = group % 16

    def spread_field(i):
        out = strip
        for f in range(4):
            if f != i:
                out = jnp.where(field == f, right(strip, 4 * (f - i)), out)
        return out

    rim_new[...] = surface_step(
        strip, right(strip, -1), right(strip, 1), strip_n, strip_s, right(strip, -16),
        (right(wets[2], -1), right(wets[2], 1), wets[0], wets[1], wets[2]),
        right(strip, -48), coriolis, spread_field(2), spread_field(3), field,
        lambda d: HALINE * right(d, 4) - THERMAL * right(d, 8),
        lambda d: HALINE * right(d, 8) - THERMAL * right(d, 12),
    )

    at = lambda x, src, dst: pltpu.roll(x, (dst - src + cols) % cols, 1)
    w_east = pltpu.roll(jnp.where(lane == 0, at(east_rim, 34, 0), wet), cols - 1, 1)
    w_west = pltpu.roll(jnp.where(lane == cols - 1, at(west_rim, 33, cols - 1), wet), 1, 1)
    w_north = wet_pad[ROW0 + 1 : end + 1, :]
    w_south = wet_pad[ROW0 - 1 : end - 1, :]
    total = w_east + w_west + w_north + w_south
    for base, rate in ((0, rate_t), (5, TIMESTEP * VISCOSITY)):
        coef[base] = wet * (centre - rate * total)
        for j, w in enumerate((w_east, w_west, w_north, w_south)):
            coef[base + 1 + j] = wet * (rate * w)
    coef[10] = vertical * wet
    coef[11] = TIMESTEP * coriolis * wet

    pressure_rate = 0.5 * TIMESTEP * GRAVITY
    assert abs(pressure_rate - TIMESTEP * VERTICAL_MIX) < 1e-12

    def level(x, k, side_of, carry, store):
        above = lax.max(k - 1, 0) if not isinstance(k, int) else max(k - 1, 0)
        below = lax.min(k + 1, levels - 1) if not isinstance(k, int) else min(k + 1, levels - 1)
        carry = list(carry)
        for c in range(chunks):
            mid = part(c)
            ahead = slice(ROW0 + 8 * c + 1, ROW0 + 8 * c + 9)
            behind = slice(ROW0 + 8 * c - 1, ROW0 + 8 * c + 7)
            own = slice(8 * c, 8 * c + 8)
            q, e, w, n, s = [], [], [], [], []
            for f in range(4):
                value = x[k, f, mid, :]
                side = side_of(own, k, f)
                q.append(value)
                e.append(pltpu.roll(jnp.where(first, side, value), cols - 1, 1))
                w.append(pltpu.roll(jnp.where(last, side, value), 1, 1))
                n.append(x[k, f, ahead, :])
                s.append(x[k, f, behind, :])
            gx = HALINE * (e[1] - w[1]) - THERMAL * (e[0] - w[0])
            gy = HALINE * (n[1] - s[1]) - THERMAL * (n[0] - s[0])
            sx = carry[2 * c] + gx
            sy = carry[2 * c + 1] + gy
            carry[2 * c], carry[2 * c + 1] = sx, sy
            push = (None, None, sx - 0.5 * gx, sy - 0.5 * gy)
            u = (0.5 * TIMESTEP) * q[2]
            v = (0.5 * TIMESTEP) * q[3]
            vert = coef[10, own, :]
            turn = coef[11, own, :]
            for f in range(4):
                if f % 2 == 0:
                    base = 0 if f == 0 else 5
                    a = coef[base, own, :]
                    ce = coef[base + 1, own, :] - u
                    cw = coef[base + 2, own, :] + u
                    cn = coef[base + 3, own, :] - v
                    cs = coef[base + 4, own, :] + v
                column = x[above, f, mid, :] + x[below, f, mid, :]
                if f >= 2:
                    column = column - push[f]
                value = (a * q[f] + vert * column) + (ce * e[f] + cw * w[f]) + (cn * n[f] + cs * s[f])
                if f == 2:
                    value = value + turn * q[3]
                if f == 3:
                    value = value - turn * q[2]
                store(k, f, c, value)
        return tuple(carry)

    def merge(edge, from_e, from_w):
        edge[...] = jnp.where(lax.rem(lane, 2) == 0, from_e[...], from_w[...])

    def unfold(fold, lo, hi, put):
        @pl.when(lat == top)
        def _():
            for k in range(lo, hi, 2):
                width = min(2, hi - k)
                pair = fold[k : k + width].reshape(4 * width, cols)
                pair = reverse_lanes(pair)
                field = lax.rem(iota(pair.shape, 0), 4)
                pair = jnp.where(field < 2, pair, -pair)
                put(k, width, pair)

    def packed_side(edge):
        return lambda own, k, f: pltpu.roll(edge[own, :], lax.rem(2 * cols - 2 * (4 * k + f), cols), 1)

    def rim_side(from_east, lane_e, from_west, lane_w):
        def side(own, k, f):
            i = 4 * (4 * k + f)
            east_value = at(from_east[own, :], lane_e + i, 0)
            return jnp.where(first, east_value, at(from_west[own, :], lane_w + i, cols - 1))

        return side

    zeros = tuple(jnp.zeros((8, cols), f32) for _ in range(2 * chunks))

    def step1(k, side_of, carry, tiles):
        tiles = list(tiles)

        def store(k, f, c, value):
            x1[k, f, part(c), :] = value
            if tiles:
                tiles[c] = packed(tiles[c], value, 4 * k + f)

        carry = level(x0, k, side_of, carry, store)
        return carry, tuple(tiles)

    near_side = rim_side(rim_e, 2, rim_w, 1)
    carry1, _ = step1(0, near_side, zeros, ())
    carry1, tiles = step1(1, near_side, carry1, empty)

    def store2(k, f, c, value):
        x2[k, f, 8 * c : 8 * c + 8, :] = value

    carry2 = level(x1, 0, rim_side(rim_new, 65, rim_new, 1), zeros, store2)
    surf = x2[0].reshape(4 * rows, cols)
    late = dot(onehot[...], jnp.concatenate(split(surf), axis=0))
    out_late[...] = late.reshape(devices, 8, cols)
    in_late[devices - 1 : devices] = out_late[pl.ds(me, 1)]
    late_all = exchange(out_late, in_late, 1, 8)

    for copy in halo0_cols:
        copy.wait_recv()
    wait_rows(*halo0_rows)
    merge(edge0, from_e0, from_w0)

    def put_rows(k, width, pair):
        for j in range(width):
            for f in range(4):
                x0[k + j, f, end : end + 1, :] = pair[4 * j + f : 4 * j + f + 1]

    unfold(fold0, 2, levels, put_rows)
    _, tiles = lax.fori_loop(
        2, levels, lambda k, s: step1(k, packed_side(edge0), *s), (carry1, tiles), unroll=UNROLL1
    )
    for c in range(chunks):
        pack1b[8 * c : 8 * c + 8, :] = tiles[c]
    halo2_rows = row_copies(
        x1, 1, 4, rows_s.at[1:levels], rows_n.at[1:levels], rows_n.at[1:levels]
    )
    halo2_cols = col_copies(pack1b, from_wb, from_eb, 6)
    start_rows(*halo2_rows)
    for copy in halo2_cols:
        copy.start()

    nothing = jnp.zeros((8, cols), f32)
    lax.fori_loop(
        1, levels, lambda k, s: level(x1, k, lambda own, k, f: nothing, s, store2), carry2, unroll=UNROLL2
    )

    for copy in early_all:
        copy.wait_recv()
    tile = (cols // 8, 8, cols)
    sub3 = iota(tile, 1)
    lane3 = iota(tile, 2)
    keep = (sub3 // 2) == (lane3 // ATM_ROWS)
    wanted = (lax.rem(lane3, ATM_ROWS) + 1).astype(f32)
    for j in range(devices * 8 // cols):
        got = in_early[tile[0] * j : tile[0] * (j + 1)]
        ids = jnp.where((sub3 // 2) == 1, got, 0.0)
        ids = (ids + pltpu.roll(ids, 2, 1)) + (pltpu.roll(ids, 4, 1) + pltpu.roll(ids, 6, 1))
        hit = jnp.where(keep & (ids == wanted), 1.0, 0.0)
        row_hot[:, cols * j : cols * (j + 1)] = hit.reshape(cols, cols).T.astype(bf16)
    wets = jnp.where(iota((devices, 8, cols), 1) < 2, in_early[...], 0.0)
    cover = dot(row_hot[0:ATM_ROWS, :], wets.reshape(devices * 8, cols).astype(bf16))
    cover_v[...] = cover
    share = 1.0 / jnp.maximum(cover, 1.0)

    for copy in halo2_cols:
        copy.wait_recv()
    wait_rows(*halo2_rows)
    edge2b[...] = jnp.where(
        lax.rem(lane, 2) == 0, pltpu.roll(from_wb[...], 1, 1), pltpu.roll(from_eb[...], cols - 1, 1)
    )

    def put_back(k, width, pair):
        rows_n[k : k + width] = pair.reshape(width, 4, cols)

    unfold(rows_n, 1, levels, put_back)

    def halo_share(k, carry):
        carry = list(carry)
        for c in range(chunks):
            own, mid = slice(8 * c, 8 * c + 8), part(c)
            u = (0.5 * TIMESTEP) * x1[k, 2, mid, :]
            v = (0.5 * TIMESTEP) * x1[k, 3, mid, :]
            vert = coef[10, own, :]
            side = edge2b[own, :]
            halo = [pltpu.roll(side, lax.rem(2 * cols - 2 * (4 * k + f), cols), 1) for f in range(4)]
            gx = HALINE * halo[1] - THERMAL * halo[0]
            gx = jnp.where(last, gx, jnp.where(first, -gx, 0.0))
            carry[c] = carry[c] + gx
            add = []
            for f in range(4):
                base = 0 if f < 2 else 5
                rate = jnp.where(
                    last, coef[base + 1, own, :] - u, jnp.where(first, coef[base + 2, own, :] + u, 0.0)
                )
                add.append(rate * halo[f])
            add[2] = add[2] - vert * (carry[c] - 0.5 * gx)
            for outside, rows_of, edge, index, sign in (
                (c == 0, rows_s, 0, 4, 1.0), (c == chunks - 1, rows_n, 7, 3, -1.0)
            ):
                if outside:
                    here = iota((8, cols), 0) == edge
                    line_of = [
                        jnp.where(here, jnp.broadcast_to(rows_of[k, f : f + 1, :], (8, cols)), 0.0)
                        for f in range(4)
                    ]
                    gy = -sign * (HALINE * line_of[1] - THERMAL * line_of[0])
                    slot = chunks + (0 if c == 0 else 1)
                    carry[slot] = carry[slot] + gy
                    for f in range(4):
                        base = 0 if f < 2 else 5
                        add[f] = add[f] + (coef[base + index, own, :] + sign * v) * line_of[f]
                    add[3] = add[3] - vert * (carry[slot] - 0.5 * gy)
            for f in range(4):
                x2[k, f, own, :] = x2[k, f, own, :] + add[f]
        return tuple(carry)

    lax.fori_loop(1, levels, halo_share, (nothing,) * (chunks + 2), unroll=UNROLL2)
    sums = jnp.zeros((4 * ATM_ROWS, cols), f32)
    for half, copy in enumerate(late_all):
        copy.wait_recv()
        lo, hi = ((0, near), (near, devices))[half]
        got = in_late[lo:hi].reshape((hi - lo) * 8, cols)
        placed = row_hot[:, 8 * lo : 8 * hi]
        for piece in split(got):
            sums = sums + dot(placed, piece)
    surf_v[...] = sums.reshape(4, ATM_ROWS, cols) * share

    for cond, copy in ups + downs:
        pl.when(cond)(copy.wait_send)
    drain_rows(*halo0_rows)
    drain_rows(*halo2_rows)
    for copy in [*sides, *halo0_cols, *halo2_cols]:
        copy.wait_send()
    whole = lambda ref, height: ref.at[0 : devices - 1, 0:height, :]
    for sem, (out, into, height) in enumerate(((out_early, in_early, 4), (out_late, in_late, 8))):
        pltpu.make_async_remote_copy(
            src_ref=whole(out, height), dst_ref=whole(into, height),
            send_sem=a_send.at[sem], recv_sem=a_recv.at[2 * sem], device_id=east, device_id_type=MESH,
        ).wait_send()


def write_out(x2, surf_v, cover_v, tracers_out, velocity_out, surface_out, cover_out, sem):
    stores = []
    for f in range(4):
        dst = (tracers_out if f < 2 else velocity_out).at[f % 2]
        stores.append(pltpu.make_async_copy(x2.at[:, f], dst, sem.at[f]))
    stores.append(pltpu.make_async_copy(cover_v, cover_out, sem.at[4]))
    stores.append(pltpu.make_async_copy(surf_v, surface_out, sem.at[5]))
    for store in stores:
        store.start()
    for store in stores:
        store.wait()


def local(tracers, velocity, land_mask, mixing, owners, atm_row):
    n_lon, n_lat = lax.axis_size("lon"), lax.axis_size("lat")
    levels = tracers.shape[1]
    rows, cols = land_mask.shape
    devices = n_lon * n_lat
    blocks = rows * cols // 128
    assert cols == 128 and blocks == rows and ATM_ROWS == 32
    any_spec = pl.BlockSpec(memory_space=pl.ANY)
    vmem = lambda *shape: pltpu.VMEM(shape, f32)
    tile = vmem(rows, cols)
    padded = rows + 16
    scratch = (
        [vmem(levels, 4, padded, cols)] * 2
        + [vmem(padded, cols)]
        + [pltpu.VMEM((rows, cols), jnp.int32), tile]
        + [pltpu.VMEM((1, blocks), jnp.int32)] * 2
        + [tile] * 12
        + [vmem(padded, cols)]
        + [vmem(levels, 4, cols)] * 3
        + [vmem(16, cols)] * 9
        + [vmem(12, rows, cols), pltpu.VMEM((devices * 8, PIECES * cols), bf16)]
        + [vmem(devices, 8, cols)] * 4
        + [pltpu.VMEM((4 * ATM_ROWS, devices * 8), bf16)]
        + [pltpu.SemaphoreType.DMA((12,))]
        + [pltpu.SemaphoreType.DMA((8,))] * 4
        + [pltpu.SemaphoreType.DMA((2,)), pltpu.SemaphoreType.DMA((4,))]
        + [pltpu.SemaphoreType.REGULAR]
    )
    ring = lambda d, size: min(d % size, size - d % size)
    half_lat = n_lat // 2
    hops = lambda a, c: ring(a, n_lon // 2) + ring(c // 2, half_lat // 2) + 2 * (a // (n_lon // 2)) + c // half_lat
    offsets = [(a, c) for a in range(n_lon) for c in range(n_lat) if a or c]
    offsets.sort(key=lambda o: hops(*o))
    held = pl.pallas_call(
        functools.partial(kernel, n_lon, n_lat, levels, rows, cols, offsets),
        out_shape=(vmem(levels, 4, rows, cols), vmem(4, ATM_ROWS, cols), vmem(ATM_ROWS, cols)),
        in_specs=[any_spec] * 6,
        scratch_shapes=scratch,
        compiler_params=pltpu.CompilerParams(collective_id=0, has_side_effects=True),
        name="ocean",
    )(tracers, velocity, land_mask, mixing, owners.reshape(1, blocks), atm_row.reshape(1, blocks))
    return pl.pallas_call(
        write_out,
        out_shape=(
            jax.ShapeDtypeStruct(tracers.shape, f32),
            jax.ShapeDtypeStruct(velocity.shape, f32),
            jax.ShapeDtypeStruct((4, ATM_ROWS, cols), f32),
            jax.ShapeDtypeStruct((ATM_ROWS, cols), f32),
        ),
        in_specs=[pl.BlockSpec(memory_space=pltpu.VMEM)] * 3,
        out_specs=(any_spec,) * 4,
        scratch_shapes=[pltpu.SemaphoreType.DMA((6,))],
        name="write_out",
    )(*(pltpu.with_memory_space_constraint(x, pltpu.VMEM) for x in held))


def solution(mesh):
    in_specs = (
        P(None, None, "lat", "lon"),
        P(None, None, "lat", "lon"),
        P("lat", "lon"),
        P("lat", "lon"),
        P(("lon", "lat"), None),
        P(("lon", "lat")),
    )
    out_specs = (
        P(None, None, "lat", "lon"),
        P(None, None, "lat", "lon"),
        P(None, ("lon", "lat"), None),
        P(("lon", "lat"), None),
    )
    return jax.shard_map(local, mesh=mesh, in_specs=in_specs, out_specs=out_specs, check_vma=False)
```

```python
import functools
import math

import jax
import jax.numpy as jnp
from jax import lax
from jax.experimental import pallas as pl
from jax.experimental.pallas import tpu as pltpu
from jax.sharding import PartitionSpec as P

THERMAL = 0.2
HALINE = 0.15
GRAVITY = 0.2
TIMESTEP = 0.8
VERTICAL_MIX = 0.1
VISCOSITY = 0.2
CORIOLIS_MAX = 0.3
ATM_ROWS = 32
UNROLL1, UNROLL2 = 2, 3
PIECES = 3

MESH = pl.DeviceIdType.MESH
ROW0 = 8
f32 = jnp.float32
bf16 = jnp.bfloat16


def iota(shape, dim):
    return lax.broadcasted_iota(jnp.int32, shape, dim)


def split(x):
    hi = x.astype(bf16)
    rest = x - hi.astype(f32)
    mid = rest.astype(bf16)
    lo = (rest - mid.astype(f32)).astype(bf16)
    return hi, mid, lo


def dot(a, b):
    return lax.dot_general(a, b, (((1,), (0,)), ((), ())), preferred_element_type=f32)


def reverse_lanes(x):
    lane = iota(x.shape, x.ndim - 1)
    size = x.shape[-1]
    step = size // 2
    while step:
        x = jnp.where(
            (lane & step) == 0,
            pltpu.roll(x, size - step, x.ndim - 1),
            pltpu.roll(x, step, x.ndim - 1),
        )
        step //= 2
    return x


def kernel(
    n_lon, n_lat, levels, rows, cols, offsets,
    tracers, velocity, land_mask, mixing, owners, atm_row,
    x2, surf_v, cover_v,
    x0, x1, wet_pad, mask_i, mix_v, own_v, row_v,
    pack0, pack1b, from_e0, from_w0, from_eb, from_wb, edge0, edge2b, rim, rim_e, rim_w, rim_new,
    rim_pad, fold0, rows_s, rows_n, own_up, up, down, r_s, r_se, r_sw, r_n, r_ne, r_nw,
    coef, onehot, out_early, in_early, out_late, in_late, row_hot,
    in_sem, c_send, c_recv, h_send, h_recv, a_send, a_recv, ready,
):
    devices = n_lon * n_lat
    lon = lax.axis_index("lon")
    lat = lax.axis_index("lat")
    me = lon * n_lat + lat
    top = n_lat - 1
    east = (lax.rem(lon + 1, n_lon), lat)
    west = (lax.rem(lon + n_lon - 1, n_lon), lat)
    north = (lon, lax.min(lat + 1, top))
    south = (lon, lax.max(lat - 1, 0))
    mirror = (n_lon - 1 - lon, lat)
    end = ROW0 + rows
    chunks = rows // 8

    loads = [
        pltpu.make_async_copy(land_mask, mask_i, in_sem.at[0]),
        pltpu.make_async_copy(mixing, mix_v, in_sem.at[1]),
        pltpu.make_async_copy(owners, own_v, in_sem.at[2]),
        pltpu.make_async_copy(atm_row, row_v, in_sem.at[3]),
    ]
    for lo, hi, sem in ((0, 2, 4), (2, levels, 8)):
        for f in range(4):
            src = (tracers if f < 2 else velocity).at[f % 2, lo:hi]
            loads.append(pltpu.make_async_copy(src, x0.at[lo:hi, f, ROW0:end, :], in_sem.at[sem + f]))
    for load in loads:
        load.start()

    barrier = pltpu.get_barrier_semaphore()
    for d in range(1, n_lon):
        pl.semaphore_signal(barrier, inc=1, device_id=(lax.rem(lon + d, n_lon), lat), device_id_type=MESH)
    for d in range(1, n_lat):
        pl.semaphore_signal(barrier, inc=1, device_id=(lon, lax.rem(lat + d, n_lat)), device_id_type=MESH)

    lat_n, lat_s = lax.rem(lat + 1, n_lat), lax.rem(lat + top, n_lat)
    for lon_to in (east[0], west[0]):
        for has, lat_to in ((lat < top, lat_n), (lat > 0, lat_s)):

            @pl.when(has)
            def _():
                pl.semaphore_signal(barrier, inc=1, device_id=(lon_to, lat_to), device_id_type=MESH)

    lane8 = iota((8, cols), 1)
    lane = iota((rows, cols), 1)
    first = lane8 == 0
    last = lane8 == cols - 1

    def part(c):
        return slice(ROW0 + 8 * c, ROW0 + 8 * c + 8)

    def packed(tile, value, i):
        where = (lane8 == 2 * i) | (lane8 == lax.rem(2 * i + cols - 1, cols))
        return jnp.where(where, pltpu.roll(value, 2 * i, 1), tile)

    for row in (ROW0 - 1, end):
        x1[:, :, row, :] = jnp.zeros((levels, 4, cols), f32)

    loads[0].wait()
    wet = mask_i[...].astype(f32)
    wet_pad[ROW0:end, :] = wet
    for load in loads[4:8]:
        load.wait()

    def prepare(k, tiles):
        tiles = list(tiles)
        for f in range(4):
            for c in range(chunks):
                q = x0[k, f, part(c), :] * wet_pad[part(c), :]
                x0[k, f, part(c), :] = q
                tiles[c] = packed(tiles[c], q, 4 * k + f)
        return tuple(tiles)

    empty = tuple(jnp.zeros((8, cols), f32) for _ in range(chunks))
    packs = prepare(1, prepare(0, empty))

    loads[1].wait()
    rate_t = TIMESTEP * mix_v[...]
    rate_v = jnp.full((rows, cols), TIMESTEP * VISCOSITY, f32)
    group = lane // 4
    packed_rim = jnp.zeros((rows, cols), f32)
    quantities = [x0[k, f, ROW0:end, :] for k in range(2) for f in range(4)]
    quantities += [wet] * 4 + [rate_t, rate_t, rate_v, rate_v]
    for i, value in enumerate(quantities):
        packed_rim = jnp.where(group == i, pltpu.roll(value, 4 * i + 2, 1), packed_rim)
    rim[...] = packed_rim
    for buf, edge, second in ((own_up, end - 1, end - 2), (down, ROW0, ROW0 + 1)):
        for f in range(4):
            buf[f : f + 1, :] = x0[0, f, edge : edge + 1, :]
            buf[4 + f : 5 + f, :] = x0[0, f, second : second + 1, :]
            buf[8 + f : 9 + f, :] = x0[1, f, edge : edge + 1, :]
        buf[12:13, :] = wet_pad[edge : edge + 1, :]
        buf[13:14, :] = wet_pad[second : second + 1, :]
        buf[14:15, :] = mix_v[edge - ROW0 : edge - ROW0 + 1, :]
        buf[15:16, :] = rim[edge - ROW0 : edge - ROW0 + 1, :]
    up[...] = own_up[...]

    @pl.when(lat == top)
    def _():
        raw = own_up[...]
        turned = reverse_lanes(raw)
        sub16, lane16 = iota((16, cols), 0), iota((16, cols), 1)
        swapped = jnp.where(lane16 % 4 == 1, pltpu.roll(raw, cols - 1, 1), pltpu.roll(raw, 1, 1))
        turned = jnp.where(sub16 == 15, swapped, turned)
        which = jnp.where(sub16 == 15, lane16 // 4, sub16)
        turned = jnp.where((which < jnp.where(sub16 == 15, 8, 12)) & (which % 4 >= 2), -turned, turned)
        up[...] = turned

    @pl.when(lat == 0)
    def _():
        x0[:, :, ROW0 - 1, :] = jnp.zeros((levels, 4, cols), f32)
        rows_s[...] = jnp.zeros((levels, 4, cols), f32)
        for ref in (r_s, r_se, r_sw):
            ref[...] = jnp.zeros((16, cols), f32)

    pl.semaphore_wait(barrier, n_lon + n_lat + 2 - 2 * jnp.where((lat == 0) | (lat == top), 1, 0))

    def link(src, dst, send_sem, recv_sem, device):
        return pltpu.make_async_remote_copy(
            src_ref=src, dst_ref=dst, send_sem=send_sem, recv_sem=recv_sem,
            device_id=device, device_id_type=MESH,
        )

    def remote(src, dst, sem, device):
        return link(src, dst, h_send.at[sem], h_recv.at[sem], device)

    def first_link(src, dst, send_sem, recv_sem, device):
        return link(src, dst, c_send.at[send_sem], c_recv.at[recv_sem], device)

    fold_ne = lax.rem(2 * n_lon - 2 - lon, n_lon)
    fold_nw = lax.rem(n_lon - lon, n_lon)
    below_top, is_top, above_bottom = lat < top, lat == top, lat > 0
    ups = [
        (below_top, first_link(up, r_s, 0, 0, north)),
        (below_top, first_link(up, r_sw, 1, 2, (east[0], north[1]))),
        (below_top, first_link(up, r_se, 2, 1, (west[0], north[1]))),
        (is_top, first_link(up, r_n, 0, 3, mirror)),
        (is_top & (fold_ne != lon), first_link(up, r_ne, 1, 4, (fold_ne, lat))),
        (is_top & (fold_nw != lon), first_link(up, r_nw, 2, 5, (fold_nw, lat))),
    ]
    downs = [
        (above_bottom, first_link(down, r_n, 3, 3, south)),
        (above_bottom, first_link(down, r_nw, 4, 5, (east[0], south[1]))),
        (above_bottom, first_link(down, r_ne, 5, 4, (west[0], south[1]))),
    ]
    sides = [first_link(rim, rim_w, 6, 6, east), first_link(rim, rim_e, 7, 7, west)]
    for copy in sides:
        copy.start()
    for cond, copy in ups + downs:
        pl.when(cond)(copy.start)

    @pl.when(is_top & (fold_ne == lon))
    def _():
        r_ne[...] = up[...]

    @pl.when(is_top & (fold_nw == lon))
    def _():
        r_nw[...] = up[...]

    def row_copies(x, lo, sem, into_s, into_n, into_fold):
        last_row, first_row = x.at[lo:levels, :, end - 1, :], x.at[lo:levels, :, ROW0, :]
        ahead = remote(last_row, into_s, sem, north)
        over = remote(last_row, into_fold, sem + 1, mirror)
        back = remote(first_row, into_n, sem + 1, south)
        return ahead, over, back

    def start_rows(ahead, over, back):
        pl.when(lat < top)(ahead.start)
        pl.when(lat == top)(over.start)
        pl.when(lat > 0)(back.start)

    def wait_rows(ahead, over, back):
        pl.when(lat > 0)(ahead.wait_recv)
        pl.when(lat == top)(over.wait_recv)
        pl.when(lat < top)(back.wait_recv)

    def drain_rows(ahead, over, back):
        pl.when(lat < top)(ahead.wait_send)
        pl.when(lat == top)(over.wait_send)
        pl.when(lat > 0)(back.wait_send)

    def col_copies(pack, from_w, from_e, sem):
        return remote(pack, from_w, sem, east), remote(pack, from_e, sem + 1, west)

    for d in range(1, n_lat):
        pl.semaphore_signal(ready, inc=1, device_id=(lon, lax.rem(lat + d, n_lat)), device_id_type=MESH)

    for load in loads[8:]:
        load.wait()
    tiles = lax.fori_loop(2, levels, prepare, packs, unroll=2)
    for c in range(chunks):
        pack0[8 * c : 8 * c + 8, :] = tiles[c]
    halo0_rows = row_copies(
        x0, 2, 0, x0.at[2:levels, :, ROW0 - 1, :], x0.at[2:levels, :, end, :], fold0.at[2:levels]
    )
    halo0_cols = col_copies(pack0, from_w0, from_e0, 2)
    start_rows(*halo0_rows)
    for copy in halo0_cols:
        copy.start()

    loads[2].wait()
    loads[3].wait()
    blocks = rows
    pad_row = lambda ref: jnp.concatenate([ref[...].astype(f32)] * (cols // blocks), axis=1)
    own_lane = pad_row(own_v)
    row_lane = pad_row(row_v)
    sub = iota((blocks, cols), 0)
    own_col = jnp.sum(jnp.where(lane == sub, own_lane, 0.0), axis=1, keepdims=True)
    row_col = jnp.sum(jnp.where(lane == sub, row_lane + 1.0, 0.0), axis=1, keepdims=True)
    same = jnp.where((own_col == own_lane) & (sub < lax.rem(lane, blocks)), 1.0, 0.0)
    position = jnp.sum(same, axis=0, keepdims=True)
    lane1 = iota((1, cols), 1)
    target = own_lane.astype(jnp.int32) * 8 + (lane1 // blocks) * 2 + position.astype(jnp.int32)
    hot = jnp.where(iota((devices * 8, cols), 0) == target, 1.0, 0.0).astype(bf16)
    for j in range(PIECES):
        onehot[:, cols * j : cols * (j + 1)] = hot
    early = jnp.concatenate(
        [wet, jnp.broadcast_to(row_col, (blocks, cols)), jnp.zeros((2 * blocks, cols), f32)], axis=0
    )
    out_early[...] = dot(hot, early.astype(bf16)).reshape(devices, 8, cols)
    in_early[devices - 1 : devices] = out_early[pl.ds(me, 1)]

    def turning(row):
        angle = math.pi * (-0.43 + 0.93 * (row.astype(f32) + 0.5) / (n_lat * rows))
        return CORIOLIS_MAX * jnp.sin(angle)

    coriolis = turning(lat * rows + iota((rows, cols), 0))
    rim_row = jnp.where(iota((8, cols), 0) < 4, lat * rows - 1, lax.min((lat + 1) * rows, n_lat * rows - 1))
    coriolis8 = turning(rim_row)

    near = devices // 16 * 15

    def exchange(out, into, sem, height):
        for slot, (a, c) in enumerate(offsets):
            to_lon, to_lat = lax.rem(lon + a, n_lon), lax.rem(lat + c, n_lat)
            pltpu.make_async_remote_copy(
                src_ref=out.at[to_lon * n_lat + to_lat, 0:height, :], dst_ref=into.at[slot, 0:height, :],
                send_sem=a_send.at[sem], recv_sem=a_recv.at[2 * sem + slot // near],
                device_id=(to_lon, to_lat), device_id_type=MESH,
            ).start()
        parts = []
        for lo, hi, half in ((0, near, 0), (near, devices - 1, 1)):
            span = lambda ref: ref.at[lo:hi, 0:height, :]
            parts.append(pltpu.make_async_remote_copy(
                src_ref=span(out), dst_ref=span(into),
                send_sem=a_send.at[sem], recv_sem=a_recv.at[2 * sem + half],
                device_id=east, device_id_type=MESH,
            ))
        return parts

    pl.semaphore_wait(ready, n_lat - 1)
    early_all = exchange(out_early, in_early, 0, 4)

    for copy in sides:
        copy.wait_recv()
    arrivals = [
        (above_bottom, ups[0]), (above_bottom, ups[1]), (above_bottom, ups[2]),
        (below_top, downs[0]), (below_top, downs[1]), (below_top, downs[2]), (is_top, ups[3]),
        (is_top & (fold_ne != lon), ups[4]), (is_top & (fold_nw != lon), ups[5]),
    ]
    for cond, (_, copy) in arrivals:
        pl.when(cond)(copy.wait_recv)

    centre = 1.0 - 2.0 * TIMESTEP * VERTICAL_MIX
    vertical = TIMESTEP * VERTICAL_MIX

    def surface_step(q, e, w, n, s, below, wets, rate, turn, u, v, field, gx, gy):
        we, ww, wn, ws, wc = wets
        dx, dy = e - w, n - s
        extra = jnp.where(
            field == 2, TIMESTEP * turn * v - (0.25 * TIMESTEP * GRAVITY) * gx(dx),
            jnp.where(field == 3, -TIMESTEP * turn * u - (0.25 * TIMESTEP * GRAVITY) * gy(dy), 0.0),
        )
        spread = (we * e + ww * w) + (wn * n + ws * s)
        return wc * (
            q * (centre - rate * (we + ww + wn + ws)) + vertical * (q + below) + rate * spread
            - (0.5 * TIMESTEP) * (u * dx + v * dy) + extra
        )

    two = lambda a, b: jnp.concatenate([a, b], axis=0)
    four = lambda a, b: two(jnp.broadcast_to(a, (4, cols)), jnp.broadcast_to(b, (4, cols)))
    from_right = lambda x, corner: pltpu.roll(jnp.where(first, corner, x), cols - 1, 1)
    from_left = lambda x, corner: pltpu.roll(jnp.where(last, corner, x), 1, 1)
    both = lambda a, b, lo: two(a[lo : lo + 4, :], b[lo : lo + 4, :])
    line = lambda a, b, i: four(a[i : i + 1, :], b[i : i + 1, :])
    q8 = both(r_s, r_n, 0)
    wet8 = line(r_s, r_n, 12)
    field8 = iota((8, cols), 0) % 4
    of = lambda x, i: four(x[i : i + 1], x[4 + i : 5 + i])
    slope = lambda d: HALINE * of(d, 1) - THERMAL * of(d, 0)
    rows_new = surface_step(
        q8, from_right(q8, both(r_se, r_ne, 0)), from_left(q8, both(r_sw, r_nw, 0)),
        two(down[0:4, :], r_n[4:8, :]), two(r_s[4:8, :], own_up[0:4, :]), both(r_s, r_n, 8),
        (
            from_right(wet8, line(r_se, r_ne, 12)), from_left(wet8, line(r_sw, r_nw, 12)),
            four(down[12:13, :], r_n[13:14, :]), four(r_s[13:14, :], own_up[12:13, :]), wet8,
        ),
        jnp.where(field8 < 2, TIMESTEP * line(r_s, r_n, 14), TIMESTEP * VISCOSITY),
        coriolis8, of(q8, 2), of(q8, 3), field8, slope, slope,
    )
    for f in range(4):
        x1[0, f, ROW0 - 1 : ROW0, :] = rows_new[f : f + 1]
        x1[0, f, end : end + 1, :] = rows_new[4 + f : 5 + f]
        for k in range(2):
            x0[k, f, ROW0 - 1 : ROW0, :] = r_s[8 * k + f : 8 * k + f + 1, :]
            x0[k, f, end : end + 1, :] = r_n[8 * k + f : 8 * k + f + 1, :]
    wet_pad[ROW0 - 1 : ROW0, :] = r_s[12:13, :]
    wet_pad[end : end + 1, :] = r_n[12:13, :]

    low = lane % 4 < 2
    halves = lambda a, b: jnp.where(iota(a.shape, 1) < cols // 2, a, pltpu.roll(b, cols // 2 - 1, 1))
    own_rim, east_rim, west_rim = rim[...], rim_e[...], rim_w[...]
    strip = halves(jnp.where(low, west_rim, own_rim), jnp.where(low, own_rim, east_rim))
    rim_pad[ROW0:end, :] = strip
    wide = lambda ref: jnp.broadcast_to(ref[15:16, :], (8, cols))
    rim_pad[ROW0 - 1 : ROW0, :] = halves(wide(r_sw), wide(r_se))[0:1]
    rim_pad[end : end + 1, :] = halves(wide(r_nw), wide(r_ne))[0:1]
    strip_n = rim_pad[ROW0 + 1 : end + 1, :]
    strip_s = rim_pad[ROW0 - 1 : end - 1, :]
    right = lambda x, d: pltpu.roll(x, (d + cols) % cols, 1)
    wets = [right(x, -32) for x in (strip_n, strip_s, strip)]
    field = group % 16

    def spread_field(i):
        out = strip
        for f in range(4):
            if f != i:
                out = jnp.where(field == f, right(strip, 4 * (f - i)), out)
        return out

    rim_new[...] = surface_step(
        strip, right(strip, -1), right(strip, 1), strip_n, strip_s, right(strip, -16),
        (right(wets[2], -1), right(wets[2], 1), wets[0], wets[1], wets[2]),
        right(strip, -48), coriolis, spread_field(2), spread_field(3), field,
        lambda d: HALINE * right(d, 4) - THERMAL * right(d, 8),
        lambda d: HALINE * right(d, 8) - THERMAL * right(d, 12),
    )

    at = lambda x, src, dst: pltpu.roll(x, (dst - src + cols) % cols, 1)
    w_east = pltpu.roll(jnp.where(lane == 0, at(east_rim, 34, 0), wet), cols - 1, 1)
    w_west = pltpu.roll(jnp.where(lane == cols - 1, at(west_rim, 33, cols - 1), wet), 1, 1)
    w_north = wet_pad[ROW0 + 1 : end + 1, :]
    w_south = wet_pad[ROW0 - 1 : end - 1, :]
    total = w_east + w_west + w_north + w_south
    for base, rate in ((0, rate_t), (5, TIMESTEP * VISCOSITY)):
        coef[base] = wet * (centre - rate * total)
        for j, w in enumerate((w_east, w_west, w_north, w_south)):
            coef[base + 1 + j] = wet * (rate * w)
    coef[10] = vertical * wet
    coef[11] = TIMESTEP * coriolis * wet

    pressure_rate = 0.5 * TIMESTEP * GRAVITY
    assert abs(pressure_rate - TIMESTEP * VERTICAL_MIX) < 1e-12

    def level(x, k, side_of, carry, store):
        above = lax.max(k - 1, 0) if not isinstance(k, int) else max(k - 1, 0)
        below = lax.min(k + 1, levels - 1) if not isinstance(k, int) else min(k + 1, levels - 1)
        carry = list(carry)
        for c in range(chunks):
            mid = part(c)
            ahead = slice(ROW0 + 8 * c + 1, ROW0 + 8 * c + 9)
            behind = slice(ROW0 + 8 * c - 1, ROW0 + 8 * c + 7)
            own = slice(8 * c, 8 * c + 8)
            q, e, w, n, s = [], [], [], [], []
            for f in range(4):
                value = x[k, f, mid, :]
                side = side_of(own, k, f)
                q.append(value)
                e.append(pltpu.roll(jnp.where(first, side, value), cols - 1, 1))
                w.append(pltpu.roll(jnp.where(last, side, value), 1, 1))
                n.append(x[k, f, ahead, :])
                s.append(x[k, f, behind, :])
            gx = HALINE * (e[1] - w[1]) - THERMAL * (e[0] - w[0])
            gy = HALINE * (n[1] - s[1]) - THERMAL * (n[0] - s[0])
            sx = carry[2 * c] + gx
            sy = carry[2 * c + 1] + gy
            carry[2 * c], carry[2 * c + 1] = sx, sy
            push = (None, None, sx - 0.5 * gx, sy - 0.5 * gy)
            u = (0.5 * TIMESTEP) * q[2]
            v = (0.5 * TIMESTEP) * q[3]
            vert = coef[10, own, :]
            turn = coef[11, own, :]
            for f in range(4):
                if f % 2 == 0:
                    base = 0 if f == 0 else 5
                    a = coef[base, own, :]
                    ce = coef[base + 1, own, :] - u
                    cw = coef[base + 2, own, :] + u
                    cn = coef[base + 3, own, :] - v
                    cs = coef[base + 4, own, :] + v
                column = x[above, f, mid, :] + x[below, f, mid, :]
                if f >= 2:
                    column = column - push[f]
                value = (a * q[f] + vert * column) + (ce * e[f] + cw * w[f]) + (cn * n[f] + cs * s[f])
                if f == 2:
                    value = value + turn * q[3]
                if f == 3:
                    value = value - turn * q[2]
                store(k, f, c, value)
        return tuple(carry)

    def merge(edge, from_e, from_w):
        edge[...] = jnp.where(lax.rem(lane, 2) == 0, from_e[...], from_w[...])

    def unfold(fold, lo, hi, put):
        @pl.when(lat == top)
        def _():
            for k in range(lo, hi, 2):
                width = min(2, hi - k)
                pair = fold[k : k + width].reshape(4 * width, cols)
                pair = reverse_lanes(pair)
                field = lax.rem(iota(pair.shape, 0), 4)
                pair = jnp.where(field < 2, pair, -pair)
                put(k, width, pair)

    def packed_side(edge):
        return lambda own, k, f: pltpu.roll(edge[own, :], lax.rem(2 * cols - 2 * (4 * k + f), cols), 1)

    def rim_side(from_east, lane_e, from_west, lane_w):
        def side(own, k, f):
            i = 4 * (4 * k + f)
            east_value = at(from_east[own, :], lane_e + i, 0)
            return jnp.where(first, east_value, at(from_west[own, :], lane_w + i, cols - 1))

        return side

    zeros = tuple(jnp.zeros((8, cols), f32) for _ in range(2 * chunks))

    def step1(k, side_of, carry, tiles):
        tiles = list(tiles)

        def store(k, f, c, value):
            x1[k, f, part(c), :] = value
            if tiles:
                tiles[c] = packed(tiles[c], value, 4 * k + f)

        carry = level(x0, k, side_of, carry, store)
        return carry, tuple(tiles)

    near_side = rim_side(rim_e, 2, rim_w, 1)
    carry1, _ = step1(0, near_side, zeros, ())
    carry1, tiles = step1(1, near_side, carry1, empty)

    def store2(k, f, c, value):
        x2[k, f, 8 * c : 8 * c + 8, :] = value

    carry2 = level(x1, 0, rim_side(rim_new, 65, rim_new, 1), zeros, store2)
    surf = x2[0].reshape(4 * rows, cols)
    late = dot(onehot[...], jnp.concatenate(split(surf), axis=0))
    out_late[...] = late.reshape(devices, 8, cols)
    in_late[devices - 1 : devices] = out_late[pl.ds(me, 1)]
    late_all = exchange(out_late, in_late, 1, 8)

    for copy in halo0_cols:
        copy.wait_recv()
    wait_rows(*halo0_rows)
    merge(edge0, from_e0, from_w0)

    def put_rows(k, width, pair):
        for j in range(width):
            for f in range(4):
                x0[k + j, f, end : end + 1, :] = pair[4 * j + f : 4 * j + f + 1]

    unfold(fold0, 2, levels, put_rows)
    _, tiles = lax.fori_loop(
        2, levels, lambda k, s: step1(k, packed_side(edge0), *s), (carry1, tiles), unroll=UNROLL1
    )
    for c in range(chunks):
        pack1b[8 * c : 8 * c + 8, :] = tiles[c]
    halo2_rows = row_copies(
        x1, 1, 4, rows_s.at[1:levels], rows_n.at[1:levels], rows_n.at[1:levels]
    )
    halo2_cols = col_copies(pack1b, from_wb, from_eb, 6)
    start_rows(*halo2_rows)
    for copy in halo2_cols:
        copy.start()

    nothing = jnp.zeros((8, cols), f32)
    lax.fori_loop(
        1, levels, lambda k, s: level(x1, k, lambda own, k, f: nothing, s, store2), carry2, unroll=UNROLL2
    )

    for copy in early_all:
        copy.wait_recv()
    tile = (cols // 8, 8, cols)
    sub3 = iota(tile, 1)
    lane3 = iota(tile, 2)
    keep = (sub3 // 2) == (lane3 // ATM_ROWS)
    wanted = (lax.rem(lane3, ATM_ROWS) + 1).astype(f32)
    for j in range(devices * 8 // cols):
        got = in_early[tile[0] * j : tile[0] * (j + 1)]
        ids = jnp.where((sub3 // 2) == 1, got, 0.0)
        ids = (ids + pltpu.roll(ids, 2, 1)) + (pltpu.roll(ids, 4, 1) + pltpu.roll(ids, 6, 1))
        hit = jnp.where(keep & (ids == wanted), 1.0, 0.0)
        row_hot[:, cols * j : cols * (j + 1)] = hit.reshape(cols, cols).T.astype(bf16)
    wets = jnp.where(iota((devices, 8, cols), 1) < 2, in_early[...], 0.0)
    cover = dot(row_hot[0:ATM_ROWS, :], wets.reshape(devices * 8, cols).astype(bf16))
    cover_v[...] = cover
    share = 1.0 / jnp.maximum(cover, 1.0)

    for copy in halo2_cols:
        copy.wait_recv()
    wait_rows(*halo2_rows)
    edge2b[...] = jnp.where(
        lax.rem(lane, 2) == 0, pltpu.roll(from_wb[...], 1, 1), pltpu.roll(from_eb[...], cols - 1, 1)
    )

    def put_back(k, width, pair):
        rows_n[k : k + width] = pair.reshape(width, 4, cols)

    unfold(rows_n, 1, levels, put_back)

    def halo_share(k, carry):
        carry = list(carry)
        for c in range(chunks):
            own, mid = slice(8 * c, 8 * c + 8), part(c)
            u = (0.5 * TIMESTEP) * x1[k, 2, mid, :]
            v = (0.5 * TIMESTEP) * x1[k, 3, mid, :]
            vert = coef[10, own, :]
            side = edge2b[own, :]
            halo = [pltpu.roll(side, lax.rem(2 * cols - 2 * (4 * k + f), cols), 1) for f in range(4)]
            gx = HALINE * halo[1] - THERMAL * halo[0]
            gx = jnp.where(last, gx, jnp.where(first, -gx, 0.0))
            carry[c] = carry[c] + gx
            add = []
            for f in range(4):
                base = 0 if f < 2 else 5
                rate = jnp.where(
                    last, coef[base + 1, own, :] - u, jnp.where(first, coef[base + 2, own, :] + u, 0.0)
                )
                add.append(rate * halo[f])
            add[2] = add[2] - vert * (carry[c] - 0.5 * gx)
            for outside, rows_of, edge, index, sign in (
                (c == 0, rows_s, 0, 4, 1.0), (c == chunks - 1, rows_n, 7, 3, -1.0)
            ):
                if outside:
                    here = iota((8, cols), 0) == edge
                    line_of = [
                        jnp.where(here, jnp.broadcast_to(rows_of[k, f : f + 1, :], (8, cols)), 0.0)
                        for f in range(4)
                    ]
                    gy = -sign * (HALINE * line_of[1] - THERMAL * line_of[0])
                    slot = chunks + (0 if c == 0 else 1)
                    carry[slot] = carry[slot] + gy
                    for f in range(4):
                        base = 0 if f < 2 else 5
                        add[f] = add[f] + (coef[base + index, own, :] + sign * v) * line_of[f]
                    add[3] = add[3] - vert * (carry[slot] - 0.5 * gy)
            for f in range(4):
                x2[k, f, own, :] = x2[k, f, own, :] + add[f]
        return tuple(carry)

    lax.fori_loop(1, levels, halo_share, (nothing,) * (chunks + 2), unroll=UNROLL2)
    sums = jnp.zeros((4 * ATM_ROWS, cols), f32)
    for half, copy in enumerate(late_all):
        copy.wait_recv()
        lo, hi = ((0, near), (near, devices))[half]
        got = in_late[lo:hi].reshape((hi - lo) * 8, cols)
        placed = row_hot[:, 8 * lo : 8 * hi]
        for piece in split(got):
            sums = sums + dot(placed, piece)
    surf_v[...] = sums.reshape(4, ATM_ROWS, cols) * share

    for cond, copy in ups + downs:
        pl.when(cond)(copy.wait_send)
    drain_rows(*halo0_rows)
    drain_rows(*halo2_rows)
    for copy in [*sides, *halo0_cols, *halo2_cols]:
        copy.wait_send()
    whole = lambda ref, height: ref.at[0 : devices - 1, 0:height, :]
    for sem, (out, into, height) in enumerate(((out_early, in_early, 4), (out_late, in_late, 8))):
        pltpu.make_async_remote_copy(
            src_ref=whole(out, height), dst_ref=whole(into, height),
            send_sem=a_send.at[sem], recv_sem=a_recv.at[2 * sem], device_id=east, device_id_type=MESH,
        ).wait_send()


def write_out(x2, surf_v, cover_v, tracers_out, velocity_out, surface_out, cover_out, sem):
    stores = []
    for f in range(4):
        dst = (tracers_out if f < 2 else velocity_out).at[f % 2]
        stores.append(pltpu.make_async_copy(x2.at[:, f], dst, sem.at[f]))
    stores.append(pltpu.make_async_copy(cover_v, cover_out, sem.at[4]))
    stores.append(pltpu.make_async_copy(surf_v, surface_out, sem.at[5]))
    for store in stores:
        store.start()
    for store in stores:
        store.wait()


def local(tracers, velocity, land_mask, mixing, owners, atm_row):
    n_lon, n_lat = lax.axis_size("lon"), lax.axis_size("lat")
    levels = tracers.shape[1]
    rows, cols = land_mask.shape
    devices = n_lon * n_lat
    blocks = rows * cols // 128
    assert cols == 128 and blocks == rows and ATM_ROWS == 32
    any_spec = pl.BlockSpec(memory_space=pl.ANY)
    vmem = lambda *shape: pltpu.VMEM(shape, f32)
    tile = vmem(rows, cols)
    padded = rows + 16
    scratch = (
        [vmem(levels, 4, padded, cols)] * 2
        + [vmem(padded, cols)]
        + [pltpu.VMEM((rows, cols), jnp.int32), tile]
        + [pltpu.VMEM((1, blocks), jnp.int32)] * 2
        + [tile] * 12
        + [vmem(padded, cols)]
        + [vmem(levels, 4, cols)] * 3
        + [vmem(16, cols)] * 9
        + [vmem(12, rows, cols), pltpu.VMEM((devices * 8, PIECES * cols), bf16)]
        + [vmem(devices, 8, cols)] * 4
        + [pltpu.VMEM((4 * ATM_ROWS, devices * 8), bf16)]
        + [pltpu.SemaphoreType.DMA((12,))]
        + [pltpu.SemaphoreType.DMA((8,))] * 4
        + [pltpu.SemaphoreType.DMA((2,)), pltpu.SemaphoreType.DMA((4,))]
        + [pltpu.SemaphoreType.REGULAR]
    )
    ring = lambda d, size: min(d % size, size - d % size)
    half_lat = n_lat // 2
    hops = lambda a, c: ring(a, n_lon // 2) + ring(c // 2, half_lat // 2) + 2 * (a // (n_lon // 2)) + c // half_lat
    offsets = [(a, c) for a in range(n_lon) for c in range(n_lat) if a or c]
    offsets.sort(key=lambda o: hops(*o))
    held = pl.pallas_call(
        functools.partial(kernel, n_lon, n_lat, levels, rows, cols, offsets),
        out_shape=(vmem(levels, 4, rows, cols), vmem(4, ATM_ROWS, cols), vmem(ATM_ROWS, cols)),
        in_specs=[any_spec] * 6,
        scratch_shapes=scratch,
        compiler_params=pltpu.CompilerParams(collective_id=0, has_side_effects=True),
        name="ocean",
    )(tracers, velocity, land_mask, mixing, owners.reshape(1, blocks), atm_row.reshape(1, blocks))
    return pl.pallas_call(
        write_out,
        out_shape=(
            jax.ShapeDtypeStruct(tracers.shape, f32),
            jax.ShapeDtypeStruct(velocity.shape, f32),
            jax.ShapeDtypeStruct((4, ATM_ROWS, cols), f32),
            jax.ShapeDtypeStruct((ATM_ROWS, cols), f32),
        ),
        in_specs=[pl.BlockSpec(memory_space=pltpu.VMEM)] * 3,
        out_specs=(any_spec,) * 4,
        scratch_shapes=[pltpu.SemaphoreType.DMA((6,))],
        name="write_out",
    )(*(pltpu.with_memory_space_constraint(x, pltpu.VMEM) for x in held))


def solution(mesh):
    in_specs = (
        P(None, None, "lat", "lon"),
        P(None, None, "lat", "lon"),
        P("lat", "lon"),
        P("lat", "lon"),
        P(("lon", "lat"), None),
        P(("lon", "lat")),
    )
    out_specs = (
        P(None, None, "lat", "lon"),
        P(None, None, "lat", "lon"),
        P(None, ("lon", "lat"), None),
        P(("lon", "lat"), None),
    )
    return jax.shard_map(local, mesh=mesh, in_specs=in_specs, out_specs=out_specs, check_vma=False)
```
